512 devices in a mesh: row: 16 (over z), col: 32 (over y, x, core).
Axes of the slice: x: 4, y: 4, z: 16, core: 2. Of those that a mesh axis runs over, the one named last changes fastest.
Arguments:
- velocity: float32 [3, 256, 256, 256], P(None, 'row', 'col'), may hold values from -6 to 6
- positions: bfloat16 [16384, 3, 128], P(('row', 'col')), may hold values from -4 to 4
- weights: bfloat16 [16384, 3, 8, 128], P(('row', 'col')), may hold values from 0 to 0.5
- stiffness: bfloat16 [16384], P(('row', 'col')), may hold values from 0.099609375 to 1
- rest_sq: bfloat16 [16384], P(('row', 'col')), may hold values from 1 to 8
- owner_column: int32 [16384, 1], P(('row', 'col')), may hold values from 0 to 31; in each aligned block of 32 rows (0 to 31, 32 to 63, ...) at most 3 rows name the same one
- brick_index: int32 [16384], P(('row', 'col')), may hold values from 0 to 63
Outputs:
- new_velocity: float32 [3, 256, 256, 256], P(None, 'row', 'col')
- marker_velocity: float32 [16384, 3, 128], P(('row', 'col'))
The draws below stay inside these ranges and needn't reach their ends.
Inputs may be any that keep to these rules, and one draw needn't show every extreme that they name: `owner_column`: A block's brick lies on the device in the block's own device row and in this column; no device's 32 blocks name one column more than 3 times, and that many is reached.
All inputs are finite; a program needn't handle non-finite values.
Results may differ from the reference program's by a relative error of at most 0.0003.
Values may be sent and summed in bfloat16 or wider, within the bound.
No kernel may reach another device: no remote copies, remote signals or barrier semaphores. Data moves between devices by JAX's collectives and lax.ppermute only.
A program may use at most 64 MiB of HBM per device.

```python
import math
import jax
import jax.numpy as jnp
import numpy as np
from jax import lax

CX = 16
CY = 8
NZ = 256
BRICK = 8
MARK = 128
BLK_DEV = 32
NX = 256
NY = 256
BLOCKS = 16384
CAP = 3
BRK_DEV = 64
N_ROW = 16
N_COL = 32


def set_ends(array, rng, smallest, high):
    place = [jax.random.randint(jax.random.fold_in(rng, axis), (), 0, length) for axis, length in enumerate(array.shape)]
    longest = array.shape.index(max(array.shape))
    beside = place[:longest] + [(place[longest] + 1) % array.shape[longest]] + place[longest + 1:]
    return array.at[tuple(place)].set(smallest).at[tuple(beside)].set(high)


def levels(key, dims, pieces, least, top_value):
    level, own = 1.0, jax.random.fold_in(key, 6)
    for axis_at, parts in pieces:
        heights = jnp.exp(jax.random.uniform(jax.random.fold_in(own, axis_at), (parts,), jnp.float32, least / len(pieces), top_value / len(pieces)))
        level = level * jnp.repeat(heights, dims[axis_at] // parts).reshape([-1 if axis == axis_at else 1 for axis in range(len(dims))])
    return level


def deal_out(stream_key, own, number, rows, amount, top, most, skew):
    sequence = jax.random.permutation(stream_key, amount)
    crowded, usual = load_shares(amount, rows * top, most, skew, True), load_shares(amount, rows * top, most, skew, False)
    places = jnp.arange(amount)

    def named(lengths, rotation):
        used = int((lengths > 0).sum())
        fixed = max(1, used // 4)
        moved = fixed + (places - fixed + rotation * (used - fixed)) % max(1, amount - fixed)
        return jnp.zeros((amount,), jnp.int32).at[sequence[jnp.where(places < fixed, places, moved)]].set(jnp.asarray(lengths, jnp.int32))

    lengths = jnp.where(number % 4 == 0, named(crowded, number // 4), named(usual, number - number // 4 - 1))
    mixed = jax.random.permutation(jax.random.fold_in(own, 3), amount)
    giver, sink = mixed[0:amount // 2 * 2:2], mixed[1:amount // 2 * 2:2]
    room = jnp.minimum(lengths[giver] - 1, most - lengths[sink]) // 2
    room = jnp.where((giver == sequence[0]) | (sink == sequence[0]) | (lengths[sink] == 0), 0, jnp.maximum(room, 0))
    moved = jax.random.randint(jax.random.fold_in(own, 4), (amount // 2,), 0, 1 << 20) % (room + 1)
    lengths = lengths.at[giver].add(-moved).at[sink].add(moved)
    labels = jnp.searchsorted(jnp.cumsum(lengths), jnp.arange(rows * top), side="right").astype(jnp.int32)
    table = labels.reshape(top, rows).T
    table = table[jax.random.permutation(jax.random.fold_in(own, 1), rows)]
    rotation = jax.random.randint(jax.random.fold_in(own, 2), (rows, 1), 0, top)
    return jnp.take_along_axis(table, (jnp.arange(top)[None, :] + rotation) % top, axis=1)


def load_shares(count, total, limit, lean, full):
    loads = [(1 << 20) // math.isqrt(grade ** lean) + 1 for grade in range(1, count + 1)]
    largest = limit if full else min(limit, max(-(-total // count), total * loads[0] // sum(loads)))
    least = 1 if total - largest >= count - 1 else 0
    counts, spare = [largest] + [least] * (count - 1), total - largest - least * (count - 1)
    while spare > 0:
        movable = [i for i in range(1, count) if counts[i] < largest] or [i for i in range(1, count) if counts[i] < limit]
        mass, budget = sum([loads[i] for i in movable]), spare
        for i in movable:
            addition = min(limit - counts[i], max(1, budget * loads[i] // mass), spare)
            counts[i] = counts[i] + addition
            spare = spare - addition
    return np.array(counts)


def normal_values(rng, extent, scale, most, pieces=(), held_as=jnp.bfloat16):
    factor_of = levels(rng, extent, pieces, -0.22, 0.18) if pieces else 1.0
    drawn = jax.random.normal(rng, extent, jnp.float32) * scale * factor_of
    return jnp.minimum(jnp.maximum(drawn, -most), most).astype(held_as)


def setup_inputs(seed: int = 0) -> dict:
    seeds = jax.random.split(jax.random.key(seed), 8)
    velocity = normal_values(seeds[0], (3, NX, NY, NZ), 1.0, 6.0, ((1, 16), (2, 32)), jnp.float32)
    positions = normal_values(seeds[1], (BLOCKS, 3, MARK), 1.0, 4.0, ((0, 512),))
    weights = jnp.clip(0.5 * jax.random.uniform(seeds[2], (BLOCKS, 3, BRICK, MARK), jnp.float32) ** levels(seeds[2], (BLOCKS, 3, BRICK, MARK), ((0, 512),), -0.2, 0.2), 0.0, 0.5).astype(jnp.bfloat16)
    stiffness = jnp.clip(jnp.exp(math.log(1.0) - 2.306499 * jax.random.uniform(seeds[3], (BLOCKS,), jnp.float32) ** levels(seeds[3], (BLOCKS,), ((0, 512),), -0.2, 0.2)), 0.099609375, 1.0).astype(jnp.bfloat16)
    rest_sq = jnp.clip(jnp.exp(math.log(8.0) - 2.0794415 * jax.random.uniform(seeds[4], (BLOCKS,), jnp.float32) ** levels(seeds[4], (BLOCKS,), ((0, 512),), -0.2, 0.2)), 1.0, 8.0).astype(jnp.bfloat16)
    owner_column_keys = jax.random.split(jax.random.fold_in(seeds[5], 1), BLOCKS // BLK_DEV)
    owner_column_turns = jax.random.permutation(jax.random.fold_in(seeds[5], 3), BLOCKS // BLK_DEV)
    owner_column = jax.vmap(lambda own, number: deal_out(jax.random.fold_in(seeds[5], 2), own, number, BLK_DEV, N_COL, 1, CAP, 2))(owner_column_keys, owner_column_turns).reshape((BLOCKS, 1))
    brick_index = set_ends(jax.random.randint(seeds[6], (BLOCKS,), 0, BRK_DEV), jax.random.fold_in(seeds[6], 1), 0, BRK_DEV - 1).astype(jnp.int32)
    return dict(velocity=velocity, positions=positions, weights=weights, stiffness=stiffness, rest_sq=rest_sq, owner_column=owner_column, brick_index=brick_index)


DT_STEP = 0.5
VISCOSITY = 0.1
PRECISE = lax.Precision.HIGHEST


def to_bricks(values):
    components, size_x, size_y, size_z = values.shape
    blocks_view = values.reshape(components, size_x // BRICK, BRICK, size_y // BRICK, BRICK, size_z // BRICK, BRICK)
    blocks_view = blocks_view.transpose(1, 3, 5, 0, 2, 4, 6)
    return blocks_view.reshape(-1, components * BRICK * BRICK * BRICK)


def from_bricks(bricks, size_x, size_y, size_z):
    blocks_view = bricks.reshape(size_x // BRICK, size_y // BRICK, size_z // BRICK, 3, BRICK, BRICK, BRICK)
    blocks_view = blocks_view.transpose(3, 0, 4, 1, 5, 2, 6)
    return blocks_view.reshape(3, size_x, size_y, size_z)


def chain_force(positions_f, stiffness_f, rest_f):
    segment = jnp.roll(positions_f, -1, axis=2) - positions_f
    stretch = jnp.sum(segment * segment, axis=1, keepdims=True) / rest_f[:, None, None]
    tension = 0.5 * stiffness_f[:, None, None] * (stretch - 1.0) * segment
    return tension - jnp.roll(tension, 1, axis=2)


def interpolate(bricks_in, weights_f):
    cubes = bricks_in.reshape(-1, 3, BRICK, BRICK, BRICK)
    reduced = jnp.einsum('ncijk,nkm->ncijm', cubes, weights_f[:, 2], precision=PRECISE)
    reduced = jnp.einsum('ncijm,njm->ncim', reduced, weights_f[:, 1], precision=PRECISE)
    return jnp.einsum('ncim,nim->ncm', reduced, weights_f[:, 0], precision=PRECISE)


def spread(forces, weights_f):
    partial_sum = jnp.einsum('ncm,nim->ncim', forces, weights_f[:, 0], precision=PRECISE)
    partial_sum = jnp.einsum('ncim,njm->ncijm', partial_sum, weights_f[:, 1], precision=PRECISE)
    cubes = jnp.einsum('ncijm,nkm->ncijk', partial_sum, weights_f[:, 2], precision=PRECISE)
    return cubes.reshape(cubes.shape[0], -1)


def advect(values):
    transport = jnp.zeros_like(values)
    for direction in range(3):
        gradient = (jnp.roll(values, -1, axis=direction + 1) - jnp.roll(values, 1, axis=direction + 1)) * 0.5
        transport = transport + values[direction] * gradient
    return transport


def signed_modes(indices, length):
    return jnp.where(indices <= (length - 1) // 2, indices, indices - length)


def direction_modes(indices, length):
    return jnp.where(2 * indices == length, 0, signed_modes(indices, length))


def reference(velocity, positions, weights, stiffness, rest_sq, owner_column, brick_index):
    brick_table = to_bricks(velocity)
    local_x = CX // BRICK
    local_y = CY // BRICK
    local_z = NZ // BRICK
    total_y = NY // BRICK
    block_ids = jnp.arange(BLOCKS, dtype=jnp.int32)
    row_index = block_ids // (BLK_DEV * N_COL)
    column = owner_column[:, 0]
    brick_x = brick_index // (local_y * local_z)
    brick_y = (brick_index // local_z) % local_y
    brick_z = brick_index % local_z
    global_ids = ((row_index * local_x + brick_x) * total_y + column * local_y + brick_y) * local_z + brick_z
    device_count = N_ROW * N_COL

    def visit_group(forcing, member):
        brick_ids, positions_g, weights_g, stiffness_g, rest_g = member
        weights_f = weights_g.astype(jnp.float32)
        marker_vel = interpolate(brick_table[brick_ids], weights_f)
        forces = chain_force(positions_g.astype(jnp.float32), stiffness_g.astype(jnp.float32), rest_g.astype(jnp.float32))
        forcing = forcing.at[brick_ids].add(spread(forces, weights_f))
        return forcing, marker_vel

    members = (global_ids.reshape(device_count, BLK_DEV),
               positions.reshape(device_count, BLK_DEV, 3, MARK),
               weights.reshape(device_count, BLK_DEV, 3, BRICK, MARK),
               stiffness.reshape(device_count, BLK_DEV),
               rest_sq.reshape(device_count, BLK_DEV))
    forcing, gathered = lax.scan(visit_group, jnp.zeros_like(brick_table), members)
    marker_velocity = gathered.reshape(BLOCKS, 3, MARK)
    force_field = from_bricks(forcing, NX, NY, NZ)
    star = velocity + DT_STEP * (force_field - advect(velocity))
    spectrum = jnp.fft.fftn(star, axes=(1, 2, 3))
    index_x = jnp.arange(NX, dtype=jnp.int32)
    index_y = jnp.arange(NY, dtype=jnp.int32)
    index_z = jnp.arange(NZ, dtype=jnp.int32)
    full_x = (2.0 * jnp.pi / NX) * signed_modes(index_x, NX).astype(jnp.float32)[:, None, None]
    full_y = (2.0 * jnp.pi / NY) * signed_modes(index_y, NY).astype(jnp.float32)[None, :, None]
    full_z = (2.0 * jnp.pi / NZ) * signed_modes(index_z, NZ).astype(jnp.float32)[None, None, :]
    dir_x = direction_modes(index_x, NX)[:, None, None]
    dir_y = direction_modes(index_y, NY)[None, :, None]
    dir_z = direction_modes(index_z, NZ)[None, None, :]
    no_direction = (dir_x == 0) & (dir_y == 0) & (dir_z == 0)
    wave_x = (2.0 * jnp.pi / NX) * dir_x.astype(jnp.float32)
    wave_y = (2.0 * jnp.pi / NY) * dir_y.astype(jnp.float32)
    wave_z = (2.0 * jnp.pi / NZ) * dir_z.astype(jnp.float32)
    wave_sq = wave_x * wave_x + wave_y * wave_y + wave_z * wave_z
    inverse_sq = jnp.where(no_direction, 0.0, 1.0 / jnp.where(no_direction, 1.0, wave_sq))
    damping = 1.0 / (1.0 + DT_STEP * VISCOSITY * (full_x * full_x + full_y * full_y + full_z * full_z))
    normal_part = (wave_x * spectrum[0] + wave_y * spectrum[1] + wave_z * spectrum[2]) * inverse_sq
    projected = jnp.stack([(spectrum[0] - wave_x * normal_part) * damping,
                           (spectrum[1] - wave_y * normal_part) * damping,
                           (spectrum[2] - wave_z * normal_part) * damping])
    new_velocity = jnp.real(jnp.fft.ifftn(projected, axes=(1, 2, 3))).astype(jnp.float32)
    return new_velocity, marker_velocity
```

```python
import jax
import jax.numpy as jnp
import numpy as np
from jax import lax
from jax.experimental import pallas as pl
from jax.experimental.pallas import tpu as pltpu
from jax.sharding import PartitionSpec as P


DT_STEP = 0.5
VISCOSITY = 0.1
N = 256
FIRST = np.array([k for r in range(16) for k in ((0, 16) if r == 0 else (r, 32 - r))])
F32 = jnp.float32
BF16 = jnp.bfloat16
TURN = 2.0 * np.pi


def split_table(table):
    table = np.asarray(table, np.float32)
    high = table.astype(BF16)
    low = (table - high.astype(np.float32)).astype(BF16)
    return np.stack([high, low])


def rotation(angle):
    rows, cols = angle.shape
    out = np.zeros((rows, 2, 4, cols, 2, 4))
    for j in range(4):
        out[:, 0, j, :, 0, j] = np.cos(angle)
        out[:, 0, j, :, 1, j] = np.sin(angle)
        out[:, 1, j, :, 0, j] = -np.sin(angle)
        out[:, 1, j, :, 1, j] = np.cos(angle)
    return out.reshape(rows * 8, cols * 8)


def z_tables():
    z = np.arange(N)
    fore = np.zeros((32, 2, 4, N))
    back = np.zeros((32, 2, 4, N))
    for k in range(128):
        angle = TURN / N * (k * z % N)
        twice = 2.0 if k else 1.0
        sine = np.sin(angle) if k else -np.cos(np.pi * z)
        fore[k // 4, 0, k % 4] = np.cos(angle)
        fore[k // 4, 1, k % 4] = -sine
        back[k // 4, 0, k % 4] = twice * np.cos(angle) / N
        back[k // 4, 1, k % 4] = -twice * sine / N
    return split_table(fore.reshape(N, N)), split_table(back.reshape(N, N))


def y_tables():
    angle = TURN / 32 * np.outer(FIRST, np.arange(32))
    fore = split_table(rotation(angle))
    back = split_table(rotation(-angle.T) / N)
    small = TURN / 8 * np.outer(np.arange(8), np.arange(8))
    cosine, sine = (np.kron(np.eye(16), f(small)) for f in (np.cos, np.sin))
    lanes_fore = split_table(np.concatenate([cosine, sine], 1))
    lanes_back = split_table(np.concatenate([cosine, -sine], 1))
    phase = TURN / N * np.outer(FIRST, np.tile(np.arange(8), 16))
    twiddle = np.stack([np.cos(phase), np.sin(phase)]).astype(np.float32)[:, :, None, :]
    return fore, back, lanes_fore, lanes_back, twiddle


def x_tables():
    angle = TURN / 16 * np.outer(np.arange(16), np.arange(16))
    pair = np.eye(2)

    def both(turn):
        grid = np.zeros((16, 2, 8, 16, 2, 8))
        base = rotation(turn).reshape(16, 8, 16, 8)
        for p in range(2):
            grid[:, p, :, :, p, :] = base
        return grid

    main = both(angle).reshape(256, 256)
    extra = both(angle).reshape(8, 2, 2, 2, 4, 16, 2, 2, 4)[:, :, :, :, 0]
    extra = extra.transpose(0, 3, 1, 2, 4, 5, 6, 7).copy()
    extra[..., 1:] = 0.0
    extra = extra.reshape(64, 256)
    back_main = both(-angle).reshape(256, 256) / N
    back_extra = both(-angle).reshape(16, 2, 2, 4, 8, 2, 2, 2, 4)[..., 0]
    back_extra = back_extra.transpose(0, 1, 2, 3, 4, 7, 5, 6).copy()
    back_extra[:, :, :, 1:] = 0.0
    back_extra = back_extra.reshape(256, 64) / N
    back = np.concatenate([back_main, back_extra], 1)
    cosine, sine = (np.kron(f(angle), np.eye(8)) for f in (np.cos, np.sin))
    lanes_fore = split_table(np.concatenate([cosine, sine], 1))
    lanes_back = split_table(np.concatenate([cosine, -sine], 1))
    phase = TURN / N * np.outer(np.arange(16), np.repeat(np.arange(16), 8))
    wide = np.zeros((2, 320, 128), np.float32)
    k_main = np.repeat(np.arange(16), 16)
    k_extra = (2 * np.arange(8)[:, None, None, None] + np.arange(2)[None, None, :, None]
               + np.zeros((8, 2, 2, 2), int)).reshape(64)
    p_main = np.tile(np.repeat(np.arange(2), 8), 16)
    p_extra = np.tile(np.arange(2), 32)
    j_main = np.tile(np.arange(4), 64)
    first = np.concatenate([k_main, k_extra])
    wide[0] = np.cos(phase)[first]
    wide[1] = np.sin(phase)[first]
    marks = (first, np.concatenate([p_main, p_extra]), np.concatenate([j_main, np.zeros(64, int)]))
    reverse = np.kron(np.eye(16), np.eye(8)[(7 - np.arange(8))])
    negate = np.kron(np.eye(16), np.eye(8)[(-np.arange(8)) % 8])
    flips = np.concatenate([reverse, negate], 1).astype(BF16)
    return (split_table(main), split_table(extra), split_table(back), lanes_fore, lanes_back,
            wide.reshape(2, 40, 8, 128), marks, flips)


def dot(a, b, dims=((1,), (0,))):
    return lax.dot_general(a, b, (dims, ((), ())), preferred_element_type=F32)


def halves(x):
    high = x.astype(BF16)
    return high, (x - high.astype(F32)).astype(BF16)


def table_left(table, x, dims=((1,), (0,))):
    high, low = halves(x)
    return dot(table[0], high, dims) + dot(table[0], low, dims) + dot(table[1], high, dims)


def table_right(x, table, dims=((1,), (0,))):
    high, low = halves(x)
    return dot(high, table[0], dims) + dot(low, table[0], dims) + dot(high, table[1], dims)


def signs(shape):
    at = lax.broadcasted_iota(jnp.int32, shape, len(shape) - 2)
    return jnp.where(at % 8 < 4, 1.0, -1.0).astype(F32)


def swapped(x):
    return pltpu.roll(x, 4, 1) * signs((1, 8, 128))


def lane_pass(x, table):
    both = table_right(x, table)
    rows = x.shape[0]
    cosine = both[:, :128].reshape(rows // 8, 8, 128)
    sine = both[:, 128:].reshape(rows // 8, 8, 128)
    return cosine + swapped(sine)


def stacked(x):
    return jnp.concatenate([x[:, 128 * c:128 * c + 128] for c in range(3)], 0)


def unstacked(x):
    rows = x.shape[0] // 3
    return jnp.concatenate([x[rows * c:rows * c + rows] for c in range(3)], 1)


def twiddled(x, cosine, sine):
    groups = cosine.shape[0]
    turned = swapped(x)
    parts = [x[groups * c:groups * c + groups] * cosine + turned[groups * c:groups * c + groups] * sine
             for c in range(3)]
    return jnp.concatenate(parts, 0)


def tile_place(slot, c):
    at = 3 * slot + c
    return at >> 1, at & 1


def lane_half(shape=(8, 128)):
    return lax.broadcasted_iota(jnp.int32, shape, len(shape) - 1) // 64


def spread_kernel(params, owner, brick, positions, weights, out, slots, count, cubes):
    out[...] = jnp.zeros(out.shape, F32)
    for d in range(32):
        count[d] = 0
    for n in range(32):
        place = positions[n].astype(F32)
        segment = pltpu.roll(place, 127, 1) - place
        stretch = jnp.sum(segment * segment, axis=0, keepdims=True) / params[1, n]
        tension = 0.5 * params[0, n] * (stretch - 1.0) * segment
        force = tension - pltpu.roll(tension, 1, 1)
        w0, w1, w2 = (weights[n, a].astype(F32) for a in range(3))
        cells = (w0[:, None, :] * w1[None, :, :]).reshape(64, 128)
        cells = jnp.concatenate([cells, cells], 0)
        pushed = (force[:, None, :] * w2[None, :, :]).reshape(24, 128)
        cells_high, cells_low = halves(cells)
        pushed_high, pushed_low = halves(pushed)
        both = ((1,), (1,))
        cubes[n] = (dot(pushed_high, cells_high, both) + dot(pushed_low, cells_high, both)
                    + dot(pushed_high, cells_low, both))
    half = lane_half()
    lane = lax.broadcasted_iota(jnp.int32, (8, 128), 1)

    @pl.loop(0, 32)
    def _(n):
        d = owner[n, 0]
        s = count[d]
        count[d] = s + 1
        slots[n] = s
        for c in range(3):
            tile, side = tile_place(s, c)
            out[d, tile] += jnp.where(half == side, cubes[n, 8 * c:8 * c + 8, :], 0.0)
        out[d, 4] += jnp.where(lane == 64 + s, brick[n].astype(F32), 0.0)


def advect_kernel(table, velocity, x_low, x_high, y_low, y_high, spectrum, turned):
    u = [velocity[c].reshape(128, 256) for c in range(3)]
    sub = lax.broadcasted_iota(jnp.int32, (16, 8, 256), 1)
    rows = []
    for c in range(3):
        v = velocity[c]
        turned[c] = jnp.transpose(u[c]).reshape(32, 8, 128)
        ahead = jnp.concatenate([v[1:], x_high[c]], 0)
        behind = jnp.concatenate([x_low[c], v[:-1]], 0)
        total = u[0] * (ahead - behind).reshape(128, 256)
        ahead = jnp.where(sub == 7, y_high[c], pltpu.roll(v, 7, 1))
        behind = jnp.where(sub == 0, y_low[c], pltpu.roll(v, 1, 1))
        total = total + u[1] * (ahead - behind).reshape(128, 256)
        total = total + u[2] * (pltpu.roll(u[c], 255, 1) - pltpu.roll(u[c], 1, 1))
        rows.append(u[c] - (0.5 * DT_STEP) * total)
    star = jnp.concatenate(rows, 0)
    spectrum[...] = table_left(table, star, ((1,), (1,)))


def gather_kernel(ids, table, pushes, spectrum, out, force0, force1, force2):
    forces = (force0, force1, force2)
    for force in forces:
        force[...] = jnp.zeros(force.shape, F32)
    half = lane_half()

    @pl.loop(0, 32, unroll=4)
    def _(src):
        tiles = [pushes[src, t] for t in range(5)]
        turned = [pltpu.roll(tile, 64, 1) for tile in tiles]
        for slot in range(3):
            brick = ids[src, slot]
            x_half, z_block = brick >> 5, brick & 31
            for c in range(3):
                tile, side = tile_place(slot, c)
                wide = jnp.where(half == side, tiles[tile], turned[tile])
                forces[c][z_block] += jnp.where(half == x_half, wide, 0.0)

    field = jnp.concatenate([force[...].reshape(256, 128) for force in forces], 1)
    total = spectrum[...] + table_left(table, DT_STEP * field)
    out[...] = total.reshape(32, 8, 384)


def reply_kernel(ids, turned, out):
    half = lane_half()

    @pl.loop(0, 32, unroll=4)
    def _(src):
        wides = []
        for slot in range(3):
            brick = ids[src, slot]
            x_half, z_block = brick >> 5, brick & 31
            for c in range(3):
                tile = turned[c, z_block]
                wides.append(jnp.where(half == x_half, tile, pltpu.roll(tile, 64, 1)))
        wides.append(wides[0])
        for t in range(5):
            out[src, t] = jnp.where(half == 0, wides[2 * t], wides[2 * t + 1])


def interpolate_kernel(owner, slots, replies, weights, out):
    half = lane_half()
    for n in range(32):
        d, s = owner[n, 0], slots[n]
        parts = []
        for c in range(3):
            tile, side = tile_place(s, c)
            cube = replies[d, tile]
            parts.append(jnp.where(half == side, cube, pltpu.roll(cube, 64, 1)))
        cube_high, cube_low = halves(jnp.concatenate(parts, 0)[:, :64])
        w0, w1, w2 = (weights[n, a].astype(F32) for a in range(3))
        cells_high, cells_low = halves((w0[:, None, :] * w1[None, :, :]).reshape(64, 128))
        partial = dot(cube_high, cells_high) + dot(cube_low, cells_high) + dot(cube_high, cells_low)
        out[n] = jnp.sum(partial.reshape(3, 8, 128) * w2[None], axis=1)


def y_kernel(left, lanes, twiddle, values, out):
    spectrum = table_left(left, values[...].reshape(256, 384))
    spectrum = stacked(spectrum).reshape(96, 8, 128)
    spectrum = twiddled(spectrum, twiddle[0], twiddle[1])
    spectrum = lane_pass(spectrum.reshape(768, 128), lanes)
    out[...] = unstacked(spectrum.reshape(768, 128)).reshape(16, 16, 384)


def x_kernel(flags, left, left_extra, back, lanes, lanes_back, twiddle, flips, waves, damping, values, out):
    packed = stacked(values[...].reshape(256, 384))
    high, low = halves(packed)
    flipped = dot(high, flips[...]) + dot(low, flips[...])
    by_pair = (3, 16, 2, 8, 128)
    reverse = flipped[:, :128].reshape(by_pair)
    negate = flipped[:, 128:].reshape(by_pair)
    packed = packed.reshape(by_pair)
    own = flags[0] == 1
    first = jnp.where(own, negate[:, :, 0:1], reverse[:, :, 1:2])
    second = jnp.where(own, reverse[:, :, 1:2], reverse[:, :, 0:1])
    mirrored = jnp.concatenate([first, second], 2) * signs((1, 1, 1, 8, 128))
    sub = lax.broadcasted_iota(jnp.int32, (1, 1, 1, 8, 128), 3)
    lowest = (sub % 4 == 0) & (flags[1] == 1)
    main = jnp.where(lowest, 0.5 * (packed + mirrored), packed)
    extra = jnp.where(lowest, 0.5 * (packed - mirrored), 0.0)
    main = table_left(left, unstacked(main.reshape(768, 128)))
    extra = table_left(left_extra, unstacked(extra.reshape(768, 128)))
    spectrum = stacked(jnp.concatenate([main, extra], 0)).reshape(120, 8, 128)
    spectrum = twiddled(spectrum, twiddle[0], twiddle[1])
    spectrum = lane_pass(spectrum.reshape(960, 128), lanes).reshape(3, 320, 128)
    normal = waves[0] * spectrum[0] + waves[1] * spectrum[1] + waves[2] * spectrum[2]
    damp = damping[...]
    projected = jnp.concatenate([(spectrum[c] - waves[c] * normal) * damp for c in range(3)], 0)
    projected = lane_pass(projected, lanes_back)
    projected = twiddled(projected, twiddle[0], -twiddle[1])
    projected = unstacked(projected.reshape(960, 128))
    out[...] = table_left(back, projected).reshape(16, 16, 384)


def y_back_kernel(back, lanes, twiddle, values, out):
    spectrum = lane_pass(stacked(values[...].reshape(256, 384)), lanes)
    spectrum = twiddled(spectrum, twiddle[0], -twiddle[1])
    spectrum = table_left(back, unstacked(spectrum.reshape(768, 128)))
    out[...] = spectrum.reshape(32, 8, 384)


def z_back_kernel(back, values, out):
    spectrum = values[...].reshape(256, 384)
    field = table_right(jnp.transpose(spectrum), back)
    out[...] = field.reshape(3, 16, 8, 256)


VMEM = pl.BlockSpec(memory_space=pltpu.VMEM)
SMEM = pl.BlockSpec(memory_space=pltpu.SMEM)


def call(kernel, specs, shapes, scratch=(), out_specs=None):
    single = not isinstance(shapes, tuple)
    structs = [jax.ShapeDtypeStruct(s, F32) if isinstance(s, list) else s
               for s in ((shapes,) if single else shapes)]
    outs = out_specs or [VMEM] * len(structs)
    return pl.pallas_call(
        kernel,
        out_shape=structs[0] if single else structs,
        in_specs=specs,
        out_specs=outs[0] if single else outs,
        scratch_shapes=list(scratch),
        compiler_params=pltpu.CompilerParams(vmem_limit_bytes=48 << 20),
    )


def signed(indices):
    return jnp.where(indices <= (N - 1) // 2, indices, indices - N)


def wave_tables(marks, row, col):
    first, pair, slot = (jnp.asarray(m, jnp.int32)[:, None] for m in marks)
    lane = jnp.arange(128, dtype=jnp.int32)[None, :]
    nyquist = jnp.arange(320, dtype=jnp.int32)[:, None] >= 256
    second = jnp.where(row == 0, 16, 32 - row)
    index_x = first + 16 * (lane // 8)
    index_y = jnp.where(pair == 0, row, second) + 32 * (lane % 8)
    index_z = jnp.where(nyquist, N // 2, 4 * col + slot) + 0 * lane
    scale = 2.0 * jnp.pi / N
    full_sq, waves = 0.0, []
    for index in (index_x, index_y, index_z):
        full = scale * signed(index).astype(F32)
        full_sq = full_sq + full * full
        waves.append(jnp.where(2 * index == N, 0.0, full))
    wave_sq = waves[0] * waves[0] + waves[1] * waves[1] + waves[2] * waves[2]
    still = wave_sq == 0.0
    inverse = jnp.where(still, 0.0, lax.rsqrt(jnp.where(still, 1.0, wave_sq)))
    units = jnp.stack([w * inverse for w in waves])
    return units, 1.0 / (1.0 + DT_STEP * VISCOSITY * full_sq)


def moved(x, axis):
    return lax.all_to_all(x, axis, split_axis=0, concat_axis=0, tiled=True)


def neighbours(plane_low, plane_high, axis):
    count = lax.axis_size(axis)
    up = [(i, (i + 1) % count) for i in range(count)]
    down = [((i + 1) % count, i) for i in range(count)]
    return lax.ppermute(plane_high, axis, up), lax.ppermute(plane_low, axis, down)


def local(velocity, positions, weights, stiffness, rest_sq, owner_column, brick_index):
    row, col = lax.axis_index("row"), lax.axis_index("col")
    z_fore, z_back = z_tables()
    y_fore, y_back, y_lanes, y_lanes_back, y_twiddle = y_tables()
    x_fore, x_extra, x_back, x_lanes, x_lanes_back, x_twiddle, marks, flips = x_tables()
    flags = jnp.stack([row == 0, col == 0]).astype(jnp.int32)
    units, damping = wave_tables(marks, row, col)

    params = jnp.stack([stiffness, rest_sq]).astype(F32)
    pushes, slots = call(
        spread_kernel, [SMEM, SMEM, SMEM, VMEM, VMEM],
        ([32, 5, 8, 128], jax.ShapeDtypeStruct((32,), jnp.int32)),
        [pltpu.SMEM((32,), jnp.int32), pltpu.VMEM((32, 24, 128), F32)], [VMEM, SMEM],
    )(params, owner_column, brick_index, positions, weights)
    x_low, x_high = neighbours(velocity[:, :1], velocity[:, 15:], "row")
    y_low, y_high = neighbours(velocity[:, :, :1], velocity[:, :, 7:], "col")
    pushes = moved(pushes, "col")
    ids = pushes[:, 4, 0, 64:67].astype(jnp.int32)

    spectrum, turned = call(advect_kernel, [VMEM] * 6, ([256, 384], [3, 32, 8, 128]))(
        z_fore, velocity, x_low, x_high, y_low, y_high)
    spectrum = call(gather_kernel, [SMEM, VMEM, VMEM, VMEM], [32, 8, 384],
                    [pltpu.VMEM((32, 8, 128), F32)] * 3)(ids, z_fore, pushes, spectrum)
    spectrum = moved(spectrum, "col")
    spectrum = call(y_kernel, [VMEM] * 4, [16, 16, 384])(y_fore, y_lanes, y_twiddle, spectrum)
    spectrum = moved(spectrum, "row")
    spectrum = call(x_kernel, [SMEM] + [VMEM] * 10, [16, 16, 384])(
        flags, x_fore, x_extra, x_back, x_lanes, x_lanes_back, x_twiddle, flips, units, damping, spectrum)
    spectrum = moved(spectrum, "row")
    spectrum = call(y_back_kernel, [VMEM] * 4, [32, 8, 384])(y_back, y_lanes_back, y_twiddle, spectrum)
    spectrum = moved(spectrum, "col")
    new_velocity = call(z_back_kernel, [VMEM] * 2, [3, 16, 8, 256])(z_back, spectrum)

    replies = moved(call(reply_kernel, [SMEM, VMEM], [32, 5, 8, 128])(ids, turned), "col")
    marker_velocity = call(interpolate_kernel, [SMEM, SMEM, VMEM, VMEM], [32, 3, 128])(
        owner_column, slots, replies, weights)
    return new_velocity, marker_velocity


def solution(mesh):
    both = ("row", "col")
    placed = (
        P(None, "row", "col", None),
        P(both, None, None),
        P(both, None, None, None),
        P(both),
        P(both),
        P(both, None),
        P(both),
    )
    return jax.shard_map(
        local,
        mesh=mesh,
        in_specs=placed,
        out_specs=(P(None, "row", "col", None), P(both, None, None)),
        check_vma=False,
    )
```

```python
import jax
import jax.numpy as jnp
import numpy as np
from jax import lax
from jax.experimental import pallas as pl
from jax.experimental.pallas import tpu as pltpu
from jax.sharding import PartitionSpec as P


DT_STEP = 0.5
VISCOSITY = 0.1
N = 256
FIRST = np.array([k for r in range(16) for k in ((0, 16) if r == 0 else (r, 32 - r))])
F32 = jnp.float32
BF16 = jnp.bfloat16
TURN = 2.0 * np.pi


def split_table(table):
    table = np.asarray(table, np.float32)
    high = table.astype(BF16)
    low = (table - high.astype(np.float32)).astype(BF16)
    return np.stack([high, low])


def rotation(angle):
    rows, cols = angle.shape
    out = np.zeros((rows, 2, 4, cols, 2, 4))
    for j in range(4):
        out[:, 0, j, :, 0, j] = np.cos(angle)
        out[:, 0, j, :, 1, j] = np.sin(angle)
        out[:, 1, j, :, 0, j] = -np.sin(angle)
        out[:, 1, j, :, 1, j] = np.cos(angle)
    return out.reshape(rows * 8, cols * 8)


def z_tables():
    z = np.arange(N)
    fore = np.zeros((32, 2, 4, N))
    back = np.zeros((32, 2, 4, N))
    for k in range(128):
        angle = TURN / N * (k * z % N)
        twice = 2.0 if k else 1.0
        sine = np.sin(angle) if k else -np.cos(np.pi * z)
        fore[k // 4, 0, k % 4] = np.cos(angle)
        fore[k // 4, 1, k % 4] = -sine
        back[k // 4, 0, k % 4] = twice * np.cos(angle) / N
        back[k // 4, 1, k % 4] = -twice * sine / N
    return split_table(fore.reshape(N, N)), split_table(back.reshape(N, N))


def y_tables():
    angle = TURN / 32 * np.outer(FIRST, np.arange(32))
    fore = split_table(rotation(angle))
    back = split_table(rotation(-angle.T) / N)
    small = TURN / 8 * np.outer(np.arange(8), np.arange(8))
    cosine, sine = (np.kron(np.eye(16), f(small)) for f in (np.cos, np.sin))
    lanes_fore = split_table(np.concatenate([cosine, sine], 1))
    lanes_back = split_table(np.concatenate([cosine, -sine], 1))
    phase = TURN / N * np.outer(FIRST, np.tile(np.arange(8), 16))
    twiddle = np.stack([np.cos(phase), np.sin(phase)]).astype(np.float32)[:, :, None, :]
    return fore, back, lanes_fore, lanes_back, twiddle


def x_tables():
    angle = TURN / 16 * np.outer(np.arange(16), np.arange(16))
    pair = np.eye(2)

    def both(turn):
        grid = np.zeros((16, 2, 8, 16, 2, 8))
        base = rotation(turn).reshape(16, 8, 16, 8)
        for p in range(2):
            grid[:, p, :, :, p, :] = base
        return grid

    main = both(angle).reshape(256, 256)
    extra = both(angle).reshape(8, 2, 2, 2, 4, 16, 2, 2, 4)[:, :, :, :, 0]
    extra = extra.transpose(0, 3, 1, 2, 4, 5, 6, 7).copy()
    extra[..., 1:] = 0.0
    extra = extra.reshape(64, 256)
    back_main = both(-angle).reshape(256, 256) / N
    back_extra = both(-angle).reshape(16, 2, 2, 4, 8, 2, 2, 2, 4)[..., 0]
    back_extra = back_extra.transpose(0, 1, 2, 3, 4, 7, 5, 6).copy()
    back_extra[:, :, :, 1:] = 0.0
    back_extra = back_extra.reshape(256, 64) / N
    back = np.concatenate([back_main, back_extra], 1)
    cosine, sine = (np.kron(f(angle), np.eye(8)) for f in (np.cos, np.sin))
    lanes_fore = split_table(np.concatenate([cosine, sine], 1))
    lanes_back = split_table(np.concatenate([cosine, -sine], 1))
    phase = TURN / N * np.outer(np.arange(16), np.repeat(np.arange(16), 8))
    wide = np.zeros((2, 320, 128), np.float32)
    k_main = np.repeat(np.arange(16), 16)
    k_extra = (2 * np.arange(8)[:, None, None, None] + np.arange(2)[None, None, :, None]
               + np.zeros((8, 2, 2, 2), int)).reshape(64)
    p_main = np.tile(np.repeat(np.arange(2), 8), 16)
    p_extra = np.tile(np.arange(2), 32)
    j_main = np.tile(np.arange(4), 64)
    first = np.concatenate([k_main, k_extra])
    wide[0] = np.cos(phase)[first]
    wide[1] = np.sin(phase)[first]
    marks = (first, np.concatenate([p_main, p_extra]), np.concatenate([j_main, np.zeros(64, int)]))
    reverse = np.kron(np.eye(16), np.eye(8)[(7 - np.arange(8))])
    negate = np.kron(np.eye(16), np.eye(8)[(-np.arange(8)) % 8])
    flips = np.concatenate([reverse, negate], 1).astype(BF16)
    return (split_table(main), split_table(extra), split_table(back), lanes_fore, lanes_back,
            wide.reshape(2, 40, 8, 128), marks, flips)


def dot(a, b, dims=((1,), (0,))):
    return lax.dot_general(a, b, (dims, ((), ())), preferred_element_type=F32)


def halves(x):
    high = x.astype(BF16)
    return high, (x - high.astype(F32)).astype(BF16)


def table_left(table, x, dims=((1,), (0,))):
    high, low = halves(x)
    return dot(table[0], high, dims) + dot(table[0], low, dims) + dot(table[1], high, dims)


def table_right(x, table, dims=((1,), (0,))):
    high, low = halves(x)
    return dot(high, table[0], dims) + dot(low, table[0], dims) + dot(high, table[1], dims)


def signs(shape):
    at = lax.broadcasted_iota(jnp.int32, shape, len(shape) - 2)
    return jnp.where(at % 8 < 4, 1.0, -1.0).astype(F32)


def swapped(x):
    return pltpu.roll(x, 4, 1) * signs((1, 8, 128))


def lane_pass(x, table):
    both = table_right(x, table)
    rows = x.shape[0]
    cosine = both[:, :128].reshape(rows // 8, 8, 128)
    sine = both[:, 128:].reshape(rows // 8, 8, 128)
    return cosine + swapped(sine)


def stacked(x):
    return jnp.concatenate([x[:, 128 * c:128 * c + 128] for c in range(3)], 0)


def unstacked(x):
    rows = x.shape[0] // 3
    return jnp.concatenate([x[rows * c:rows * c + rows] for c in range(3)], 1)


def twiddled(x, cosine, sine):
    groups = cosine.shape[0]
    turned = swapped(x)
    parts = [x[groups * c:groups * c + groups] * cosine + turned[groups * c:groups * c + groups] * sine
             for c in range(3)]
    return jnp.concatenate(parts, 0)


def tile_place(slot, c):
    at = 3 * slot + c
    return at >> 1, at & 1


def lane_half(shape=(8, 128)):
    return lax.broadcasted_iota(jnp.int32, shape, len(shape) - 1) // 64


def to_exponent(largest):
    return jnp.ceil(16.0 * jnp.log(jnp.maximum(largest, 1e-36)))


def steps_per_unit(exponent):
    return 32767.0 * jnp.exp(exponent * (-1.0 / 16.0))


def step(exponent):
    return jnp.exp(exponent * (1.0 / 16.0)) * (1.0 / 32767.0)


def narrow(codes):
    return codes.astype(jnp.int32).astype(jnp.int16)


def wide(codes):
    return codes.astype(jnp.int32).astype(F32)


def row_largest(x):
    return jnp.max(jnp.abs(x), axis=-1, keepdims=True)


def encoded(x):
    largest = jnp.maximum(jnp.maximum(jnp.abs(x[0]), jnp.abs(x[1])), jnp.abs(x[2]))
    largest = jnp.broadcast_to(jnp.max(largest, axis=-1, keepdims=True), largest.shape)
    exponent = to_exponent(largest)
    return jnp.round(x * steps_per_unit(exponent)[None]), exponent


def put_pairs(out, spectrum):
    codes, exponent = encoded(spectrum)
    codes = narrow(codes).reshape(3, 16, 2, 8, 128)
    exponent = exponent.reshape(16, 2, 8, 128)
    for p in range(2):
        for c in range(3):
            out[:, 3 * p + c] = codes[c, :, p]
    half = lane_half((1, 8, 128))
    out[:, 6] = narrow(jnp.where(half == 0, exponent[:, 0], exponent[:, 1]))


def take_pairs(values):
    half = lane_half((1, 8, 128))
    steps = step(wide(values[:, 6]))
    turned = pltpu.roll(steps, 64, 2)
    steps = (jnp.where(half == 0, steps, turned), jnp.where(half == 0, turned, steps))
    parts = []
    for c in range(3):
        pair = [wide(values[:, 3 * p + c]) * steps[p] for p in range(2)]
        parts.append(jnp.stack(pair, 1).reshape(256, 128))
    return jnp.concatenate(parts, 0)


def to_column(row):
    size = row.shape[1]
    same = (lax.broadcasted_iota(jnp.int32, (size, size), 0)
            == lax.broadcasted_iota(jnp.int32, (size, size), 1))
    return jnp.sum(jnp.where(same, row, 0.0), axis=1, keepdims=True)


def spread_kernel(owner, brick, stiffness, rest_sq, positions, weights, out, slots, count, cubes, marks, total):
    total[...] = jnp.zeros(total.shape, F32)
    for d in range(32):
        count[d] = 0
    place = [positions[c].astype(F32) for c in range(3)]
    segment = [pltpu.roll(p, 127, 1) - p for p in place]
    stretch = (segment[0] * segment[0] + segment[1] * segment[1] + segment[2] * segment[2])
    stretch = stretch / to_column(rest_sq[...].astype(F32))
    pull = 0.5 * to_column(stiffness[...].astype(F32)) * (stretch - 1.0)
    force = []
    for c in range(3):
        tension = pull * segment[c]
        force.append(tension - pltpu.roll(tension, 1, 1))
    for n in range(32):
        w0, w1, w2 = (weights[n, a].astype(F32) for a in range(3))
        cells = (w0[:, None, :] * w1[None, :, :]).reshape(64, 128)
        cells = jnp.concatenate([cells, cells], 0)
        pushed = jnp.concatenate([force[c][n:n + 1] * w2 for c in range(3)], 0)
        cells_high, cells_low = halves(cells)
        pushed_high, pushed_low = halves(pushed)
        both = ((1,), (1,))
        cube = (dot(pushed_high, cells_high, both) + dot(pushed_low, cells_high, both)
                + dot(pushed_high, cells_low, both))
        exponent = to_exponent(jnp.broadcast_to(row_largest(cube), cube.shape))
        marks[n] = exponent
        cubes[n] = jnp.round(cube * steps_per_unit(exponent))
    half = lane_half()
    lane = lax.broadcasted_iota(jnp.int32, (8, 128), 1)

    @pl.loop(0, 32)
    def _(n):
        d = owner[n]
        s = count[d]
        count[d] = s + 1
        slots[n] = s
        last = jnp.where(lane == 73 + s, brick[n].astype(F32), 0.0)
        for c in range(3):
            tile, side = tile_place(s, c)
            total[d, tile] += jnp.where(half == side, cubes[n, 8 * c:8 * c + 8, :], 0.0)
            last = jnp.where(lane == 64 + 3 * s + c, marks[n, 8 * c:8 * c + 8, :], last)
        total[d, 4] += last

    out[...] = narrow(total[...])


def advect_kernel(table, velocity, x_low, x_high, y_low, y_high, spectrum, turned):
    u = [velocity[c].reshape(128, 256) for c in range(3)]
    sub = lax.broadcasted_iota(jnp.int32, (16, 8, 256), 1)
    rows = []
    for c in range(3):
        v = velocity[c]
        turned[c] = jnp.transpose(u[c]).reshape(32, 8, 128)
        ahead = jnp.concatenate([v[1:], x_high[c]], 0)
        behind = jnp.concatenate([x_low[c], v[:-1]], 0)
        total = u[0] * (ahead - behind).reshape(128, 256)
        ahead = jnp.where(sub == 7, y_high[c], pltpu.roll(v, 7, 1))
        behind = jnp.where(sub == 0, y_low[c], pltpu.roll(v, 1, 1))
        total = total + u[1] * (ahead - behind).reshape(128, 256)
        total = total + u[2] * (pltpu.roll(u[c], 255, 1) - pltpu.roll(u[c], 1, 1))
        rows.append(u[c] - (0.5 * DT_STEP) * total)
    star = jnp.concatenate(rows, 0)
    spectrum[...] = table_left(table, star, ((1,), (1,)))


def gather_kernel(ids, table, pushes, spectrum, out, force0, force1, force2):
    forces = (force0, force1, force2)
    for force in forces:
        force[...] = jnp.zeros(force.shape, F32)
    half = lane_half()

    @pl.loop(0, 32, unroll=4)
    def _(src):
        tiles = [wide(pushes[src, t]) for t in range(5)]
        turned = [pltpu.roll(tile, 64, 1) for tile in tiles]
        steps = step(tiles[4])
        for slot in range(3):
            brick = ids[src, slot]
            x_half, z_block = brick >> 5, brick & 31
            for c in range(3):
                at = 3 * slot + c
                tile, side = tile_place(slot, c)
                codes = jnp.where(half == side, tiles[tile], turned[tile])
                cube = codes * jnp.broadcast_to(steps[:, 64 + at:65 + at], (8, 128))
                forces[c][z_block] += jnp.where(half == x_half, cube, 0.0)

    field = jnp.concatenate([force[...].reshape(256, 128) for force in forces], 1)
    total = spectrum[...] + table_left(table, DT_STEP * field)
    codes, exponent = encoded(stacked(total).reshape(3, 32, 8, 128))
    for c in range(3):
        out[:, c] = narrow(codes[c])
    out[:, 3] = narrow(exponent)


def reply_kernel(ids, turned, out):
    half = lane_half()
    lane = lax.broadcasted_iota(jnp.int32, (8, 128), 1)

    @pl.loop(0, 32, unroll=4)
    def _(src):
        cubes = []
        largest = jnp.ones((8, 128), F32)
        for slot in range(3):
            brick = ids[src, slot]
            x_half, z_block = brick >> 5, brick & 31
            for c in range(3):
                tile = turned[c, z_block]
                cube = jnp.where(half == x_half, tile, pltpu.roll(tile, 64, 1))
                largest = jnp.where(lane == 64 + len(cubes), row_largest(cube), largest)
                cubes.append(cube)
        exponent = to_exponent(largest)
        steps = steps_per_unit(exponent)
        codes = [jnp.round(cube * jnp.broadcast_to(steps[:, 64 + at:65 + at], (8, 128)))
                 for at, cube in enumerate(cubes)]
        codes.append(exponent)
        for t in range(5):
            out[src, t] = narrow(jnp.where(half == 0, codes[2 * t], codes[2 * t + 1]))


def interpolate_kernel(owner, slots, replies, weights, out):
    half = lane_half()
    lane = lax.broadcasted_iota(jnp.int32, (8, 128), 1)
    for n in range(32):
        d, s = owner[n], slots[n]
        steps = step(wide(replies[d, 7]))
        parts = []
        for c in range(3):
            tile, side = tile_place(s, c)
            cube = wide(replies[d, 3 + tile])
            cube = jnp.where(half == side, cube, pltpu.roll(cube, 64, 1))
            own = jnp.sum(jnp.where(lane == 64 + 3 * s + c, steps, 0.0), axis=1, keepdims=True)
            parts.append(cube * own)
        cube_high, cube_low = halves(jnp.concatenate(parts, 0)[:, :64])
        w0, w1, w2 = (weights[n, a].astype(F32) for a in range(3))
        cells_high, cells_low = halves((w0[:, None, :] * w1[None, :, :]).reshape(64, 128))
        partial = dot(cube_high, cells_high) + dot(cube_low, cells_high) + dot(cube_high, cells_low)
        for c in range(3):
            out[c, n:n + 1] = jnp.sum(partial[8 * c:8 * c + 8] * w2, axis=0, keepdims=True)


def y_kernel(left, lanes, twiddle, values, out):
    steps = step(wide(values[:, 3]))
    spectrum = [(wide(values[:, c]) * steps).reshape(256, 128) for c in range(3)]
    spectrum = table_left(left, jnp.concatenate(spectrum, 1))
    spectrum = stacked(spectrum).reshape(96, 8, 128)
    spectrum = twiddled(spectrum, twiddle[0], twiddle[1])
    spectrum = lane_pass(spectrum.reshape(768, 128), lanes)
    put_pairs(out, spectrum.reshape(3, 32, 8, 128))


def x_kernel(flags, left, left_extra, back, lanes, lanes_back, twiddle, flips, waves, damping, values, out):
    packed = take_pairs(values)
    high, low = halves(packed)
    flipped = dot(high, flips[...]) + dot(low, flips[...])
    by_pair = (3, 16, 2, 8, 128)
    reverse = flipped[:, :128].reshape(by_pair)
    negate = flipped[:, 128:].reshape(by_pair)
    packed = packed.reshape(by_pair)
    own = flags[0] == 1
    first = jnp.where(own, negate[:, :, 0:1], reverse[:, :, 1:2])
    second = jnp.where(own, reverse[:, :, 1:2], reverse[:, :, 0:1])
    mirrored = jnp.concatenate([first, second], 2) * signs((1, 1, 1, 8, 128))
    sub = lax.broadcasted_iota(jnp.int32, (1, 1, 1, 8, 128), 3)
    lowest = (sub % 4 == 0) & (flags[1] == 1)
    main = jnp.where(lowest, 0.5 * (packed + mirrored), packed)
    extra = jnp.where(lowest, 0.5 * (packed - mirrored), 0.0)
    main = table_left(left, unstacked(main.reshape(768, 128)))
    extra = table_left(left_extra, unstacked(extra.reshape(768, 128)))
    spectrum = stacked(jnp.concatenate([main, extra], 0)).reshape(120, 8, 128)
    spectrum = twiddled(spectrum, twiddle[0], twiddle[1])
    spectrum = lane_pass(spectrum.reshape(960, 128), lanes).reshape(3, 320, 128)
    normal = waves[0] * spectrum[0] + waves[1] * spectrum[1] + waves[2] * spectrum[2]
    damp = damping[...]
    projected = jnp.concatenate([(spectrum[c] - waves[c] * normal) * damp for c in range(3)], 0)
    projected = lane_pass(projected, lanes_back)
    projected = twiddled(projected, twiddle[0], -twiddle[1])
    projected = unstacked(projected.reshape(960, 128))
    put_pairs(out, stacked(table_left(back, projected)).reshape(3, 32, 8, 128))


def y_back_kernel(back, lanes, twiddle, values, replies, out):
    spectrum = lane_pass(take_pairs(values), lanes)
    spectrum = twiddled(spectrum, twiddle[0], -twiddle[1])
    spectrum = table_left(back, unstacked(spectrum.reshape(768, 128)))
    codes, exponent = encoded(stacked(spectrum).reshape(3, 32, 8, 128))
    for c in range(3):
        out[:, c] = narrow(codes[c])
    for t in range(4):
        out[:, 3 + t] = replies[:, t]
    lane = lax.broadcasted_iota(jnp.int32, (1, 8, 128), 2)
    out[:, 7] = narrow(jnp.where(lane == 76, exponent, wide(replies[:, 4])))


def z_back_kernel(back, values, out):
    steps = step(wide(values[:, 7])[:, :, 76:77])
    spectrum = [(wide(values[:, c]) * steps).reshape(256, 128) for c in range(3)]
    field = table_right(jnp.transpose(jnp.concatenate(spectrum, 1)), back)
    out[...] = field.reshape(3, 16, 8, 256)


VMEM = pl.BlockSpec(memory_space=pltpu.VMEM)
SMEM = pl.BlockSpec(memory_space=pltpu.SMEM)


def call(kernel, specs, shapes, scratch=(), out_specs=None):
    single = not isinstance(shapes, tuple)
    structs = [jax.ShapeDtypeStruct(s, F32) if isinstance(s, list) else s
               for s in ((shapes,) if single else shapes)]
    outs = out_specs or [VMEM] * len(structs)
    return pl.pallas_call(
        kernel,
        out_shape=structs[0] if single else structs,
        in_specs=specs,
        out_specs=outs[0] if single else outs,
        scratch_shapes=list(scratch),
        compiler_params=pltpu.CompilerParams(vmem_limit_bytes=48 << 20),
    )


def codes_of(count, tiles):
    return jax.ShapeDtypeStruct((count, tiles, 8, 128), jnp.int16)


def signed(indices):
    return jnp.where(indices <= (N - 1) // 2, indices, indices - N)


def wave_tables(marks, row, col):
    first, pair, slot = (jnp.asarray(m, jnp.int32)[:, None] for m in marks)
    lane = jnp.arange(128, dtype=jnp.int32)[None, :]
    nyquist = jnp.arange(320, dtype=jnp.int32)[:, None] >= 256
    second = jnp.where(row == 0, 16, 32 - row)
    index_x = first + 16 * (lane // 8)
    index_y = jnp.where(pair == 0, row, second) + 32 * (lane % 8)
    index_z = jnp.where(nyquist, N // 2, 4 * col + slot) + 0 * lane
    scale = 2.0 * jnp.pi / N
    full_sq, waves = 0.0, []
    for index in (index_x, index_y, index_z):
        full = scale * signed(index).astype(F32)
        full_sq = full_sq + full * full
        waves.append(jnp.where(2 * index == N, 0.0, full))
    wave_sq = waves[0] * waves[0] + waves[1] * waves[1] + waves[2] * waves[2]
    still = wave_sq == 0.0
    inverse = jnp.where(still, 0.0, lax.rsqrt(jnp.where(still, 1.0, wave_sq)))
    units = jnp.stack([w * inverse for w in waves])
    return units, 1.0 / (1.0 + DT_STEP * VISCOSITY * full_sq)


def moved(x, axis):
    return lax.all_to_all(x, axis, split_axis=0, concat_axis=0, tiled=True)


def neighbours(plane_low, plane_high, axis):
    count = lax.axis_size(axis)
    up = [(i, (i + 1) % count) for i in range(count)]
    down = [((i + 1) % count, i) for i in range(count)]
    return lax.ppermute(plane_high, axis, up), lax.ppermute(plane_low, axis, down)


def local(velocity, positions, weights, stiffness, rest_sq, owner_column, brick_index):
    row, col = lax.axis_index("row"), lax.axis_index("col")
    z_fore, z_back = z_tables()
    y_fore, y_back, y_lanes, y_lanes_back, y_twiddle = y_tables()
    x_fore, x_extra, x_back, x_lanes, x_lanes_back, x_twiddle, marks, flips = x_tables()
    flags = jnp.stack([row == 0, col == 0]).astype(jnp.int32)
    units, damping = wave_tables(marks, row, col)

    owner = owner_column.reshape(32)
    spread_outs = (jax.ShapeDtypeStruct((32, 5, 8, 128), jnp.int16), jax.ShapeDtypeStruct((32,), jnp.int32))
    pushes, slots = call(
        spread_kernel, [SMEM, SMEM, VMEM, VMEM, VMEM, VMEM], spread_outs,
        [pltpu.SMEM((32,), jnp.int32), pltpu.VMEM((32, 24, 128), F32), pltpu.VMEM((32, 24, 128), F32),
         pltpu.VMEM((32, 5, 8, 128), F32)], [VMEM, SMEM],
    )(owner, brick_index, stiffness.reshape(1, 32), rest_sq.reshape(1, 32), positions.transpose(1, 0, 2), weights)
    x_low, x_high = neighbours(velocity[:, :1], velocity[:, 15:], "row")
    y_low, y_high = neighbours(velocity[:, :, :1], velocity[:, :, 7:], "col")
    pushes = moved(pushes, "col")
    ids = pushes[:, 4, 0, 73:76].astype(jnp.int32)

    spectrum, turned = call(advect_kernel, [VMEM] * 6, ([256, 384], [3, 32, 8, 128]))(
        z_fore, velocity, x_low, x_high, y_low, y_high)
    spectrum = call(gather_kernel, [SMEM, VMEM, VMEM, VMEM], codes_of(32, 4),
                    [pltpu.VMEM((32, 8, 128), F32)] * 3)(ids, z_fore, pushes, spectrum)
    spectrum = moved(spectrum, "col")
    spectrum = call(y_kernel, [VMEM] * 4, codes_of(16, 7))(y_fore, y_lanes, y_twiddle, spectrum)
    spectrum = moved(spectrum, "row")
    spectrum = call(x_kernel, [SMEM] + [VMEM] * 10, codes_of(16, 7))(
        flags, x_fore, x_extra, x_back, x_lanes, x_lanes_back, x_twiddle, flips, units, damping, spectrum)
    spectrum = moved(spectrum, "row")
    replies = call(reply_kernel, [SMEM, VMEM], codes_of(32, 5))(ids, turned)
    spectrum = call(y_back_kernel, [VMEM] * 5, codes_of(32, 8))(
        y_back, y_lanes_back, y_twiddle, spectrum, replies)
    spectrum = moved(spectrum, "col")
    new_velocity = call(z_back_kernel, [VMEM] * 2, [3, 16, 8, 256])(z_back, spectrum)
    marker_velocity = call(interpolate_kernel, [SMEM, SMEM, VMEM, VMEM], [3, 32, 128])(
        owner, slots, spectrum, weights)
    return new_velocity, marker_velocity.transpose(1, 0, 2)


def solution(mesh):
    both = ("row", "col")
    placed = (
        P(None, "row", "col", None),
        P(both, None, None),
        P(both, None, None, None),
        P(both),
        P(both),
        P(both, None),
        P(both),
    )
    return jax.shard_map(
        local,
        mesh=mesh,
        in_specs=placed,
        out_specs=(P(None, "row", "col", None), P(both, None, None)),
        check_vma=False,
    )
```

```python
import jax
import jax.numpy as jnp
import numpy as np
from jax import lax
from jax.experimental import pallas as pl
from jax.experimental.pallas import tpu as pltpu
from jax.sharding import PartitionSpec as P


DT_STEP = 0.5
VISCOSITY = 0.1
N = 256
FIRST = np.array([k for r in range(16) for k in ((0, 16) if r == 0 else (r, 32 - r))])
F32 = jnp.float32
BF16 = jnp.bfloat16
TURN = 2.0 * np.pi


def split_table(table):
    table = np.asarray(table, np.float32)
    high = table.astype(BF16)
    low = (table - high.astype(np.float32)).astype(BF16)
    return np.stack([high, low])


def rotation(angle):
    rows, cols = angle.shape
    out = np.zeros((rows, 2, 4, cols, 2, 4))
    for j in range(4):
        out[:, 0, j, :, 0, j] = np.cos(angle)
        out[:, 0, j, :, 1, j] = np.sin(angle)
        out[:, 1, j, :, 0, j] = -np.sin(angle)
        out[:, 1, j, :, 1, j] = np.cos(angle)
    return out.reshape(rows * 8, cols * 8)


def z_tables():
    z = np.arange(N)
    fore = np.zeros((32, 2, 4, N))
    back = np.zeros((32, 2, 4, N))
    for k in range(128):
        angle = TURN / N * (k * z % N)
        twice = 2.0 if k else 1.0
        sine = np.sin(angle) if k else -np.cos(np.pi * z)
        fore[k // 4, 0, k % 4] = np.cos(angle)
        fore[k // 4, 1, k % 4] = -sine
        back[k // 4, 0, k % 4] = twice * np.cos(angle) / N
        back[k // 4, 1, k % 4] = -twice * sine / N
    return split_table(fore.reshape(N, N)), split_table(back.reshape(N, N))


def y_tables():
    angle = TURN / 32 * np.outer(FIRST, np.arange(32))
    fore = split_table(rotation(angle))
    back = split_table(rotation(-angle.T) / N)
    small = TURN / 8 * np.outer(np.arange(8), np.arange(8))
    cosine, sine = (np.kron(np.eye(16), f(small)) for f in (np.cos, np.sin))
    lanes_fore = split_table(np.concatenate([cosine, sine], 1))
    lanes_back = split_table(np.concatenate([cosine, -sine], 1))
    phase = TURN / N * np.outer(FIRST, np.tile(np.arange(8), 16))
    twiddle = np.stack([np.cos(phase), np.sin(phase)]).astype(np.float32)[:, :, None, :]
    return fore, back, lanes_fore, lanes_back, twiddle


def x_tables():
    angle = TURN / 16 * np.outer(np.arange(16), np.arange(16))
    pair = np.eye(2)

    def both(turn):
        grid = np.zeros((16, 2, 8, 16, 2, 8))
        base = rotation(turn).reshape(16, 8, 16, 8)
        for p in range(2):
            grid[:, p, :, :, p, :] = base
        return grid

    main = both(angle).reshape(256, 256)
    extra = both(angle).reshape(8, 2, 2, 2, 4, 16, 2, 2, 4)[:, :, :, :, 0]
    extra = extra.transpose(0, 3, 1, 2, 4, 5, 6, 7).copy()
    extra[..., 1:] = 0.0
    extra = extra.reshape(64, 256)
    back_main = both(-angle).reshape(256, 256) / N
    back_extra = both(-angle).reshape(16, 2, 2, 4, 8, 2, 2, 2, 4)[..., 0]
    back_extra = back_extra.transpose(0, 1, 2, 3, 4, 7, 5, 6).copy()
    back_extra[:, :, :, 1:] = 0.0
    back_extra = back_extra.reshape(256, 64) / N
    back = np.concatenate([back_main, back_extra], 1)
    cosine, sine = (np.kron(f(angle), np.eye(8)) for f in (np.cos, np.sin))
    lanes_fore = split_table(np.concatenate([cosine, sine], 1))
    lanes_back = split_table(np.concatenate([cosine, -sine], 1))
    phase = TURN / N * np.outer(np.arange(16), np.repeat(np.arange(16), 8))
    wide = np.zeros((2, 320, 128), np.float32)
    k_main = np.repeat(np.arange(16), 16)
    k_extra = (2 * np.arange(8)[:, None, None, None] + np.arange(2)[None, None, :, None]
               + np.zeros((8, 2, 2, 2), int)).reshape(64)
    p_main = np.tile(np.repeat(np.arange(2), 8), 16)
    p_extra = np.tile(np.arange(2), 32)
    j_main = np.tile(np.arange(4), 64)
    first = np.concatenate([k_main, k_extra])
    wide[0] = np.cos(phase)[first]
    wide[1] = np.sin(phase)[first]
    marks = (first, np.concatenate([p_main, p_extra]), np.concatenate([j_main, np.zeros(64, int)]))
    reverse = np.kron(np.eye(16), np.eye(8)[(7 - np.arange(8))])
    negate = np.kron(np.eye(16), np.eye(8)[(-np.arange(8)) % 8])
    flips = np.concatenate([reverse, negate], 1).astype(BF16)
    return (split_table(main), split_table(extra), split_table(back), lanes_fore, lanes_back,
            wide.reshape(2, 40, 8, 128), marks, flips)


def dot(a, b, dims=((1,), (0,))):
    return lax.dot_general(a, b, (dims, ((), ())), preferred_element_type=F32)


def halves(x):
    high = x.astype(BF16)
    return high, (x - high.astype(F32)).astype(BF16)


def table_left(table, x, dims=((1,), (0,))):
    high, low = halves(x)
    return dot(table[0], high, dims) + dot(table[0], low, dims) + dot(table[1], high, dims)


def table_right(x, table, dims=((1,), (0,))):
    high, low = halves(x)
    return dot(high, table[0], dims) + dot(low, table[0], dims) + dot(high, table[1], dims)


def signs(shape):
    at = lax.broadcasted_iota(jnp.int32, shape, len(shape) - 2)
    return jnp.where(at % 8 < 4, 1.0, -1.0).astype(F32)


def swapped(x):
    return pltpu.roll(x, 4, 1) * signs((1, 8, 128))


def lane_pass(x, table):
    high, low = halves(x)
    twice = jnp.concatenate([table[0], table[0]], 0)
    both = dot(jnp.concatenate([high, low], 1), twice) + dot(high, table[1])
    rows = x.shape[0]
    cosine = both[:, :128].reshape(rows // 8, 8, 128)
    sine = both[:, 128:].reshape(rows // 8, 8, 128)
    return cosine + swapped(sine)


def stacked(x):
    return jnp.concatenate([x[:, 128 * c:128 * c + 128] for c in range(3)], 0)


def unstacked(x):
    rows = x.shape[0] // 3
    return jnp.concatenate([x[rows * c:rows * c + rows] for c in range(3)], 1)


def twiddled(x, cosine, sine):
    groups = cosine.shape[0]
    turned = swapped(x)
    parts = [x[groups * c:groups * c + groups] * cosine + turned[groups * c:groups * c + groups] * sine
             for c in range(3)]
    return jnp.concatenate(parts, 0)


def tile_place(slot, c):
    at = 3 * slot + c
    return at >> 1, at & 1


def lane_half(shape=(8, 128)):
    return lax.broadcasted_iota(jnp.int32, shape, len(shape) - 1) // 64


def to_exponent(largest):
    return jnp.ceil(16.0 * jnp.log(jnp.maximum(largest, 1e-36)))


def steps_per_unit(exponent):
    return 32767.0 * jnp.exp(exponent * (-1.0 / 16.0))


def step(exponent):
    return jnp.exp(exponent * (1.0 / 16.0)) * (1.0 / 32767.0)


def narrow(codes):
    return codes.astype(jnp.int32).astype(jnp.int16)


def wide(codes):
    return codes.astype(jnp.int32).astype(F32)


def row_largest(x):
    return jnp.max(jnp.abs(x), axis=-1, keepdims=True)


def encoded(x):
    largest = jnp.maximum(jnp.maximum(jnp.abs(x[0]), jnp.abs(x[1])), jnp.abs(x[2]))
    largest = jnp.broadcast_to(jnp.max(largest, axis=-1, keepdims=True), largest.shape)
    exponent = to_exponent(largest)
    return jnp.round(x * steps_per_unit(exponent)[None]), exponent


def put_pairs(out, spectrum):
    codes, exponent = encoded(spectrum)
    codes = narrow(codes).reshape(3, 16, 2, 8, 128)
    exponent = exponent.reshape(16, 2, 8, 128)
    for p in range(2):
        for c in range(3):
            out[:, 3 * p + c] = codes[c, :, p]
    half = lane_half((1, 8, 128))
    out[:, 6] = narrow(jnp.where(half == 0, exponent[:, 0], exponent[:, 1]))


def take_pairs(values):
    half = lane_half((1, 8, 128))
    steps = step(wide(values[:, 6]))
    turned = pltpu.roll(steps, 64, 2)
    steps = (jnp.where(half == 0, steps, turned), jnp.where(half == 0, turned, steps))
    parts = []
    for c in range(3):
        pair = [wide(values[:, 3 * p + c]) * steps[p] for p in range(2)]
        parts.append(jnp.stack(pair, 1).reshape(256, 128))
    return jnp.concatenate(parts, 0)


def to_column(row):
    size = row.shape[1]
    same = (lax.broadcasted_iota(jnp.int32, (size, size), 0)
            == lax.broadcasted_iota(jnp.int32, (size, size), 1))
    return jnp.sum(jnp.where(same, row, 0.0), axis=1, keepdims=True)


def spread_kernel(owner_in, brick_in, stiffness_in, rest_in, positions_in, weights_in, out, slots,
                  owner, brick, stiffness, rest_sq, positions, weights, count, cubes, marks, total, arrived):
    pairs = ((weights_in, weights), (positions_in, positions), (rest_in, rest_sq),
             (stiffness_in, stiffness), (owner_in, owner), (brick_in, brick))
    copies = [pltpu.make_async_copy(a, b, arrived.at[i]) for i, (a, b) in enumerate(pairs)]
    for copy in copies:
        copy.start()
    total[...] = jnp.zeros(total.shape, F32)
    for d in range(32):
        count[d] = 0
    for copy in copies:
        copy.wait()
    place = [positions[c].astype(F32) for c in range(3)]
    segment = [pltpu.roll(p, 127, 1) - p for p in place]
    stretch = (segment[0] * segment[0] + segment[1] * segment[1] + segment[2] * segment[2])
    stretch = stretch / to_column(rest_sq[...].astype(F32))
    pull = 0.5 * to_column(stiffness[...].astype(F32)) * (stretch - 1.0)
    force = []
    for c in range(3):
        tension = pull * segment[c]
        force.append(tension - pltpu.roll(tension, 1, 1))
    for n in range(32):
        w0, w1, w2 = (weights[n, a].astype(F32) for a in range(3))
        cells = (w0[:, None, :] * w1[None, :, :]).reshape(64, 128)
        cells = jnp.concatenate([cells, cells], 0)
        pushed = jnp.concatenate([force[c][n:n + 1] * w2 for c in range(3)], 0)
        cells_high, cells_low = halves(cells)
        pushed_high, pushed_low = halves(pushed)
        both = ((1,), (1,))
        cube = (dot(pushed_high, cells_high, both) + dot(pushed_low, cells_high, both)
                + dot(pushed_high, cells_low, both))
        exponent = to_exponent(jnp.broadcast_to(row_largest(cube), cube.shape))
        marks[n] = exponent
        cubes[n] = jnp.round(cube * steps_per_unit(exponent))
    half = lane_half()
    lane = lax.broadcasted_iota(jnp.int32, (8, 128), 1)

    @pl.loop(0, 32)
    def _(n):
        d = owner[n]
        s = count[d]
        count[d] = s + 1
        slots[n] = s
        last = jnp.where(lane == 73 + s, brick[n].astype(F32), 0.0)
        for c in range(3):
            tile, side = tile_place(s, c)
            total[d, tile] += jnp.where(half == side, cubes[n, 8 * c:8 * c + 8, :], 0.0)
            last = jnp.where(lane == 64 + 3 * s + c, marks[n, 8 * c:8 * c + 8, :], last)
        total[d, 4] += last

    out[...] = narrow(total[...])


def advect_kernel(table, velocity, x_low, x_high, y_low, y_high, spectrum, turned):
    u = [velocity[c].reshape(128, 256) for c in range(3)]
    sub = lax.broadcasted_iota(jnp.int32, (16, 8, 256), 1)
    rows = []
    for c in range(3):
        v = velocity[c]
        turned[c] = jnp.transpose(u[c]).reshape(32, 8, 128)
        ahead = jnp.concatenate([v[1:], x_high[c]], 0)
        behind = jnp.concatenate([x_low[c], v[:-1]], 0)
        total = u[0] * (ahead - behind).reshape(128, 256)
        ahead = jnp.where(sub == 7, y_high[c], pltpu.roll(v, 7, 1))
        behind = jnp.where(sub == 0, y_low[c], pltpu.roll(v, 1, 1))
        total = total + u[1] * (ahead - behind).reshape(128, 256)
        total = total + u[2] * (pltpu.roll(u[c], 255, 1) - pltpu.roll(u[c], 1, 1))
        rows.append(u[c] - (0.5 * DT_STEP) * total)
    star = jnp.concatenate(rows, 0)
    spectrum[...] = table_left(table, star, ((1,), (1,)))


def gather_kernel(ids, table, pushes, spectrum, out, force0, force1, force2):
    forces = (force0, force1, force2)
    for force in forces:
        force[...] = jnp.zeros(force.shape, F32)
    half = lane_half()

    @pl.loop(0, 32, unroll=4)
    def _(src):
        tiles = [wide(pushes[src, t]) for t in range(5)]
        turned = [pltpu.roll(tile, 64, 1) for tile in tiles]
        steps = step(tiles[4])
        for slot in range(3):
            brick = ids[src, slot]
            x_half, z_block = brick >> 5, brick & 31
            for c in range(3):
                at = 3 * slot + c
                tile, side = tile_place(slot, c)
                codes = jnp.where(half == side, tiles[tile], turned[tile])
                cube = codes * jnp.broadcast_to(steps[:, 64 + at:65 + at], (8, 128))
                forces[c][z_block] += jnp.where(half == x_half, cube, 0.0)

    field = jnp.concatenate([force[...].reshape(256, 128) for force in forces], 1)
    total = spectrum[...] + table_left(table, DT_STEP * field)
    codes, exponent = encoded(stacked(total).reshape(3, 32, 8, 128))
    for c in range(3):
        out[:, c] = narrow(codes[c])
    out[:, 3] = narrow(exponent)


def reply_kernel(ids, turned, out):
    half = lane_half()
    lane = lax.broadcasted_iota(jnp.int32, (8, 128), 1)

    @pl.loop(0, 32, unroll=4)
    def _(src):
        cubes, largest = [], []
        for slot in range(3):
            brick = ids[src, slot]
            x_half, z_block = brick >> 5, brick & 31
            for c in range(3):
                tile = turned[c, z_block]
                cube = jnp.where(half == x_half, tile, pltpu.roll(tile, 64, 1))
                largest.append(jnp.max(jnp.abs(cube), axis=0, keepdims=True))
                cubes.append(cube)
        largest = jnp.concatenate(largest + largest[:7], 0)
        exponent = to_exponent(jnp.broadcast_to(row_largest(largest), (16, 128)))
        steps = steps_per_unit(exponent)
        codes = [jnp.round(cube * steps[at:at + 1]) for at, cube in enumerate(cubes)]
        last = jnp.zeros((8, 128), F32)
        for at in range(9):
            last = jnp.where(lane == 64 + at, exponent[at:at + 1], last)
        codes.append(last)
        for t in range(5):
            out[src, t] = narrow(jnp.where(half == 0, codes[2 * t], codes[2 * t + 1]))


def interpolate(owner, slots, replies, weights, out):
    half = lane_half()
    lane = lax.broadcasted_iota(jnp.int32, (8, 128), 1)
    for n in range(32):
        d, s = owner[n], slots[n]
        steps = step(wide(replies[d, 7]))
        parts = []
        for c in range(3):
            tile, side = tile_place(s, c)
            cube = wide(replies[d, 3 + tile])
            cube = jnp.where(half == side, cube, pltpu.roll(cube, 64, 1))
            own = jnp.sum(jnp.where(lane == 64 + 3 * s + c, steps, 0.0), axis=1, keepdims=True)
            parts.append(cube * own)
        cube_high, cube_low = halves(jnp.concatenate(parts, 0)[:, :64])
        w0, w1, w2 = (weights[n, a].astype(F32) for a in range(3))
        cells_high, cells_low = halves((w0[:, None, :] * w1[None, :, :]).reshape(64, 128))
        partial = dot(cube_high, cells_high) + dot(cube_low, cells_high) + dot(cube_high, cells_low)
        for c in range(3):
            out[c, n:n + 1] = jnp.sum(partial[8 * c:8 * c + 8] * w2, axis=0, keepdims=True)


def y_kernel(left, lanes, twiddle, values, out):
    steps = step(wide(values[:, 3]))
    spectrum = [(wide(values[:, c]) * steps).reshape(256, 128) for c in range(3)]
    spectrum = table_left(left, jnp.concatenate(spectrum, 1))
    spectrum = stacked(spectrum).reshape(96, 8, 128)
    spectrum = twiddled(spectrum, twiddle[0], twiddle[1])
    spectrum = lane_pass(spectrum.reshape(768, 128), lanes)
    put_pairs(out, spectrum.reshape(3, 32, 8, 128))


def x_kernel(flags, left, left_extra, back, lanes, lanes_back, twiddle, flips, waves, damping, values, out):
    packed = take_pairs(values)
    high, low = halves(packed)
    flipped = dot(jnp.concatenate([high, low], 1), jnp.concatenate([flips[...], flips[...]], 0))
    by_pair = (3, 16, 2, 8, 128)
    reverse = flipped[:, :128].reshape(by_pair)
    negate = flipped[:, 128:].reshape(by_pair)
    packed = packed.reshape(by_pair)
    own = flags[0] == 1
    first = jnp.where(own, negate[:, :, 0:1], reverse[:, :, 1:2])
    second = jnp.where(own, reverse[:, :, 1:2], reverse[:, :, 0:1])
    mirrored = jnp.concatenate([first, second], 2) * signs((1, 1, 1, 8, 128))
    sub = lax.broadcasted_iota(jnp.int32, (1, 1, 1, 8, 128), 3)
    lowest = (sub % 4 == 0) & (flags[1] == 1)
    main = jnp.where(lowest, 0.5 * (packed + mirrored), packed)
    extra = jnp.where(lowest, 0.5 * (packed - mirrored), 0.0)
    main = table_left(left, unstacked(main.reshape(768, 128)))
    extra = table_left(left_extra, unstacked(extra.reshape(768, 128)))
    spectrum = stacked(jnp.concatenate([main, extra], 0)).reshape(120, 8, 128)
    spectrum = twiddled(spectrum, twiddle[0], twiddle[1])
    spectrum = lane_pass(spectrum.reshape(960, 128), lanes).reshape(3, 320, 128)
    normal = waves[0] * spectrum[0] + waves[1] * spectrum[1] + waves[2] * spectrum[2]
    damp = damping[...]
    projected = jnp.concatenate([(spectrum[c] - waves[c] * normal) * damp for c in range(3)], 0)
    projected = lane_pass(projected, lanes_back)
    projected = twiddled(projected, twiddle[0], -twiddle[1])
    projected = unstacked(projected.reshape(960, 128))
    put_pairs(out, stacked(table_left(back, projected)).reshape(3, 32, 8, 128))


def y_back_kernel(back, lanes, twiddle, values, replies, out):
    spectrum = lane_pass(take_pairs(values), lanes)
    spectrum = twiddled(spectrum, twiddle[0], -twiddle[1])
    spectrum = table_left(back, unstacked(spectrum.reshape(768, 128)))
    codes, exponent = encoded(stacked(spectrum).reshape(3, 32, 8, 128))
    for c in range(3):
        out[:, c] = narrow(codes[c])
    for t in range(4):
        out[:, 3 + t] = replies[:, t]
    lane = lax.broadcasted_iota(jnp.int32, (1, 8, 128), 2)
    out[:, 7] = narrow(jnp.where(lane == 76, exponent, wide(replies[:, 4])))


def last_kernel(owner, slots, back, values, weights, out, markers):
    interpolate(owner, slots, values, weights, markers)
    steps = step(wide(values[:, 7])[:, :, 76:77])
    spectrum = [(wide(values[:, c]) * steps).reshape(256, 128) for c in range(3)]
    field = table_right(jnp.transpose(jnp.concatenate(spectrum, 1)), back)
    out[...] = field.reshape(3, 16, 8, 256)


VMEM = pl.BlockSpec(memory_space=pltpu.VMEM)
SMEM = pl.BlockSpec(memory_space=pltpu.SMEM)
HBM = pl.BlockSpec(memory_space=pltpu.HBM)


def call(kernel, specs, shapes, scratch=(), out_specs=None):
    single = not isinstance(shapes, tuple)
    structs = [jax.ShapeDtypeStruct(s, F32) if isinstance(s, list) else s
               for s in ((shapes,) if single else shapes)]
    outs = out_specs or [VMEM] * len(structs)
    return pl.pallas_call(
        kernel,
        out_shape=structs[0] if single else structs,
        in_specs=specs,
        out_specs=outs[0] if single else outs,
        scratch_shapes=list(scratch),
        compiler_params=pltpu.CompilerParams(vmem_limit_bytes=48 << 20),
    )


def codes_of(count, tiles):
    return jax.ShapeDtypeStruct((count, tiles, 8, 128), jnp.int16)


def signed(indices):
    return jnp.where(indices <= (N - 1) // 2, indices, indices - N)


def wave_tables(marks, row, col):
    first, pair, slot = (jnp.asarray(m, jnp.int32)[:, None] for m in marks)
    lane = jnp.arange(128, dtype=jnp.int32)[None, :]
    nyquist = jnp.arange(320, dtype=jnp.int32)[:, None] >= 256
    second = jnp.where(row == 0, 16, 32 - row)
    index_x = first + 16 * (lane // 8)
    index_y = jnp.where(pair == 0, row, second) + 32 * (lane % 8)
    index_z = jnp.where(nyquist, N // 2, 4 * col + slot) + 0 * lane
    scale = 2.0 * jnp.pi / N
    full_sq, waves = 0.0, []
    for index in (index_x, index_y, index_z):
        full = scale * signed(index).astype(F32)
        full_sq = full_sq + full * full
        waves.append(jnp.where(2 * index == N, 0.0, full))
    wave_sq = waves[0] * waves[0] + waves[1] * waves[1] + waves[2] * waves[2]
    still = wave_sq == 0.0
    inverse = jnp.where(still, 0.0, lax.rsqrt(jnp.where(still, 1.0, wave_sq)))
    units = jnp.stack([w * inverse for w in waves])
    return units, 1.0 / (1.0 + DT_STEP * VISCOSITY * full_sq)


def moved(x, axis):
    return lax.all_to_all(x, axis, split_axis=0, concat_axis=0, tiled=True)


def neighbours(plane_low, plane_high, axis):
    count = lax.axis_size(axis)
    up = [(i, (i + 1) % count) for i in range(count)]
    down = [((i + 1) % count, i) for i in range(count)]
    return lax.ppermute(plane_high, axis, up), lax.ppermute(plane_low, axis, down)


def local(velocity, positions, weights, stiffness, rest_sq, owner_column, brick_index):
    row, col = lax.axis_index("row"), lax.axis_index("col")
    z_fore, z_back = z_tables()
    y_fore, y_back, y_lanes, y_lanes_back, y_twiddle = y_tables()
    x_fore, x_extra, x_back, x_lanes, x_lanes_back, x_twiddle, marks, flips = x_tables()
    flags = jnp.stack([row == 0, col == 0]).astype(jnp.int32)
    units, damping = wave_tables(marks, row, col)

    owner = owner_column.reshape(32)
    spread_outs = (jax.ShapeDtypeStruct((32, 5, 8, 128), jnp.int16), jax.ShapeDtypeStruct((32,), jnp.int32))
    pushes, slots = call(
        spread_kernel, [HBM] * 6, spread_outs,
        [pltpu.SMEM((32,), jnp.int32), pltpu.SMEM((32,), jnp.int32), pltpu.VMEM((1, 32), BF16),
         pltpu.VMEM((1, 32), BF16), pltpu.VMEM((3, 32, 128), BF16), pltpu.VMEM((32, 3, 8, 128), BF16),
         pltpu.SMEM((32,), jnp.int32), pltpu.VMEM((32, 24, 128), F32), pltpu.VMEM((32, 24, 128), F32),
         pltpu.VMEM((32, 5, 8, 128), F32), pltpu.SemaphoreType.DMA((6,))], [VMEM, SMEM],
    )(owner, brick_index, stiffness.reshape(1, 32), rest_sq.reshape(1, 32), positions.transpose(1, 0, 2), weights)
    planes = (velocity[:, :1], velocity[:, 15:], velocity[:, :, :1], velocity[:, :, 7:])
    planes, pushes, slots = lax.optimization_barrier((planes, pushes, slots))
    x_low, x_high = neighbours(planes[0], planes[1], "row")
    y_low, y_high = neighbours(planes[2], planes[3], "col")
    pushes = moved(pushes, "col")
    ids = pushes[:, 4, 0, 73:76].astype(jnp.int32)

    spectrum, turned = call(advect_kernel, [VMEM] * 6, ([256, 384], [3, 32, 8, 128]))(
        z_fore, velocity, x_low, x_high, y_low, y_high)
    spectrum = call(gather_kernel, [SMEM, VMEM, VMEM, VMEM], codes_of(32, 4),
                    [pltpu.VMEM((32, 8, 128), F32)] * 3)(ids, z_fore, pushes, spectrum)
    spectrum = moved(spectrum, "col")
    spectrum = call(y_kernel, [VMEM] * 4, codes_of(16, 7))(y_fore, y_lanes, y_twiddle, spectrum)
    spectrum = moved(spectrum, "row")
    spectrum = call(x_kernel, [SMEM] + [VMEM] * 10, codes_of(16, 7))(
        flags, x_fore, x_extra, x_back, x_lanes, x_lanes_back, x_twiddle, flips, units, damping, spectrum)
    spectrum = moved(spectrum, "row")
    replies = call(reply_kernel, [SMEM, VMEM], codes_of(32, 5))(ids, turned)
    spectrum = call(y_back_kernel, [VMEM] * 5, codes_of(32, 8))(
        y_back, y_lanes_back, y_twiddle, spectrum, replies)
    spectrum = moved(spectrum, "col")
    new_velocity, marker_velocity = call(
        last_kernel, [SMEM, SMEM, VMEM, VMEM, VMEM], ([3, 16, 8, 256], [3, 32, 128]))(
        owner, slots, z_back, spectrum, weights)
    return new_velocity, marker_velocity.transpose(1, 0, 2)


def solution(mesh):
    both = ("row", "col")
    placed = (
        P(None, "row", "col", None),
        P(both, None, None),
        P(both, None, None, None),
        P(both),
        P(both),
        P(both, None),
        P(both),
    )
    return jax.shard_map(
        local,
        mesh=mesh,
        in_specs=placed,
        out_specs=(P(None, "row", "col", None), P(both, None, None)),
        check_vma=False,
    )
```

```python
import jax
import jax.numpy as jnp
import numpy as np
from jax import lax
from jax.experimental import pallas as pl
from jax.experimental.pallas import tpu as pltpu
from jax.sharding import PartitionSpec as P


DT_STEP = 0.5
VISCOSITY = 0.1
N = 256
FIRST = np.array([k for r in range(16) for k in ((0, 16) if r == 0 else (r, 32 - r))])
F32 = jnp.float32
BF16 = jnp.bfloat16
TURN = 2.0 * np.pi


def split_table(table):
    table = np.asarray(table, np.float32)
    high = table.astype(BF16)
    low = (table - high.astype(np.float32)).astype(BF16)
    return np.stack([high, low])


def rotation(angle):
    rows, cols = angle.shape
    out = np.zeros((rows, 2, 4, cols, 2, 4))
    for j in range(4):
        out[:, 0, j, :, 0, j] = np.cos(angle)
        out[:, 0, j, :, 1, j] = np.sin(angle)
        out[:, 1, j, :, 0, j] = -np.sin(angle)
        out[:, 1, j, :, 1, j] = np.cos(angle)
    return out.reshape(rows * 8, cols * 8)


def z_tables():
    z = np.arange(N)
    fore = np.zeros((32, 2, 4, N))
    back = np.zeros((32, 2, 4, N))
    for k in range(128):
        angle = TURN / N * (k * z % N)
        twice = 2.0 if k else 1.0
        sine = np.sin(angle) if k else -np.cos(np.pi * z)
        fore[k // 4, 0, k % 4] = np.cos(angle)
        fore[k // 4, 1, k % 4] = -sine
        back[k // 4, 0, k % 4] = twice * np.cos(angle) / N
        back[k // 4, 1, k % 4] = -twice * sine / N
    return split_table(fore.reshape(N, N)), split_table(back.reshape(N, N))


def y_tables():
    angle = TURN / 32 * np.outer(FIRST, np.arange(32))
    fore = split_table(rotation(angle))
    back = split_table(rotation(-angle.T) / N)
    small = TURN / 8 * np.outer(np.arange(8), np.arange(8))
    cosine, sine = (np.kron(np.eye(16), f(small)) for f in (np.cos, np.sin))
    lanes_fore = split_table(np.concatenate([cosine, sine], 1))
    lanes_back = split_table(np.concatenate([cosine, -sine], 1))
    phase = TURN / N * np.outer(FIRST, np.tile(np.arange(8), 16))
    twiddle = np.stack([np.cos(phase), np.sin(phase)]).astype(np.float32)[:, :, None, :]
    return fore, back, lanes_fore, lanes_back, twiddle


def x_tables():
    angle = TURN / 16 * np.outer(np.arange(16), np.arange(16))
    pair = np.eye(2)

    def both(turn):
        grid = np.zeros((16, 2, 8, 16, 2, 8))
        base = rotation(turn).reshape(16, 8, 16, 8)
        for p in range(2):
            grid[:, p, :, :, p, :] = base
        return grid

    main = both(angle).reshape(256, 256)
    extra = both(angle).reshape(8, 2, 2, 2, 4, 16, 2, 2, 4)[:, :, :, :, 0]
    extra = extra.transpose(0, 3, 1, 2, 4, 5, 6, 7).copy()
    extra[..., 1:] = 0.0
    extra = extra.reshape(64, 256)
    back_main = both(-angle).reshape(256, 256) / N
    back_extra = both(-angle).reshape(16, 2, 2, 4, 8, 2, 2, 2, 4)[..., 0]
    back_extra = back_extra.transpose(0, 1, 2, 3, 4, 7, 5, 6).copy()
    back_extra[:, :, :, 1:] = 0.0
    back_extra = back_extra.reshape(256, 64) / N
    back = np.concatenate([back_main, back_extra], 1)
    cosine, sine = (np.kron(f(angle), np.eye(8)) for f in (np.cos, np.sin))
    lanes_fore = split_table(np.concatenate([cosine, sine], 1))
    lanes_back = split_table(np.concatenate([cosine, -sine], 1))
    phase = TURN / N * np.outer(np.arange(16), np.repeat(np.arange(16), 8))
    wide = np.zeros((2, 320, 128), np.float32)
    k_main = np.repeat(np.arange(16), 16)
    k_extra = (2 * np.arange(8)[:, None, None, None] + np.arange(2)[None, None, :, None]
               + np.zeros((8, 2, 2, 2), int)).reshape(64)
    p_main = np.tile(np.repeat(np.arange(2), 8), 16)
    p_extra = np.tile(np.arange(2), 32)
    j_main = np.tile(np.arange(4), 64)
    first = np.concatenate([k_main, k_extra])
    wide[0] = np.cos(phase)[first]
    wide[1] = np.sin(phase)[first]
    marks = (first, np.concatenate([p_main, p_extra]), np.concatenate([j_main, np.zeros(64, int)]))
    reverse = np.kron(np.eye(16), np.eye(8)[(7 - np.arange(8))])
    negate = np.kron(np.eye(16), np.eye(8)[(-np.arange(8)) % 8])
    flips = np.concatenate([reverse, negate], 1).astype(BF16)
    return (split_table(main), split_table(extra), split_table(back), lanes_fore, lanes_back,
            wide.reshape(2, 40, 8, 128), marks, flips)


def dot(a, b, dims=((1,), (0,))):
    return lax.dot_general(a, b, (dims, ((), ())), preferred_element_type=F32)


def halves(x):
    high = x.astype(BF16)
    return high, (x - high.astype(F32)).astype(BF16)


def table_left(table, x, dims=((1,), (0,))):
    high, low = halves(x)
    return dot(table[0], high, dims) + dot(table[0], low, dims) + dot(table[1], high, dims)


def table_right(x, table, dims=((1,), (0,))):
    high, low = halves(x)
    return dot(high, table[0], dims) + dot(low, table[0], dims) + dot(high, table[1], dims)


def signs(shape):
    at = lax.broadcasted_iota(jnp.int32, shape, len(shape) - 2)
    return jnp.where(at % 8 < 4, 1.0, -1.0).astype(F32)


def swapped(x):
    return pltpu.roll(x, 4, 1) * signs((1, 8, 128))


def lane_pass(x, table):
    high, low = halves(x)
    twice = jnp.concatenate([table[0], table[0]], 0)
    both = dot(jnp.concatenate([high, low], 1), twice) + dot(high, table[1])
    rows = x.shape[0]
    cosine = both[:, :128].reshape(rows // 8, 8, 128)
    sine = both[:, 128:].reshape(rows // 8, 8, 128)
    return cosine + swapped(sine)


def stacked(x):
    return jnp.concatenate([x[:, 128 * c:128 * c + 128] for c in range(3)], 0)


def unstacked(x):
    rows = x.shape[0] // 3
    return jnp.concatenate([x[rows * c:rows * c + rows] for c in range(3)], 1)


def twiddled(x, cosine, sine):
    groups = cosine.shape[0]
    turned = swapped(x)
    parts = [x[groups * c:groups * c + groups] * cosine + turned[groups * c:groups * c + groups] * sine
             for c in range(3)]
    return jnp.concatenate(parts, 0)


def tile_place(slot, c):
    at = 3 * slot + c
    return at >> 1, at & 1


def lane_half(shape=(8, 128)):
    return lax.broadcasted_iota(jnp.int32, shape, len(shape) - 1) // 64


def to_exponent(largest):
    return jnp.ceil(16.0 * jnp.log(jnp.maximum(largest, 1e-36)))


def steps_per_unit(exponent):
    return 32767.0 * jnp.exp(exponent * (-1.0 / 16.0))


def step(exponent):
    return jnp.exp(exponent * (1.0 / 16.0)) * (1.0 / 32767.0)


def narrow(codes):
    return codes.astype(jnp.int32).astype(jnp.int16)


def wide(codes):
    return codes.astype(jnp.int32).astype(F32)


def row_largest(x):
    return jnp.max(jnp.abs(x), axis=-1, keepdims=True)


def encoded(x):
    largest = jnp.max(jnp.abs(x), axis=0)
    largest = jnp.broadcast_to(jnp.max(largest, axis=-1, keepdims=True), largest.shape)
    exponent = to_exponent(largest)
    return jnp.round(x * steps_per_unit(exponent)[None]), exponent


def put_pairs(out, spectrum):
    codes, exponent = encoded(spectrum)
    codes = narrow(codes).reshape(3, 16, 2, 8, 128)
    exponent = exponent.reshape(16, 2, 8, 128)
    for p in range(2):
        for c in range(3):
            out[:, 3 * p + c] = codes[c, :, p]
    half = lane_half((1, 8, 128))
    out[:, 6] = narrow(jnp.where(half == 0, exponent[:, 0], exponent[:, 1]))


def take_pairs(values):
    half = lane_half((1, 8, 128))
    steps = step(wide(values[:, 6]))
    turned = pltpu.roll(steps, 64, 2)
    steps = (jnp.where(half == 0, steps, turned), jnp.where(half == 0, turned, steps))
    parts = []
    for c in range(3):
        pair = [wide(values[:, 3 * p + c]) * steps[p] for p in range(2)]
        parts.append(jnp.stack(pair, 1).reshape(256, 128))
    return jnp.concatenate(parts, 0)


def to_column(row):
    size = row.shape[1]
    same = (lax.broadcasted_iota(jnp.int32, (size, size), 0)
            == lax.broadcasted_iota(jnp.int32, (size, size), 1))
    return jnp.sum(jnp.where(same, row, 0.0), axis=1, keepdims=True)


def spread_kernel(owner_in, brick_in, stiffness_in, rest_in, positions_in, weights_in, velocity,
                  out, slots, x_first, x_last, y_last, owner, brick, stiffness, rest_sq, positions, weights, count, cubes, marks, total, arrived):
    pairs = ((weights_in, weights), (positions_in, positions), (rest_in, rest_sq),
             (stiffness_in, stiffness), (owner_in, owner), (brick_in, brick))
    copies = [pltpu.make_async_copy(a, b, arrived.at[i]) for i, (a, b) in enumerate(pairs)]
    for copy in copies:
        copy.start()
    total[...] = jnp.zeros(total.shape, F32)
    for d in range(32):
        count[d] = 0
    for c in range(3):
        x_first[c] = velocity[c, 0:1]
        x_last[c] = velocity[c, 15:16]
        y_last[c] = velocity[c, :, 7:8, :]
    for copy in copies:
        copy.wait()
    place = [positions[c].astype(F32) for c in range(3)]
    segment = [pltpu.roll(p, 127, 1) - p for p in place]
    stretch = (segment[0] * segment[0] + segment[1] * segment[1] + segment[2] * segment[2])
    stretch = stretch / to_column(rest_sq[...].astype(F32))
    pull = 0.5 * to_column(stiffness[...].astype(F32)) * (stretch - 1.0)
    force = []
    for c in range(3):
        tension = pull * segment[c]
        force.append(tension - pltpu.roll(tension, 1, 1))
    largest = []
    for n in range(32):
        w0, w1, w2 = (weights[n, a].astype(F32) for a in range(3))
        cells = (w0[:, None, :] * w1[None, :, :]).reshape(64, 128)
        cells = jnp.concatenate([cells, cells], 0)
        pushed = jnp.concatenate([force[c][n:n + 1] * w2 for c in range(3)], 0)
        cells_high, cells_low = halves(cells)
        pushed_high, pushed_low = halves(pushed)
        both = ((1,), (1,))
        cube = dot(jnp.concatenate([pushed_high, pushed_low], 1), jnp.concatenate([cells_high, cells_high], 1), both)
        cube = cube + dot(pushed_high, cells_low, both)
        cubes[n] = cube
        largest += [jnp.max(jnp.abs(cube[8 * c:8 * c + 8]), axis=0, keepdims=True) for c in range(3)]
    largest = jnp.concatenate(largest, 0)
    exponent = to_exponent(jnp.broadcast_to(row_largest(largest), (96, 128)))
    marks[...] = exponent
    steps = steps_per_unit(exponent)
    for n in range(32):
        for c in range(3):
            cubes[n, 8 * c:8 * c + 8] = jnp.round(cubes[n, 8 * c:8 * c + 8] * steps[3 * n + c:3 * n + c + 1])
    half = lane_half()
    lane = lax.broadcasted_iota(jnp.int32, (8, 128), 1)

    @pl.loop(0, 32)
    def _(n):
        d = owner[n]
        s = count[d]
        count[d] = s + 1
        slots[n] = s
        last = jnp.where(lane == 73 + s, brick[n].astype(F32), 0.0)
        for c in range(3):
            tile, side = tile_place(s, c)
            total[d, tile] += jnp.where(half == side, cubes[n, 8 * c:8 * c + 8, :], 0.0)
            last = jnp.where(lane == 64 + 3 * s + c, marks[pl.ds(3 * n + c, 1), :], last)
        total[d, 4] += last

    out[...] = narrow(total[...])


def advect_kernel(table, velocity, x_low, x_high, y_low, spectrum, turned):
    u = [velocity[c].reshape(128, 256) for c in range(3)]
    sub = lax.broadcasted_iota(jnp.int32, (16, 8, 256), 1)
    rows = []
    beyond = jnp.zeros((16, 8, 256), F32)
    for c in range(3):
        v = velocity[c]
        beyond = jnp.where(sub == c, v[:, 0:1, :], beyond)
        turned[c] = jnp.transpose(u[c]).reshape(32, 8, 128)
        ahead = jnp.concatenate([v[1:], x_high[c]], 0)
        behind = jnp.concatenate([x_low[c], v[:-1]], 0)
        total = u[0] * (ahead - behind).reshape(128, 256)
        ahead = jnp.where(sub == 7, 0.0, pltpu.roll(v, 7, 1))
        behind = jnp.where(sub == 0, y_low[c], pltpu.roll(v, 1, 1))
        total = total + u[1] * (ahead - behind).reshape(128, 256)
        total = total + u[2] * (pltpu.roll(u[c], 255, 1) - pltpu.roll(u[c], 1, 1))
        rows.append(u[c] - (0.5 * DT_STEP) * total)
    beyond = (-0.5 * DT_STEP) * y_low[1] * beyond
    star = jnp.concatenate(rows + [beyond.reshape(128, 256)], 0)
    spectrum[...] = table_left(table, star, ((1,), (1,)))


def gather_kernel(ids, table, pushes, spectrum, out, force0, force1, force2):
    forces = (force0, force1, force2)
    for force in forces:
        force[...] = jnp.zeros(force.shape, F32)
    half = lane_half()

    @pl.loop(0, 32, unroll=4)
    def _(src):
        tiles = [wide(pushes[src, t]) for t in range(5)]
        turned = [pltpu.roll(tile, 64, 1) for tile in tiles]
        steps = step(tiles[4])
        for slot in range(3):
            brick = ids[src, slot]
            x_half, z_block = brick >> 5, brick & 31
            for c in range(3):
                at = 3 * slot + c
                tile, side = tile_place(slot, c)
                codes = jnp.where(half == side, tiles[tile], turned[tile])
                cube = codes * jnp.broadcast_to(steps[:, 64 + at:65 + at], (8, 128))
                forces[c][z_block] += jnp.where(half == x_half, cube, 0.0)

    field = jnp.concatenate([force[...].reshape(256, 128) for force in forces], 1)
    total = spectrum[:, :384] + table_left(table, DT_STEP * field)
    total = jnp.concatenate([stacked(total), spectrum[:, 384:]], 0)
    codes, exponent = encoded(total.reshape(4, 32, 8, 128))
    for t in range(4):
        out[:, t] = narrow(codes[t])
    out[:, 4] = narrow(exponent)


def reply_kernel(ids, turned, out):
    half = lane_half()
    lane = lax.broadcasted_iota(jnp.int32, (8, 128), 1)

    @pl.loop(0, 32, unroll=4)
    def _(src):
        cubes, largest = [], []
        for slot in range(3):
            brick = ids[src, slot]
            x_half, z_block = brick >> 5, brick & 31
            for c in range(3):
                tile = turned[c, z_block]
                cube = jnp.where(half == x_half, tile, pltpu.roll(tile, 64, 1))
                largest.append(jnp.max(jnp.abs(cube), axis=0, keepdims=True))
                cubes.append(cube)
        largest = jnp.concatenate(largest + largest[:7], 0)
        exponent = to_exponent(jnp.broadcast_to(row_largest(largest), (16, 128)))
        steps = steps_per_unit(exponent)
        codes = [jnp.round(cube * steps[at:at + 1]) for at, cube in enumerate(cubes)]
        last = jnp.zeros((8, 128), F32)
        for at in range(9):
            last = jnp.where(lane == 64 + at, exponent[at:at + 1], last)
        codes.append(last)
        for t in range(5):
            out[src, t] = narrow(jnp.where(half == 0, codes[2 * t], codes[2 * t + 1]))


def interpolate(owner, slots, replies, weights, out):
    half = lane_half()
    lane = lax.broadcasted_iota(jnp.int32, (8, 128), 1)
    for n in range(32):
        d, s = owner[n], slots[n]
        steps = step(wide(replies[d, 7]))
        parts = []
        for c in range(3):
            tile, side = tile_place(s, c)
            cube = wide(replies[d, 3 + tile])
            cube = jnp.where(half == side, cube, pltpu.roll(cube, 64, 1))
            own = jnp.sum(jnp.where(lane == 64 + 3 * s + c, steps, 0.0), axis=1, keepdims=True)
            parts.append(cube * own)
        cube_high, cube_low = halves(jnp.concatenate(parts, 0)[:, :64])
        w0, w1, w2 = (weights[n, a].astype(F32) for a in range(3))
        cells_high, cells_low = halves((w0[:, None, :] * w1[None, :, :]).reshape(64, 128))
        partial = dot(cube_high, cells_high) + dot(cube_low, cells_high) + dot(cube_high, cells_low)
        for c in range(3):
            out[c, n:n + 1] = jnp.sum(partial[8 * c:8 * c + 8] * w2, axis=0, keepdims=True)


def y_kernel(left, lanes, twiddle, values, out):
    steps = step(wide(values[:, 4]))
    beyond = wide(values[:, 3]) * steps
    beyond = jnp.concatenate([beyond[1:], beyond[:1]], 0)
    last = lax.broadcasted_iota(jnp.int32, (1, 8, 128), 2) % 8 == 7
    spectrum = []
    for c in range(3):
        part = wide(values[:, c]) * steps + jnp.where(last, pltpu.roll(beyond, 7 - c, 2), 0.0)
        spectrum.append(part.reshape(256, 128))
    spectrum = table_left(left, jnp.concatenate(spectrum, 1))
    spectrum = stacked(spectrum).reshape(96, 8, 128)
    spectrum = twiddled(spectrum, twiddle[0], twiddle[1])
    spectrum = lane_pass(spectrum.reshape(768, 128), lanes)
    put_pairs(out, spectrum.reshape(3, 32, 8, 128))


def x_kernel(flags, left, left_extra, back, lanes, lanes_back, twiddle, flips, waves, damping, values, out):
    packed = take_pairs(values)
    high, low = halves(packed)
    flipped = dot(jnp.concatenate([high, low], 1), jnp.concatenate([flips[...], flips[...]], 0))
    by_pair = (3, 16, 2, 8, 128)
    reverse = flipped[:, :128].reshape(by_pair)
    negate = flipped[:, 128:].reshape(by_pair)
    packed = packed.reshape(by_pair)
    own = flags[0] == 1
    first = jnp.where(own, negate[:, :, 0:1], reverse[:, :, 1:2])
    second = jnp.where(own, reverse[:, :, 1:2], reverse[:, :, 0:1])
    mirrored = jnp.concatenate([first, second], 2) * signs((1, 1, 1, 8, 128))
    sub = lax.broadcasted_iota(jnp.int32, (1, 1, 1, 8, 128), 3)
    lowest = (sub % 4 == 0) & (flags[1] == 1)
    main = jnp.where(lowest, 0.5 * (packed + mirrored), packed)
    extra = jnp.where(lowest, 0.5 * (packed - mirrored), 0.0)
    main = table_left(left, unstacked(main.reshape(768, 128)))
    extra = table_left(left_extra, unstacked(extra.reshape(768, 128)))
    spectrum = stacked(jnp.concatenate([main, extra], 0)).reshape(120, 8, 128)
    spectrum = twiddled(spectrum, twiddle[0], twiddle[1])
    spectrum = lane_pass(spectrum.reshape(960, 128), lanes).reshape(3, 320, 128)
    normal = waves[0] * spectrum[0] + waves[1] * spectrum[1] + waves[2] * spectrum[2]
    damp = damping[...]
    projected = jnp.concatenate([(spectrum[c] - waves[c] * normal) * damp for c in range(3)], 0)
    projected = lane_pass(projected, lanes_back)
    projected = twiddled(projected, twiddle[0], -twiddle[1])
    projected = unstacked(projected.reshape(960, 128))
    put_pairs(out, stacked(table_left(back, projected)).reshape(3, 32, 8, 128))


def y_back_kernel(back, lanes, twiddle, values, replies, out):
    spectrum = lane_pass(take_pairs(values), lanes)
    spectrum = twiddled(spectrum, twiddle[0], -twiddle[1])
    spectrum = table_left(back, unstacked(spectrum.reshape(768, 128)))
    codes, exponent = encoded(stacked(spectrum).reshape(3, 32, 8, 128))
    for c in range(3):
        out[:, c] = narrow(codes[c])
    for t in range(4):
        out[:, 3 + t] = replies[:, t]
    lane = lax.broadcasted_iota(jnp.int32, (1, 8, 128), 2)
    out[:, 7] = narrow(jnp.where(lane == 76, exponent, wide(replies[:, 4])))


def last_kernel(owner, slots, back, values, weights, out, markers):
    interpolate(owner, slots, values, weights, markers)
    steps = step(wide(values[:, 7])[:, :, 76:77])
    spectrum = [(wide(values[:, c]) * steps).reshape(256, 128) for c in range(3)]
    field = table_right(jnp.transpose(jnp.concatenate(spectrum, 1)), back)
    out[...] = field.reshape(3, 16, 8, 256)


VMEM = pl.BlockSpec(memory_space=pltpu.VMEM)
SMEM = pl.BlockSpec(memory_space=pltpu.SMEM)
HBM = pl.BlockSpec(memory_space=pltpu.HBM)


def call(kernel, specs, shapes, scratch=(), out_specs=None):
    single = not isinstance(shapes, tuple)
    structs = [jax.ShapeDtypeStruct(s, F32) if isinstance(s, list) else s
               for s in ((shapes,) if single else shapes)]
    outs = out_specs or [VMEM] * len(structs)
    return pl.pallas_call(
        kernel,
        out_shape=structs[0] if single else structs,
        in_specs=specs,
        out_specs=outs[0] if single else outs,
        scratch_shapes=list(scratch),
        compiler_params=pltpu.CompilerParams(vmem_limit_bytes=48 << 20),
    )


def codes_of(count, tiles):
    return jax.ShapeDtypeStruct((count, tiles, 8, 128), jnp.int16)


def signed(indices):
    return jnp.where(indices <= (N - 1) // 2, indices, indices - N)


def wave_tables(marks, row, col):
    first, pair, slot = (jnp.asarray(m, jnp.int32)[:, None] for m in marks)
    lane = jnp.arange(128, dtype=jnp.int32)[None, :]
    nyquist = jnp.arange(320, dtype=jnp.int32)[:, None] >= 256
    second = jnp.where(row == 0, 16, 32 - row)
    index_x = first + 16 * (lane // 8)
    index_y = jnp.where(pair == 0, row, second) + 32 * (lane % 8)
    index_z = jnp.where(nyquist, N // 2, 4 * col + slot) + 0 * lane
    scale = 2.0 * jnp.pi / N
    full_sq, waves = 0.0, []
    for index in (index_x, index_y, index_z):
        full = scale * signed(index).astype(F32)
        full_sq = full_sq + full * full
        waves.append(jnp.where(2 * index == N, 0.0, full))
    wave_sq = waves[0] * waves[0] + waves[1] * waves[1] + waves[2] * waves[2]
    still = wave_sq == 0.0
    inverse = jnp.where(still, 0.0, lax.rsqrt(jnp.where(still, 1.0, wave_sq)))
    units = jnp.stack([w * inverse for w in waves])
    return units, 1.0 / (1.0 + DT_STEP * VISCOSITY * full_sq)


def moved(x, axis):
    return lax.all_to_all(x, axis, split_axis=0, concat_axis=0, tiled=True)


def shifted(plane, axis, by):
    count = lax.axis_size(axis)
    return lax.ppermute(plane, axis, [(i, (i + by) % count) for i in range(count)])


def local(velocity, positions, weights, stiffness, rest_sq, owner_column, brick_index):
    row, col = lax.axis_index("row"), lax.axis_index("col")
    z_fore, z_back = z_tables()
    y_fore, y_back, y_lanes, y_lanes_back, y_twiddle = y_tables()
    x_fore, x_extra, x_back, x_lanes, x_lanes_back, x_twiddle, marks, flips = x_tables()
    flags = jnp.stack([row == 0, col == 0]).astype(jnp.int32)
    units, damping = wave_tables(marks, row, col)

    owner = owner_column.reshape(32)
    spread_outs = (codes_of(32, 5), jax.ShapeDtypeStruct((32,), jnp.int32), [3, 1, 8, 256], [3, 1, 8, 256], [3, 16, 1, 256])
    pushes, slots, x_first, x_last, y_last = call(
        spread_kernel, [HBM] * 6 + [VMEM], spread_outs,
        [pltpu.SMEM((32,), jnp.int32), pltpu.SMEM((32,), jnp.int32), pltpu.VMEM((1, 32), BF16),
         pltpu.VMEM((1, 32), BF16), pltpu.VMEM((3, 32, 128), BF16), pltpu.VMEM((32, 3, 8, 128), BF16),
         pltpu.SMEM((32,), jnp.int32), pltpu.VMEM((32, 24, 128), F32), pltpu.VMEM((96, 128), F32),
         pltpu.VMEM((32, 5, 8, 128), F32), pltpu.SemaphoreType.DMA((6,))], [VMEM, SMEM, VMEM, VMEM, VMEM],
    )(owner, brick_index, stiffness.reshape(1, 32), rest_sq.reshape(1, 32), positions.transpose(1, 0, 2), weights,
      velocity)
    y_low = shifted(y_last, "col", 1)
    x_low = shifted(x_last, "row", 1)
    x_high = shifted(x_first, "row", -1)
    pushes = moved(pushes, "col")
    ids = pushes[:, 4, 0, 73:76].astype(jnp.int32)

    spectrum, turned = call(advect_kernel, [VMEM] * 5, ([256, 512], [3, 32, 8, 128]))(
        z_fore, velocity, x_low, x_high, y_low)
    spectrum = call(gather_kernel, [SMEM, VMEM, VMEM, VMEM], codes_of(32, 5),
                    [pltpu.VMEM((32, 8, 128), F32)] * 3)(ids, z_fore, pushes, spectrum)
    spectrum = moved(spectrum, "col")
    spectrum = call(y_kernel, [VMEM] * 4, codes_of(16, 7))(y_fore, y_lanes, y_twiddle, spectrum)
    spectrum = moved(spectrum, "row")
    spectrum = call(x_kernel, [SMEM] + [VMEM] * 10, codes_of(16, 7))(
        flags, x_fore, x_extra, x_back, x_lanes, x_lanes_back, x_twiddle, flips, units, damping, spectrum)
    spectrum = moved(spectrum, "row")
    replies = call(reply_kernel, [SMEM, VMEM], codes_of(32, 5))(ids, turned)
    spectrum = call(y_back_kernel, [VMEM] * 5, codes_of(32, 8))(
        y_back, y_lanes_back, y_twiddle, spectrum, replies)
    spectrum = moved(spectrum, "col")
    new_velocity, marker_velocity = call(
        last_kernel, [SMEM, SMEM, VMEM, VMEM, VMEM], ([3, 16, 8, 256], [3, 32, 128]))(
        owner, slots, z_back, spectrum, weights)
    return new_velocity, marker_velocity.transpose(1, 0, 2)


def solution(mesh):
    both = ("row", "col")
    placed = (
        P(None, "row", "col", None),
        P(both, None, None),
        P(both, None, None, None),
        P(both),
        P(both),
        P(both, None),
        P(both),
    )
    return jax.shard_map(
        local,
        mesh=mesh,
        in_specs=placed,
        out_specs=(P(None, "row", "col", None), P(both, None, None)),
        check_vma=False,
    )
```

```python
import jax
import jax.numpy as jnp
import numpy as np
from jax import lax
from jax.experimental import pallas as pl
from jax.experimental.pallas import tpu as pltpu
from jax.sharding import PartitionSpec as P


DT_STEP = 0.5
VISCOSITY = 0.1
N = 256
FIRST = np.array([k for r in range(16) for k in ((0, 16) if r == 0 else (r, 32 - r))])
F32 = jnp.float32
BF16 = jnp.bfloat16
TURN = 2.0 * np.pi


def split_table(table):
    table = np.asarray(table, np.float32)
    high = table.astype(BF16)
    low = (table - high.astype(np.float32)).astype(BF16)
    return np.stack([high, low])


def rotation(angle):
    rows, cols = angle.shape
    out = np.zeros((rows, 2, 4, cols, 2, 4))
    for j in range(4):
        out[:, 0, j, :, 0, j] = np.cos(angle)
        out[:, 0, j, :, 1, j] = np.sin(angle)
        out[:, 1, j, :, 0, j] = -np.sin(angle)
        out[:, 1, j, :, 1, j] = np.cos(angle)
    return out.reshape(rows * 8, cols * 8)


def z_tables():
    z = np.arange(N)
    fore = np.zeros((32, 2, 4, N))
    back = np.zeros((32, 2, 4, N))
    for k in range(128):
        angle = TURN / N * (k * z % N)
        twice = 2.0 if k else 1.0
        sine = np.sin(angle) if k else -np.cos(np.pi * z)
        fore[k // 4, 0, k % 4] = np.cos(angle)
        fore[k // 4, 1, k % 4] = -sine
        back[k // 4, 0, k % 4] = twice * np.cos(angle) / N
        back[k // 4, 1, k % 4] = -twice * sine / N
    return split_table(fore.reshape(N, N)), split_table(back.reshape(N, N))


def y_tables():
    angle = TURN / 32 * np.outer(FIRST, np.arange(32))
    fore = split_table(rotation(angle))
    back = split_table(rotation(-angle.T) / N)
    small = TURN / 8 * np.outer(np.arange(8), np.arange(8))
    cosine, sine = (np.kron(np.eye(16), f(small)) for f in (np.cos, np.sin))
    lanes_fore = split_table(np.concatenate([cosine, sine], 1))
    lanes_back = split_table(np.concatenate([cosine, -sine], 1))
    phase = TURN / N * np.outer(FIRST, np.tile(np.arange(8), 16))
    twiddle = np.stack([np.cos(phase), np.sin(phase)]).astype(np.float32)[:, :, None, :]
    return fore, back, lanes_fore, lanes_back, twiddle


def x_tables():
    angle = TURN / 16 * np.outer(np.arange(16), np.arange(16))
    pair = np.eye(2)

    def both(turn):
        grid = np.zeros((16, 2, 8, 16, 2, 8))
        base = rotation(turn).reshape(16, 8, 16, 8)
        for p in range(2):
            grid[:, p, :, :, p, :] = base
        return grid

    main = both(angle).reshape(256, 256)
    extra = both(angle).reshape(8, 2, 2, 2, 4, 16, 2, 2, 4)[:, :, :, :, 0]
    extra = extra.transpose(0, 3, 1, 2, 4, 5, 6, 7).copy()
    extra[..., 1:] = 0.0
    extra = extra.reshape(64, 256)
    back_main = both(-angle).reshape(256, 256) / N
    back_extra = both(-angle).reshape(16, 2, 2, 4, 8, 2, 2, 2, 4)[..., 0]
    back_extra = back_extra.transpose(0, 1, 2, 3, 4, 7, 5, 6).copy()
    back_extra[:, :, :, 1:] = 0.0
    back_extra = back_extra.reshape(256, 64) / N
    back = np.concatenate([back_main, back_extra], 1)
    cosine, sine = (np.kron(f(angle), np.eye(8)) for f in (np.cos, np.sin))
    lanes_fore = split_table(np.concatenate([cosine, sine], 1))
    lanes_back = split_table(np.concatenate([cosine, -sine], 1))
    phase = TURN / N * np.outer(np.arange(16), np.repeat(np.arange(16), 8))
    wide = np.zeros((2, 320, 128), np.float32)
    k_main = np.repeat(np.arange(16), 16)
    k_extra = (2 * np.arange(8)[:, None, None, None] + np.arange(2)[None, None, :, None]
               + np.zeros((8, 2, 2, 2), int)).reshape(64)
    p_main = np.tile(np.repeat(np.arange(2), 8), 16)
    p_extra = np.tile(np.arange(2), 32)
    j_main = np.tile(np.arange(4), 64)
    first = np.concatenate([k_main, k_extra])
    wide[0] = np.cos(phase)[first]
    wide[1] = np.sin(phase)[first]
    marks = (first, np.concatenate([p_main, p_extra]), np.concatenate([j_main, np.full(64, -1)]))
    reverse = np.kron(np.eye(16), np.eye(8)[(7 - np.arange(8))])
    negate = np.kron(np.eye(16), np.eye(8)[(-np.arange(8)) % 8])
    flips = np.concatenate([reverse, negate], 1).astype(BF16)
    return (split_table(main), split_table(extra), split_table(back), lanes_fore, lanes_back,
            wide.reshape(2, 40, 8, 128), marks, flips)


def dot(a, b, dims=((1,), (0,))):
    return lax.dot_general(a, b, (dims, ((), ())), preferred_element_type=F32)


def halves(x):
    high = x.astype(BF16)
    return high, (x - high.astype(F32)).astype(BF16)


def table_left(table, x, dims=((1,), (0,))):
    high, low = halves(x)
    return dot(table[0], high, dims) + dot(table[0], low, dims) + dot(table[1], high, dims)


def table_right(x, table, dims=((1,), (0,))):
    high, low = halves(x)
    return dot(high, table[0], dims) + dot(low, table[0], dims) + dot(high, table[1], dims)


def signs(shape):
    at = lax.broadcasted_iota(jnp.int32, shape, len(shape) - 2)
    return jnp.where(at % 8 < 4, 1.0, -1.0).astype(F32)


def swapped(x):
    return pltpu.roll(x, 4, 1) * signs((1, 8, 128))


def lane_pass(x, table):
    high, low = halves(x)
    twice = jnp.concatenate([table[0], table[0]], 0)
    both = dot(jnp.concatenate([high, low], 1), twice) + dot(high, table[1])
    rows = x.shape[0]
    cosine = both[:, :128].reshape(rows // 8, 8, 128)
    sine = both[:, 128:].reshape(rows // 8, 8, 128)
    return cosine + swapped(sine)


def stacked(x):
    return jnp.concatenate([x[:, 128 * c:128 * c + 128] for c in range(3)], 0)


def unstacked(x):
    rows = x.shape[0] // 3
    return jnp.concatenate([x[rows * c:rows * c + rows] for c in range(3)], 1)


def twiddled(x, cosine, sine):
    groups = cosine.shape[0]
    turned = swapped(x)
    parts = [x[groups * c:groups * c + groups] * cosine + turned[groups * c:groups * c + groups] * sine
             for c in range(3)]
    return jnp.concatenate(parts, 0)


def tile_place(slot, c):
    at = 3 * slot + c
    return at >> 1, at & 1


def lane_half(shape=(8, 128)):
    return lax.broadcasted_iota(jnp.int32, shape, len(shape) - 1) // 64


def to_exponent(largest):
    return jnp.ceil(16.0 * jnp.log(jnp.maximum(largest, 1e-36)))


def steps_per_unit(exponent):
    return 32767.0 * jnp.exp(exponent * (-1.0 / 16.0))


def step(exponent):
    return jnp.exp(exponent * (1.0 / 16.0)) * (1.0 / 32767.0)


def narrow(codes):
    return codes.astype(jnp.int32).astype(jnp.int16)


def wide(codes):
    return codes.astype(jnp.int32).astype(F32)


def row_largest(x):
    return jnp.max(jnp.abs(x), axis=-1, keepdims=True)


def encoded(x):
    largest = jnp.max(jnp.abs(x), axis=0)
    largest = jnp.broadcast_to(jnp.max(largest, axis=-1, keepdims=True), largest.shape)
    exponent = to_exponent(largest)
    return jnp.round(x * steps_per_unit(exponent)[None]), exponent


def put_pairs(out, spectrum):
    codes, exponent = encoded(spectrum)
    codes = narrow(codes).reshape(3, 16, 2, 8, 128)
    exponent = exponent.reshape(16, 2, 8, 128)
    for p in range(2):
        for c in range(3):
            out[:, 3 * p + c] = codes[c, :, p]
    half = lane_half((1, 8, 128))
    out[:, 6] = narrow(jnp.where(half == 0, exponent[:, 0], exponent[:, 1]))


def take_pairs(values):
    half = lane_half((1, 8, 128))
    steps = step(wide(values[:, 6]))
    turned = pltpu.roll(steps, 64, 2)
    steps = (jnp.where(half == 0, steps, turned), jnp.where(half == 0, turned, steps))
    parts = []
    for c in range(3):
        pair = [wide(values[:, 3 * p + c]) * steps[p] for p in range(2)]
        parts.append(jnp.stack(pair, 1).reshape(256, 128))
    return jnp.concatenate(parts, 0)


def to_column(row):
    size = row.shape[1]
    same = (lax.broadcasted_iota(jnp.int32, (size, size), 0)
            == lax.broadcasted_iota(jnp.int32, (size, size), 1))
    return jnp.sum(jnp.where(same, row, 0.0), axis=1, keepdims=True)


def spread_kernel(owner_in, brick_in, stiffness_in, rest_in, positions_in, weights_in, out, slots, owner, brick, stiffness, rest_sq, positions, weights, count, cubes, marks, total, arrived):
    pairs = ((weights_in, weights), (positions_in, positions), (rest_in, rest_sq),
             (stiffness_in, stiffness), (owner_in, owner), (brick_in, brick))
    copies = [pltpu.make_async_copy(a, b, arrived.at[i]) for i, (a, b) in enumerate(pairs)]
    for copy in copies:
        copy.start()
    total[...] = jnp.zeros(total.shape, F32)
    for d in range(32):
        count[d] = 0
    for copy in copies:
        copy.wait()
    place = [positions[c].astype(F32) for c in range(3)]
    segment = [pltpu.roll(p, 127, 1) - p for p in place]
    stretch = (segment[0] * segment[0] + segment[1] * segment[1] + segment[2] * segment[2])
    stretch = stretch / to_column(rest_sq[...].astype(F32))
    pull = 0.5 * to_column(stiffness[...].astype(F32)) * (stretch - 1.0)
    force = []
    for c in range(3):
        tension = pull * segment[c]
        force.append(tension - pltpu.roll(tension, 1, 1))
    largest = []
    for n in range(32):
        w0, w1, w2 = (weights[n, a].astype(F32) for a in range(3))
        cells = (w0[:, None, :] * w1[None, :, :]).reshape(64, 128)
        cells = jnp.concatenate([cells, cells], 0)
        pushed = jnp.concatenate([force[c][n:n + 1] * w2 for c in range(3)], 0)
        cells_high, cells_low = halves(cells)
        pushed_high, pushed_low = halves(pushed)
        both = ((1,), (1,))
        cube = dot(jnp.concatenate([pushed_high, pushed_low], 1), jnp.concatenate([cells_high, cells_high], 1), both)
        cube = cube + dot(pushed_high, cells_low, both)
        cubes[n] = cube
        largest += [jnp.max(jnp.abs(cube[8 * c:8 * c + 8]), axis=0, keepdims=True) for c in range(3)]
    largest = jnp.concatenate(largest, 0)
    exponent = to_exponent(jnp.broadcast_to(row_largest(largest), (96, 128)))
    marks[...] = exponent
    steps = steps_per_unit(exponent)
    for n in range(32):
        for c in range(3):
            cubes[n, 8 * c:8 * c + 8] = jnp.round(cubes[n, 8 * c:8 * c + 8] * steps[3 * n + c:3 * n + c + 1])
    half = lane_half()
    lane = lax.broadcasted_iota(jnp.int32, (8, 128), 1)

    @pl.loop(0, 32)
    def _(n):
        d = owner[n]
        s = count[d]
        count[d] = s + 1
        slots[n] = s
        last = jnp.where(lane == 73 + s, brick[n].astype(F32), 0.0)
        for c in range(3):
            tile, side = tile_place(s, c)
            total[d, tile] += jnp.where(half == side, cubes[n, 8 * c:8 * c + 8, :], 0.0)
            last = jnp.where(lane == 64 + 3 * s + c, marks[pl.ds(3 * n + c, 1), :], last)
        total[d, 4] += last

    out[...] = narrow(total[...])


def planes_kernel(_, velocity, x_first, x_last, y_last):
    for c in range(3):
        x_first[c] = velocity[c, 0:1]
        x_last[c] = velocity[c, 15:16]
        y_last[c] = velocity[c, :, 7:8, :]


def add_up_kernel(ids, pushes, field0, field1, field2, other0, other1, other2):
    sums = ((field0, field1, field2), (other0, other1, other2))
    for group in sums:
        for field in group:
            field[...] = jnp.zeros(field.shape, F32)
    half = lane_half()

    @pl.loop(0, 16, unroll=2)
    def _(pair):
        for odd in range(2):
            src = 2 * pair + odd
            tiles = [wide(pushes[src, t]) for t in range(5)]
            turned = [pltpu.roll(tile, 64, 1) for tile in tiles]
            steps = step(tiles[4])
            for slot in range(3):
                brick = ids[src, slot]
                x_half, z_block = brick >> 5, brick & 31
                for c in range(3):
                    at = 3 * slot + c
                    tile, side = tile_place(slot, c)
                    codes = jnp.where(half == side, tiles[tile], turned[tile])
                    cube = codes * jnp.broadcast_to(steps[:, 64 + at:65 + at], (8, 128))
                    sums[odd][c][z_block] += jnp.where(half == x_half, cube, 0.0)

    for c in range(3):
        sums[0][c][...] = sums[0][c][...] + sums[1][c][...]


def star_kernel(table, velocity, x_low, x_high, y_low, field0, field1, field2, out, turned):
    u = [velocity[c].reshape(128, 256) for c in range(3)]
    sub = lax.broadcasted_iota(jnp.int32, (16, 8, 256), 1)
    rows = []
    beyond = jnp.zeros((16, 8, 256), F32)
    for c in range(3):
        v = velocity[c]
        beyond = jnp.where(sub == c, v[:, 0:1, :], beyond)
        turned[c] = jnp.transpose(u[c]).reshape(32, 8, 128)
        ahead = jnp.concatenate([v[1:], x_high[c]], 0)
        behind = jnp.concatenate([x_low[c], v[:-1]], 0)
        total = u[0] * (ahead - behind).reshape(128, 256)
        ahead = jnp.where(sub == 7, 0.0, pltpu.roll(v, 7, 1))
        behind = jnp.where(sub == 0, y_low[c], pltpu.roll(v, 1, 1))
        total = total + u[1] * (ahead - behind).reshape(128, 256)
        total = total + u[2] * (pltpu.roll(u[c], 255, 1) - pltpu.roll(u[c], 1, 1))
        rows.append(u[c] - (0.5 * DT_STEP) * total)
    beyond = (-0.5 * DT_STEP) * y_low[1] * beyond
    star = jnp.concatenate(rows + [beyond.reshape(128, 256)], 0)
    spectrum = table_left(table, star, ((1,), (1,)))
    field = jnp.concatenate([field[...].reshape(256, 128) for field in (field0, field1, field2)], 1)
    total = spectrum[:, :384] + table_left(table, DT_STEP * field)
    total = jnp.concatenate([stacked(total), spectrum[:, 384:]], 0)
    codes, exponent = encoded(total.reshape(4, 32, 8, 128))
    for t in range(4):
        out[:, t] = narrow(codes[t])
    out[:, 4] = narrow(exponent)


def reply_kernel(ids, turned, weights, out, cells_high, cells_low):
    for n in range(32):
        w0, w1 = (weights[n, a].astype(F32) for a in range(2))
        cells_high[n], cells_low[n] = halves((w0[:, None, :] * w1[None, :, :]).reshape(64, 128))
    half = lane_half()
    lane = lax.broadcasted_iota(jnp.int32, (8, 128), 1)

    @pl.loop(0, 32, unroll=4)
    def _(src):
        cubes, largest = [], []
        for slot in range(3):
            brick = ids[src, slot]
            x_half, z_block = brick >> 5, brick & 31
            for c in range(3):
                tile = turned[c, z_block]
                cube = jnp.where(half == x_half, tile, pltpu.roll(tile, 64, 1))
                largest.append(jnp.max(jnp.abs(cube), axis=0, keepdims=True))
                cubes.append(cube)
        largest = jnp.concatenate(largest + largest[:7], 0)
        exponent = to_exponent(jnp.broadcast_to(row_largest(largest), (16, 128)))
        steps = steps_per_unit(exponent)
        codes = [jnp.round(cube * steps[at:at + 1]) for at, cube in enumerate(cubes)]
        last = jnp.zeros((8, 128), F32)
        for at in range(9):
            last = jnp.where(lane == 64 + at, exponent[at:at + 1], last)
        codes.append(last)
        for t in range(5):
            out[src, t] = narrow(jnp.where(half == 0, codes[2 * t], codes[2 * t + 1]))


def interpolate(owner, slots, replies, weights, cells_high, cells_low, out):
    half = lane_half()
    lane = lax.broadcasted_iota(jnp.int32, (8, 128), 1)
    for n in range(32):
        d, s = owner[n], slots[n]
        steps = step(wide(replies[d, 7]))
        parts = []
        for c in range(3):
            tile, side = tile_place(s, c)
            cube = wide(replies[d, 3 + tile])
            cube = jnp.where(half == side, cube, pltpu.roll(cube, 64, 1))
            own = jnp.sum(jnp.where(lane == 64 + 3 * s + c, steps, 0.0), axis=1, keepdims=True)
            parts.append(cube * own)
        cube_high, cube_low = halves(jnp.concatenate(parts, 0)[:, :64])
        w2 = weights[n, 2].astype(F32)
        high = cells_high[n]
        partial = dot(cube_high, high) + dot(cube_low, high) + dot(cube_high, cells_low[n])
        for c in range(3):
            out[c, n:n + 1] = jnp.sum(partial[8 * c:8 * c + 8] * w2, axis=0, keepdims=True)


def y_kernel(left, lanes, twiddle, values, out):
    steps = step(wide(values[:, 4]))
    beyond = wide(values[:, 3]) * steps
    beyond = jnp.concatenate([beyond[1:], beyond[:1]], 0)
    last = lax.broadcasted_iota(jnp.int32, (1, 8, 128), 2) % 8 == 7
    spectrum = []
    for c in range(3):
        part = wide(values[:, c]) * steps + jnp.where(last, pltpu.roll(beyond, 7 - c, 2), 0.0)
        spectrum.append(part.reshape(256, 128))
    spectrum = table_left(left, jnp.concatenate(spectrum, 1))
    spectrum = stacked(spectrum).reshape(96, 8, 128)
    spectrum = twiddled(spectrum, twiddle[0], twiddle[1])
    spectrum = lane_pass(spectrum.reshape(768, 128), lanes)
    put_pairs(out, spectrum.reshape(3, 32, 8, 128))


def x_kernel(flags, left, left_extra, back, lanes, lanes_back, twiddle, flips, waves, damping, values, out):
    packed = take_pairs(values)
    high, low = halves(packed)
    flipped = dot(jnp.concatenate([high, low], 1), jnp.concatenate([flips[...], flips[...]], 0))
    by_pair = (3, 16, 2, 8, 128)
    reverse = flipped[:, :128].reshape(by_pair)
    negate = flipped[:, 128:].reshape(by_pair)
    packed = packed.reshape(by_pair)
    own = flags[0] == 1
    first = jnp.where(own, negate[:, :, 0:1], reverse[:, :, 1:2])
    second = jnp.where(own, reverse[:, :, 1:2], reverse[:, :, 0:1])
    mirrored = jnp.concatenate([first, second], 2) * signs((1, 1, 1, 8, 128))
    sub = lax.broadcasted_iota(jnp.int32, (1, 1, 1, 8, 128), 3)
    lowest = (sub % 4 == 0) & (flags[1] == 1)
    main = jnp.where(lowest, 0.5 * (packed + mirrored), packed)
    extra = jnp.where(lowest, 0.5 * (packed - mirrored), 0.0)
    main = table_left(left, unstacked(main.reshape(768, 128)))
    extra = table_left(left_extra, unstacked(extra.reshape(768, 128)))
    spectrum = stacked(jnp.concatenate([main, extra], 0)).reshape(120, 8, 128)
    spectrum = twiddled(spectrum, twiddle[0], twiddle[1])
    spectrum = lane_pass(spectrum.reshape(960, 128), lanes).reshape(3, 320, 128)
    normal = waves[0] * spectrum[0] + waves[1] * spectrum[1] + waves[2] * spectrum[2]
    damp = damping[...]
    projected = jnp.concatenate([(spectrum[c] - waves[c] * normal) * damp for c in range(3)], 0)
    projected = lane_pass(projected, lanes_back)
    projected = twiddled(projected, twiddle[0], -twiddle[1])
    projected = unstacked(projected.reshape(960, 128))
    put_pairs(out, stacked(table_left(back, projected)).reshape(3, 32, 8, 128))


def y_back_kernel(back, lanes, twiddle, values, replies, out):
    spectrum = lane_pass(take_pairs(values), lanes)
    spectrum = twiddled(spectrum, twiddle[0], -twiddle[1])
    spectrum = table_left(back, unstacked(spectrum.reshape(768, 128)))
    codes, exponent = encoded(stacked(spectrum).reshape(3, 32, 8, 128))
    for c in range(3):
        out[:, c] = narrow(codes[c])
    for t in range(4):
        out[:, 3 + t] = replies[:, t]
    lane = lax.broadcasted_iota(jnp.int32, (1, 8, 128), 2)
    out[:, 7] = narrow(jnp.where(lane == 76, exponent, wide(replies[:, 4])))


def last_kernel(owner, slots, back, values, weights, cells_high, cells_low, out, markers):
    interpolate(owner, slots, values, weights, cells_high, cells_low, markers)
    steps = step(wide(values[:, 7])[:, :, 76:77])
    spectrum = [(wide(values[:, c]) * steps).reshape(256, 128) for c in range(3)]
    field = table_right(jnp.transpose(jnp.concatenate(spectrum, 1)), back)
    out[...] = field.reshape(3, 16, 8, 256)


VMEM = pl.BlockSpec(memory_space=pltpu.VMEM)
SMEM = pl.BlockSpec(memory_space=pltpu.SMEM)
HBM = pl.BlockSpec(memory_space=pltpu.HBM)


def call(kernel, specs, shapes, scratch=(), out_specs=None):
    single = not isinstance(shapes, tuple)
    structs = [jax.ShapeDtypeStruct(s, F32) if isinstance(s, list) else s
               for s in ((shapes,) if single else shapes)]
    outs = out_specs or [VMEM] * len(structs)
    return pl.pallas_call(
        kernel,
        out_shape=structs[0] if single else structs,
        in_specs=specs,
        out_specs=outs[0] if single else outs,
        scratch_shapes=list(scratch),
        compiler_params=pltpu.CompilerParams(vmem_limit_bytes=48 << 20),
    )


def codes_of(count, tiles):
    return jax.ShapeDtypeStruct((count, tiles, 8, 128), jnp.int16)


def signed(indices):
    return jnp.where(indices <= (N - 1) // 2, indices, indices - N)


def wave_tables(marks, row, col):
    first, pair, slot = (m[:, None] for m in marks)
    lane = jnp.arange(128, dtype=jnp.int32)[None, :]
    second = jnp.where(row == 0, 16, 32 - row)
    index_x = first + 16 * (lane // 8)
    index_y = jnp.where(pair == 0, row, second) + 32 * (lane % 8)
    index_z = jnp.where(slot < 0, N // 2, 4 * col + slot) + 0 * lane
    scale = 2.0 * jnp.pi / N
    full_sq, waves = 0.0, []
    for index in (index_x, index_y, index_z):
        full = scale * signed(index).astype(F32)
        full_sq = full_sq + full * full
        waves.append(jnp.where(2 * index == N, 0.0, full))
    wave_sq = waves[0] * waves[0] + waves[1] * waves[1] + waves[2] * waves[2]
    still = wave_sq == 0.0
    inverse = jnp.where(still, 0.0, lax.rsqrt(jnp.where(still, 1.0, wave_sq)))
    units = jnp.stack([w * inverse for w in waves])
    return units, 1.0 / (1.0 + DT_STEP * VISCOSITY * full_sq)


def moved(x, axis):
    return lax.all_to_all(x, axis, split_axis=0, concat_axis=0, tiled=True)


def shifted(plane, axis, by):
    count = lax.axis_size(axis)
    return lax.ppermute(plane, axis, [(i, (i + by) % count) for i in range(count)])


def local(velocity, positions, weights, stiffness, rest_sq, owner_column, brick_index):
    row, col = lax.axis_index("row"), lax.axis_index("col")
    z_fore, z_back = z_tables()
    y_fore, y_back, y_lanes, y_lanes_back, y_twiddle = y_tables()
    x_fore, x_extra, x_back, x_lanes, x_lanes_back, x_twiddle, marks, flips = x_tables()
    flags = jnp.stack([row == 0, col == 0]).astype(jnp.int32)

    owner = owner_column.reshape(32)
    spread_outs = (codes_of(32, 5), jax.ShapeDtypeStruct((32,), jnp.int32))
    pushes, slots = call(
        spread_kernel, [HBM] * 6, spread_outs,
        [pltpu.SMEM((32,), jnp.int32), pltpu.SMEM((32,), jnp.int32), pltpu.VMEM((1, 32), BF16),
         pltpu.VMEM((1, 32), BF16), pltpu.VMEM((3, 32, 128), BF16), pltpu.VMEM((32, 3, 8, 128), BF16),
         pltpu.SMEM((32,), jnp.int32), pltpu.VMEM((32, 24, 128), F32), pltpu.VMEM((96, 128), F32),
         pltpu.VMEM((32, 5, 8, 128), F32), pltpu.SemaphoreType.DMA((6,))], [VMEM, SMEM],
    )(owner, brick_index, stiffness.reshape(1, 32), rest_sq.reshape(1, 32), positions.transpose(1, 0, 2), weights)
    x_first, x_last, y_last = call(
        planes_kernel, [SMEM, VMEM], ([3, 1, 8, 256], [3, 1, 8, 256], [3, 16, 1, 256]))(slots, velocity)
    y_low = shifted(y_last, "col", 1)
    x_low = shifted(x_last, "row", 1)
    x_high = shifted(x_first, "row", -1)
    pushes = moved(pushes, "col")
    ids = pushes[:, 4, 0, 73:76].astype(jnp.int32)

    field = call(add_up_kernel, [SMEM, VMEM], ([32, 8, 128],) * 3, [pltpu.VMEM((32, 8, 128), F32)] * 3)(ids, pushes)
    spectrum, turned = call(star_kernel, [VMEM] * 8, (codes_of(32, 5), [3, 32, 8, 128]))(
        z_fore, velocity, x_low, x_high, y_low, *field)
    spectrum = moved(spectrum, "col")
    spectrum = call(y_kernel, [VMEM] * 4, codes_of(16, 7))(y_fore, y_lanes, y_twiddle, spectrum)
    marks = [jnp.asarray(m, jnp.int32) for m in marks]
    spectrum, marks = lax.optimization_barrier((spectrum, marks))
    spectrum = moved(spectrum, "row")
    units, damping = wave_tables(marks, row, col)
    spectrum = call(x_kernel, [SMEM] + [VMEM] * 10, codes_of(16, 7))(
        flags, x_fore, x_extra, x_back, x_lanes, x_lanes_back, x_twiddle, flips, units, damping, spectrum)
    spectrum = moved(spectrum, "row")
    cells = jax.ShapeDtypeStruct((32, 64, 128), BF16)
    replies, cells_high, cells_low = call(reply_kernel, [SMEM, VMEM, VMEM], (codes_of(32, 5), cells, cells))(
        ids, turned, weights)
    spectrum = call(y_back_kernel, [VMEM] * 5, codes_of(32, 8))(
        y_back, y_lanes_back, y_twiddle, spectrum, replies)
    spectrum = moved(spectrum, "col")
    new_velocity, marker_velocity = call(
        last_kernel, [SMEM, SMEM] + [VMEM] * 5, ([3, 16, 8, 256], [3, 32, 128]))(
        owner, slots, z_back, spectrum, weights, cells_high, cells_low)
    return new_velocity, marker_velocity.transpose(1, 0, 2)


def solution(mesh):
    both = ("row", "col")
    placed = (
        P(None, "row", "col", None),
        P(both, None, None),
        P(both, None, None, None),
        P(both),
        P(both),
        P(both, None),
        P(both),
    )
    return jax.shard_map(
        local,
        mesh=mesh,
        in_specs=placed,
        out_specs=(P(None, "row", "col", None), P(both, None, None)),
        check_vma=False,
    )
```

```python
import jax
import jax.numpy as jnp
import numpy as np
from jax import lax
from jax.experimental import pallas as pl
from jax.experimental.pallas import tpu as pltpu
from jax.sharding import PartitionSpec as P


DT_STEP = 0.5
VISCOSITY = 0.1
N = 256
FIRST = np.array([k for r in range(16) for k in ((0, 16) if r == 0 else (r, 32 - r))])
F32 = jnp.float32
BF16 = jnp.bfloat16
TURN = 2.0 * np.pi


def split_table(table):
    table = np.asarray(table, np.float32)
    high = table.astype(BF16)
    low = (table - high.astype(np.float32)).astype(BF16)
    return np.stack([high, low])


def rotation(angle):
    rows, cols = angle.shape
    out = np.zeros((rows, 2, 4, cols, 2, 4))
    for j in range(4):
        out[:, 0, j, :, 0, j] = np.cos(angle)
        out[:, 0, j, :, 1, j] = np.sin(angle)
        out[:, 1, j, :, 0, j] = -np.sin(angle)
        out[:, 1, j, :, 1, j] = np.cos(angle)
    return out.reshape(rows * 8, cols * 8)


def z_tables():
    z = np.arange(N)
    fore = np.zeros((32, 2, 4, N))
    back = np.zeros((32, 2, 4, N))
    for k in range(128):
        angle = TURN / N * (k * z % N)
        twice = 2.0 if k else 1.0
        sine = np.sin(angle) if k else -np.cos(np.pi * z)
        fore[k // 4, 0, k % 4] = np.cos(angle)
        fore[k // 4, 1, k % 4] = -sine
        back[k // 4, 0, k % 4] = twice * np.cos(angle) / N
        back[k // 4, 1, k % 4] = -twice * sine / N
    return split_table(fore.reshape(N, N)), split_table(back.reshape(N, N))


def y_tables():
    angle = TURN / 32 * np.outer(FIRST, np.arange(32))
    fore = split_table(rotation(angle))
    back = split_table(rotation(-angle.T) / N)
    small = TURN / 8 * np.outer(np.arange(8), np.arange(8))
    cosine, sine = (np.kron(np.eye(16), f(small)) for f in (np.cos, np.sin))
    lanes_fore = split_table(np.concatenate([cosine, sine], 1))
    lanes_back = split_table(np.concatenate([cosine, -sine], 1))
    phase = TURN / N * np.outer(FIRST, np.tile(np.arange(8), 16))
    twiddle = np.stack([np.cos(phase), np.sin(phase)]).astype(np.float32)[:, :, None, :]
    return fore, back, lanes_fore, lanes_back, twiddle


def x_tables():
    angle = TURN / 16 * np.outer(np.arange(16), np.arange(16))
    pair = np.eye(2)

    def both(turn):
        grid = np.zeros((16, 2, 8, 16, 2, 8))
        base = rotation(turn).reshape(16, 8, 16, 8)
        for p in range(2):
            grid[:, p, :, :, p, :] = base
        return grid

    main = both(angle).reshape(256, 256)
    extra = both(angle).reshape(8, 2, 2, 2, 4, 16, 2, 2, 4)[:, :, :, :, 0]
    extra = extra.transpose(0, 3, 1, 2, 4, 5, 6, 7).copy()
    extra[..., 1:] = 0.0
    extra = extra.reshape(64, 256)
    back_main = both(-angle).reshape(256, 256) / N
    back_extra = both(-angle).reshape(16, 2, 2, 4, 8, 2, 2, 2, 4)[..., 0]
    back_extra = back_extra.transpose(0, 1, 2, 3, 4, 7, 5, 6).copy()
    back_extra[:, :, :, 1:] = 0.0
    back_extra = back_extra.reshape(256, 64) / N
    back = np.concatenate([back_main, back_extra], 1)
    cosine, sine = (np.kron(f(angle), np.eye(8)) for f in (np.cos, np.sin))
    lanes_fore = split_table(np.concatenate([cosine, sine], 1))
    lanes_back = split_table(np.concatenate([cosine, -sine], 1))
    phase = TURN / N * np.outer(np.arange(16), np.repeat(np.arange(16), 8))
    wide = np.zeros((2, 320, 128), np.float32)
    k_main = np.repeat(np.arange(16), 16)
    k_extra = (2 * np.arange(8)[:, None, None, None] + np.arange(2)[None, None, :, None]
               + np.zeros((8, 2, 2, 2), int)).reshape(64)
    p_main = np.tile(np.repeat(np.arange(2), 8), 16)
    p_extra = np.tile(np.arange(2), 32)
    j_main = np.tile(np.arange(4), 64)
    first = np.concatenate([k_main, k_extra])
    wide[0] = np.cos(phase)[first]
    wide[1] = np.sin(phase)[first]
    marks = (first, np.concatenate([p_main, p_extra]), np.concatenate([j_main, np.full(64, -1)]))
    reverse = np.kron(np.eye(16), np.eye(8)[(7 - np.arange(8))])
    negate = np.kron(np.eye(16), np.eye(8)[(-np.arange(8)) % 8])
    flips = np.concatenate([reverse, negate], 1).astype(BF16)
    return (split_table(main), split_table(extra), split_table(back), lanes_fore, lanes_back,
            wide.reshape(2, 40, 8, 128), marks, flips)


def dot(a, b, dims=((1,), (0,))):
    return lax.dot_general(a, b, (dims, ((), ())), preferred_element_type=F32)


def halves(x):
    high = x.astype(BF16)
    return high, (x - high.astype(F32)).astype(BF16)


def table_left(table, x, dims=((1,), (0,))):
    high, low = halves(x)
    return dot(table[0], high, dims) + dot(table[0], low, dims) + dot(table[1], high, dims)


def table_right(x, table, dims=((1,), (0,))):
    high, low = halves(x)
    return dot(high, table[0], dims) + dot(low, table[0], dims) + dot(high, table[1], dims)


def signs(shape):
    at = lax.broadcasted_iota(jnp.int32, shape, len(shape) - 2)
    return jnp.where(at % 8 < 4, 1.0, -1.0).astype(F32)


def swapped(x):
    return pltpu.roll(x, 4, 1) * signs((1, 8, 128))


def lane_pass(x, table):
    high, low = halves(x)
    twice = jnp.concatenate([table[0], table[0]], 0)
    both = dot(jnp.concatenate([high, low], 1), twice) + dot(high, table[1])
    rows = x.shape[0]
    cosine = both[:, :128].reshape(rows // 8, 8, 128)
    sine = both[:, 128:].reshape(rows // 8, 8, 128)
    return cosine + swapped(sine)


def stacked(x):
    return jnp.concatenate([x[:, 128 * c:128 * c + 128] for c in range(3)], 0)


def unstacked(x):
    rows = x.shape[0] // 3
    return jnp.concatenate([x[rows * c:rows * c + rows] for c in range(3)], 1)


def twiddled(x, cosine, sine):
    groups = cosine.shape[0]
    turned = swapped(x)
    parts = [x[groups * c:groups * c + groups] * cosine + turned[groups * c:groups * c + groups] * sine
             for c in range(3)]
    return jnp.concatenate(parts, 0)


def tile_place(slot, c):
    at = 3 * slot + c
    return at >> 1, at & 1


def lane_half(shape=(8, 128)):
    return lax.broadcasted_iota(jnp.int32, shape, len(shape) - 1) // 64


def to_exponent(largest):
    return jnp.ceil(16.0 * jnp.log(jnp.maximum(largest, 1e-36)))


def steps_per_unit(exponent):
    return 32767.0 * jnp.exp(exponent * (-1.0 / 16.0))


def step(exponent):
    return jnp.exp(exponent * (1.0 / 16.0)) * (1.0 / 32767.0)


def narrow(codes):
    return codes.astype(jnp.int32).astype(jnp.int16)


def wide(codes):
    return codes.astype(jnp.int32).astype(F32)


def row_largest(x):
    return jnp.max(jnp.abs(x), axis=-1, keepdims=True)


def encoded(x):
    largest = jnp.max(jnp.abs(x), axis=0)
    largest = jnp.broadcast_to(jnp.max(largest, axis=-1, keepdims=True), largest.shape)
    exponent = to_exponent(largest)
    return jnp.round(x * steps_per_unit(exponent)[None]), exponent


def put_pairs(out, spectrum):
    codes, exponent = encoded(spectrum)
    codes = narrow(codes).reshape(3, 16, 2, 8, 128)
    exponent = exponent.reshape(16, 2, 8, 128)
    for p in range(2):
        for c in range(3):
            out[:, 3 * p + c] = codes[c, :, p]
    half = lane_half((1, 8, 128))
    out[:, 6] = narrow(jnp.where(half == 0, exponent[:, 0], exponent[:, 1]))


def take_pairs(values):
    half = lane_half((1, 8, 128))
    steps = step(wide(values[:, 6]))
    turned = pltpu.roll(steps, 64, 2)
    steps = (jnp.where(half == 0, steps, turned), jnp.where(half == 0, turned, steps))
    parts = []
    for c in range(3):
        pair = [wide(values[:, 3 * p + c]) * steps[p] for p in range(2)]
        parts.append(jnp.stack(pair, 1).reshape(256, 128))
    return jnp.concatenate(parts, 0)


def to_column(row):
    size = row.shape[1]
    same = (lax.broadcasted_iota(jnp.int32, (size, size), 0)
            == lax.broadcasted_iota(jnp.int32, (size, size), 1))
    return jnp.sum(jnp.where(same, row, 0.0), axis=1, keepdims=True)


def spread_kernel(owner_in, brick_in, stiffness_in, rest_in, positions_in, weights_in, out, slots, owner, brick, stiffness, rest_sq, positions, weights, count, cubes, marks, total, arrived):
    pairs = ((weights_in, weights), (positions_in, positions), (rest_in, rest_sq),
             (stiffness_in, stiffness), (owner_in, owner), (brick_in, brick))
    copies = [pltpu.make_async_copy(a, b, arrived.at[i]) for i, (a, b) in enumerate(pairs)]
    for copy in copies:
        copy.start()
    total[...] = jnp.zeros(total.shape, F32)
    for d in range(32):
        count[d] = 0
    for copy in copies:
        copy.wait()
    place = [positions[c].astype(F32) for c in range(3)]
    segment = [pltpu.roll(p, 127, 1) - p for p in place]
    stretch = (segment[0] * segment[0] + segment[1] * segment[1] + segment[2] * segment[2])
    stretch = stretch / to_column(rest_sq[...].astype(F32))
    pull = 0.5 * to_column(stiffness[...].astype(F32)) * (stretch - 1.0)
    force = []
    for c in range(3):
        tension = pull * segment[c]
        force.append(tension - pltpu.roll(tension, 1, 1))
    largest = []
    for n in range(32):
        w0, w1, w2 = (weights[n, a].astype(F32) for a in range(3))
        cells = (w0[:, None, :] * w1[None, :, :]).reshape(64, 128)
        cells = jnp.concatenate([cells, cells], 0)
        pushed = jnp.concatenate([force[c][n:n + 1] * w2 for c in range(3)], 0)
        cells_high, cells_low = halves(cells)
        pushed_high, pushed_low = halves(pushed)
        both = ((1,), (1,))
        cube = dot(jnp.concatenate([pushed_high, pushed_low], 1), jnp.concatenate([cells_high, cells_high], 1), both)
        cube = cube + dot(pushed_high, cells_low, both)
        cubes[n] = cube
        largest += [jnp.max(jnp.abs(cube[8 * c:8 * c + 8]), axis=0, keepdims=True) for c in range(3)]
    largest = jnp.concatenate(largest, 0)
    exponent = to_exponent(jnp.broadcast_to(row_largest(largest), (96, 128)))
    marks[...] = exponent
    steps = steps_per_unit(exponent)
    for n in range(32):
        for c in range(3):
            cubes[n, 8 * c:8 * c + 8] = jnp.round(cubes[n, 8 * c:8 * c + 8] * steps[3 * n + c:3 * n + c + 1])
    half = lane_half()
    lane = lax.broadcasted_iota(jnp.int32, (8, 128), 1)

    @pl.loop(0, 32, unroll=4)
    def _(n):
        d = owner[n]
        s = count[d]
        count[d] = s + 1
        slots[n] = s
        last = jnp.where(lane == 73 + s, brick[n].astype(F32), 0.0)
        for c in range(3):
            tile, side = tile_place(s, c)
            pltpu.store(total.at[d, tile], cubes[n, 8 * c:8 * c + 8, :], mask=half == side)
            last = jnp.where(lane == 64 + 3 * s + c, marks[pl.ds(3 * n + c, 1), :], last)
        own = (lane == 73 + s) | ((lane >= 64 + 3 * s) & (lane < 67 + 3 * s))
        pltpu.store(total.at[d, 4], last, mask=own)

    out[...] = narrow(total[...])


def planes_kernel(_, velocity, x_first, x_last, y_last):
    for c in range(3):
        x_first[c] = velocity[c, 0:1]
        x_last[c] = velocity[c, 15:16]
        y_last[c] = velocity[c, :, 7:8, :]


def add_up_kernel(ids, pushes, field0, field1, field2, other0, other1, other2):
    sums = ((field0, field1, field2), (other0, other1, other2))
    for group in sums:
        for field in group:
            field[...] = jnp.zeros(field.shape, F32)
    half = lane_half()

    @pl.loop(0, 16, unroll=4)
    def _(pair):
        for odd in range(2):
            src = 2 * pair + odd
            tiles = [wide(pushes[src, t]) for t in range(5)]
            turned = [pltpu.roll(tile, 64, 1) for tile in tiles]
            steps = step(tiles[4])
            for slot in range(3):
                brick = ids[src, slot]
                x_half, z_block = brick >> 5, brick & 31
                for c in range(3):
                    at = 3 * slot + c
                    tile, side = tile_place(slot, c)
                    codes = jnp.where(half == side, tiles[tile], turned[tile])
                    cube = codes * jnp.broadcast_to(steps[:, 64 + at:65 + at], (8, 128))
                    sums[odd][c][z_block] += jnp.where(half == x_half, cube, 0.0)

    for c in range(3):
        sums[0][c][...] = sums[0][c][...] + sums[1][c][...]


def star_kernel(table, velocity, x_low, x_high, y_low, field0, field1, field2, out, turned):
    u = [velocity[c].reshape(128, 256) for c in range(3)]
    sub = lax.broadcasted_iota(jnp.int32, (16, 8, 256), 1)
    rows = []
    beyond = jnp.zeros((16, 8, 256), F32)
    for c in range(3):
        v = velocity[c]
        beyond = jnp.where(sub == c, v[:, 0:1, :], beyond)
        turned[c] = jnp.transpose(u[c]).reshape(32, 8, 128)
        ahead = jnp.concatenate([v[1:], x_high[c]], 0)
        behind = jnp.concatenate([x_low[c], v[:-1]], 0)
        total = u[0] * (ahead - behind).reshape(128, 256)
        ahead = jnp.where(sub == 7, 0.0, pltpu.roll(v, 7, 1))
        behind = jnp.where(sub == 0, y_low[c], pltpu.roll(v, 1, 1))
        total = total + u[1] * (ahead - behind).reshape(128, 256)
        total = total + u[2] * (pltpu.roll(u[c], 255, 1) - pltpu.roll(u[c], 1, 1))
        rows.append(u[c] - (0.5 * DT_STEP) * total)
    beyond = (-0.5 * DT_STEP) * y_low[1] * beyond
    star = jnp.concatenate(rows + [beyond.reshape(128, 256)], 0)
    spectrum = table_left(table, star, ((1,), (1,)))
    field = jnp.concatenate([field[...].reshape(256, 128) for field in (field0, field1, field2)], 1)
    total = spectrum[:, :384] + table_left(table, DT_STEP * field)
    total = jnp.concatenate([stacked(total), spectrum[:, 384:]], 0)
    codes, exponent = encoded(total.reshape(4, 32, 8, 128))
    for t in range(3):
        out[:, t] = narrow(codes[t])
    lane = lax.broadcasted_iota(jnp.int32, (1, 8, 128), 2)
    out[:, 3] = narrow(jnp.where(lane == 3, exponent, codes[3]))


def reply_kernel(ids, turned, weights, out, cells_high, cells_low):
    for n in range(32):
        w0, w1 = (weights[n, a].astype(F32) for a in range(2))
        cells_high[n], cells_low[n] = halves((w0[:, None, :] * w1[None, :, :]).reshape(64, 128))
    half = lane_half()
    lane = lax.broadcasted_iota(jnp.int32, (8, 128), 1)

    @pl.loop(0, 32, unroll=4)
    def _(src):
        cubes, largest = [], []
        for slot in range(3):
            brick = ids[src, slot]
            x_half, z_block = brick >> 5, brick & 31
            for c in range(3):
                tile = turned[c, z_block]
                cube = jnp.where(half == x_half, tile, pltpu.roll(tile, 64, 1))
                largest.append(jnp.max(jnp.abs(cube), axis=0, keepdims=True))
                cubes.append(cube)
        largest = jnp.concatenate(largest + largest[:7], 0)
        exponent = to_exponent(jnp.broadcast_to(row_largest(largest), (16, 128)))
        steps = steps_per_unit(exponent)
        codes = [jnp.round(cube * steps[at:at + 1]) for at, cube in enumerate(cubes)]
        last = jnp.zeros((8, 128), F32)
        for at in range(9):
            last = jnp.where(lane == 64 + at, exponent[at:at + 1], last)
        codes.append(last)
        for t in range(5):
            out[src, t] = narrow(jnp.where(half == 0, codes[2 * t], codes[2 * t + 1]))


def interpolate(owner, slots, replies, weights, cells_high, cells_low, out):
    half = lane_half()
    lane = lax.broadcasted_iota(jnp.int32, (8, 128), 1)
    for n in range(32):
        d, s = owner[n], slots[n]
        steps = step(wide(replies[d, 7]))
        parts = []
        for c in range(3):
            tile, side = tile_place(s, c)
            cube = wide(replies[d, 3 + tile])
            cube = jnp.where(half == side, cube, pltpu.roll(cube, 64, 1))
            own = jnp.sum(jnp.where(lane == 64 + 3 * s + c, steps, 0.0), axis=1, keepdims=True)
            parts.append(cube * own)
        cube_high, cube_low = halves(jnp.concatenate(parts, 0)[:, :64])
        w2 = weights[n, 2].astype(F32)
        high = cells_high[n]
        partial = dot(cube_high, high) + dot(cube_low, high) + dot(cube_high, cells_low[n])
        for c in range(3):
            out[c, n:n + 1] = jnp.sum(partial[8 * c:8 * c + 8] * w2, axis=0, keepdims=True)


def y_kernel(left, lanes, twiddle, values, out):
    beyond = wide(values[:, 3])
    steps = jnp.broadcast_to(step(beyond[:, :, 3:4]), (32, 8, 128))
    beyond = beyond * steps
    beyond = jnp.concatenate([beyond[1:], beyond[:1]], 0)
    last = lax.broadcasted_iota(jnp.int32, (1, 8, 128), 2) % 8 == 7
    spectrum = []
    for c in range(3):
        part = wide(values[:, c]) * steps + jnp.where(last, pltpu.roll(beyond, 7 - c, 2), 0.0)
        spectrum.append(part.reshape(256, 128))
    spectrum = table_left(left, jnp.concatenate(spectrum, 1))
    spectrum = stacked(spectrum).reshape(96, 8, 128)
    spectrum = twiddled(spectrum, twiddle[0], twiddle[1])
    spectrum = lane_pass(spectrum.reshape(768, 128), lanes)
    put_pairs(out, spectrum.reshape(3, 32, 8, 128))


def x_kernel(flags, left, left_extra, back, lanes, lanes_back, twiddle, flips, waves, damping, values, out):
    packed = take_pairs(values)
    high, low = halves(packed)
    flipped = dot(jnp.concatenate([high, low], 1), jnp.concatenate([flips[...], flips[...]], 0))
    by_pair = (3, 16, 2, 8, 128)
    reverse = flipped[:, :128].reshape(by_pair)
    negate = flipped[:, 128:].reshape(by_pair)
    packed = packed.reshape(by_pair)
    own = flags[0] == 1
    first = jnp.where(own, negate[:, :, 0:1], reverse[:, :, 1:2])
    second = jnp.where(own, reverse[:, :, 1:2], reverse[:, :, 0:1])
    mirrored = jnp.concatenate([first, second], 2) * signs((1, 1, 1, 8, 128))
    sub = lax.broadcasted_iota(jnp.int32, (1, 1, 1, 8, 128), 3)
    lowest = (sub % 4 == 0) & (flags[1] == 1)
    main = jnp.where(lowest, 0.5 * (packed + mirrored), packed)
    extra = jnp.where(lowest, 0.5 * (packed - mirrored), 0.0)
    main = table_left(left, unstacked(main.reshape(768, 128)))
    extra = table_left(left_extra, unstacked(extra.reshape(768, 128)))
    spectrum = stacked(jnp.concatenate([main, extra], 0)).reshape(120, 8, 128)
    spectrum = twiddled(spectrum, twiddle[0], twiddle[1])
    spectrum = lane_pass(spectrum.reshape(960, 128), lanes).reshape(3, 320, 128)
    normal = waves[0] * spectrum[0] + waves[1] * spectrum[1] + waves[2] * spectrum[2]
    damp = damping[...]
    projected = jnp.concatenate([(spectrum[c] - waves[c] * normal) * damp for c in range(3)], 0)
    projected = lane_pass(projected, lanes_back)
    projected = twiddled(projected, twiddle[0], -twiddle[1])
    projected = unstacked(projected.reshape(960, 128))
    put_pairs(out, stacked(table_left(back, projected)).reshape(3, 32, 8, 128))


def y_back_kernel(back, lanes, twiddle, values, replies, out):
    spectrum = lane_pass(take_pairs(values), lanes)
    spectrum = twiddled(spectrum, twiddle[0], -twiddle[1])
    spectrum = table_left(back, unstacked(spectrum.reshape(768, 128)))
    codes, exponent = encoded(stacked(spectrum).reshape(3, 32, 8, 128))
    for c in range(3):
        out[:, c] = narrow(codes[c])
    for t in range(4):
        out[:, 3 + t] = replies[:, t]
    lane = lax.broadcasted_iota(jnp.int32, (1, 8, 128), 2)
    out[:, 7] = narrow(jnp.where(lane == 76, exponent, wide(replies[:, 4])))


def last_kernel(owner, slots, back, values, weights, cells_high, cells_low, out, markers):
    interpolate(owner, slots, values, weights, cells_high, cells_low, markers)
    steps = step(wide(values[:, 7])[:, :, 76:77])
    spectrum = [(wide(values[:, c]) * steps).reshape(256, 128) for c in range(3)]
    field = table_right(jnp.transpose(jnp.concatenate(spectrum, 1)), back)
    out[...] = field.reshape(3, 16, 8, 256)


VMEM = pl.BlockSpec(memory_space=pltpu.VMEM)
SMEM = pl.BlockSpec(memory_space=pltpu.SMEM)
HBM = pl.BlockSpec(memory_space=pltpu.HBM)


def call(kernel, specs, shapes, scratch=(), out_specs=None):
    single = not isinstance(shapes, tuple)
    structs = [jax.ShapeDtypeStruct(s, F32) if isinstance(s, list) else s
               for s in ((shapes,) if single else shapes)]
    outs = out_specs or [VMEM] * len(structs)
    return pl.pallas_call(
        kernel,
        out_shape=structs[0] if single else structs,
        in_specs=specs,
        out_specs=outs[0] if single else outs,
        scratch_shapes=list(scratch),
        compiler_params=pltpu.CompilerParams(vmem_limit_bytes=48 << 20),
    )


def codes_of(count, tiles):
    return jax.ShapeDtypeStruct((count, tiles, 8, 128), jnp.int16)


def signed(indices):
    return jnp.where(indices <= (N - 1) // 2, indices, indices - N)


def wave_tables(marks, row, col):
    first, pair, slot = (m[:, None] for m in marks)
    lane = jnp.arange(128, dtype=jnp.int32)[None, :]
    second = jnp.where(row == 0, 16, 32 - row)
    index_x = first + 16 * (lane // 8)
    index_y = jnp.where(pair == 0, row, second) + 32 * (lane % 8)
    index_z = jnp.where(slot < 0, N // 2, 4 * col + slot) + 0 * lane
    scale = 2.0 * jnp.pi / N
    full_sq, waves = 0.0, []
    for index in (index_x, index_y, index_z):
        full = scale * signed(index).astype(F32)
        full_sq = full_sq + full * full
        waves.append(jnp.where(2 * index == N, 0.0, full))
    wave_sq = waves[0] * waves[0] + waves[1] * waves[1] + waves[2] * waves[2]
    still = wave_sq == 0.0
    inverse = jnp.where(still, 0.0, lax.rsqrt(jnp.where(still, 1.0, wave_sq)))
    units = jnp.stack([w * inverse for w in waves])
    return units, 1.0 / (1.0 + DT_STEP * VISCOSITY * full_sq)


def moved(x, axis):
    return lax.all_to_all(x, axis, split_axis=0, concat_axis=0, tiled=True)


def shifted(plane, axis, by):
    count = lax.axis_size(axis)
    return lax.ppermute(plane, axis, [(i, (i + by) % count) for i in range(count)])


def local(velocity, positions, weights, stiffness, rest_sq, owner_column, brick_index):
    row, col = lax.axis_index("row"), lax.axis_index("col")
    z_fore, z_back = z_tables()
    y_fore, y_back, y_lanes, y_lanes_back, y_twiddle = y_tables()
    x_fore, x_extra, x_back, x_lanes, x_lanes_back, x_twiddle, marks, flips = x_tables()
    flags = jnp.stack([row == 0, col == 0]).astype(jnp.int32)

    owner = owner_column.reshape(32)
    spread_outs = (codes_of(32, 5), jax.ShapeDtypeStruct((32,), jnp.int32))
    pushes, slots = call(
        spread_kernel, [HBM] * 6, spread_outs,
        [pltpu.SMEM((32,), jnp.int32), pltpu.SMEM((32,), jnp.int32), pltpu.VMEM((1, 32), BF16),
         pltpu.VMEM((1, 32), BF16), pltpu.VMEM((3, 32, 128), BF16), pltpu.VMEM((32, 3, 8, 128), BF16),
         pltpu.SMEM((32,), jnp.int32), pltpu.VMEM((32, 24, 128), F32), pltpu.VMEM((96, 128), F32),
         pltpu.VMEM((32, 5, 8, 128), F32), pltpu.SemaphoreType.DMA((6,))], [VMEM, SMEM],
    )(*(pltpu.with_memory_space_constraint(x, pltpu.HBM) for x in (
        owner, brick_index, stiffness.reshape(1, 32), rest_sq.reshape(1, 32), positions.transpose(1, 0, 2), weights)))
    x_first, x_last, y_last = call(
        planes_kernel, [SMEM, VMEM], ([3, 1, 8, 256], [3, 1, 8, 256], [3, 16, 1, 256]))(slots, velocity)
    y_low = shifted(y_last, "col", 1)
    x_low = shifted(x_last, "row", 1)
    x_high = shifted(x_first, "row", -1)
    pushes = moved(pushes, "col")
    ids = pushes[:, 4, 0, 73:76].astype(jnp.int32)

    field = call(add_up_kernel, [SMEM, VMEM], ([32, 8, 128],) * 3, [pltpu.VMEM((32, 8, 128), F32)] * 3)(ids, pushes)
    spectrum, turned = call(star_kernel, [VMEM] * 8, (codes_of(32, 4), [3, 32, 8, 128]))(
        z_fore, velocity, x_low, x_high, y_low, *field)
    spectrum = moved(spectrum, "col")
    spectrum = call(y_kernel, [VMEM] * 4, codes_of(16, 7))(y_fore, y_lanes, y_twiddle, spectrum)
    marks = [jnp.asarray(m, jnp.int32) for m in marks]
    spectrum, marks = lax.optimization_barrier((spectrum, marks))
    spectrum = moved(spectrum, "row")
    units, damping = wave_tables(marks, row, col)
    spectrum = call(x_kernel, [SMEM] + [VMEM] * 10, codes_of(16, 7))(
        flags, x_fore, x_extra, x_back, x_lanes, x_lanes_back, x_twiddle, flips, units, damping, spectrum)
    spectrum = moved(spectrum, "row")
    cells = jax.ShapeDtypeStruct((32, 64, 128), BF16)
    replies, cells_high, cells_low = call(reply_kernel, [SMEM, VMEM, VMEM], (codes_of(32, 5), cells, cells))(
        ids, turned, weights)
    spectrum = call(y_back_kernel, [VMEM] * 5, codes_of(32, 8))(
        y_back, y_lanes_back, y_twiddle, spectrum, replies)
    spectrum = moved(spectrum, "col")
    new_velocity, marker_velocity = call(
        last_kernel, [SMEM, SMEM] + [VMEM] * 5, ([3, 16, 8, 256], [3, 32, 128]))(
        owner, slots, z_back, spectrum, weights, cells_high, cells_low)
    return new_velocity, marker_velocity.transpose(1, 0, 2)


def solution(mesh):
    both = ("row", "col")
    placed = (
        P(None, "row", "col", None),
        P(both, None, None),
        P(both, None, None, None),
        P(both),
        P(both),
        P(both, None),
        P(both),
    )
    return jax.shard_map(
        local,
        mesh=mesh,
        in_specs=placed,
        out_specs=(P(None, "row", "col", None), P(both, None, None)),
        check_vma=False,
    )
```

```python
import jax
import jax.numpy as jnp
import numpy as np
from jax import lax
from jax.experimental import pallas as pl
from jax.experimental.pallas import tpu as pltpu
from jax.sharding import PartitionSpec as P


DT_STEP = 0.5
VISCOSITY = 0.1
N = 256
FIRST = np.array([k for r in range(16) for k in ((0, 16) if r == 0 else (r, 32 - r))])
F32 = jnp.float32
BF16 = jnp.bfloat16
TURN = 2.0 * np.pi


def split_table(table):
    table = np.asarray(table, np.float32)
    high = table.astype(BF16)
    low = (table - high.astype(np.float32)).astype(BF16)
    return np.stack([high, low])


def rotation(angle):
    rows, cols = angle.shape
    out = np.zeros((rows, 2, 4, cols, 2, 4))
    for j in range(4):
        out[:, 0, j, :, 0, j] = np.cos(angle)
        out[:, 0, j, :, 1, j] = np.sin(angle)
        out[:, 1, j, :, 0, j] = -np.sin(angle)
        out[:, 1, j, :, 1, j] = np.cos(angle)
    return out.reshape(rows * 8, cols * 8)


def z_tables():
    z = np.arange(N)
    fore = np.zeros((32, 2, 4, N))
    back = np.zeros((32, 2, 4, N))
    for k in range(128):
        angle = TURN / N * (k * z % N)
        twice = 2.0 if k else 1.0
        sine = np.sin(angle) if k else -np.cos(np.pi * z)
        fore[k // 4, 0, k % 4] = np.cos(angle)
        fore[k // 4, 1, k % 4] = -sine
        back[k // 4, 0, k % 4] = twice * np.cos(angle) / N
        back[k // 4, 1, k % 4] = -twice * sine / N
    return split_table(fore.reshape(N, N)), split_table(back.reshape(N, N))


def y_tables():
    angle = TURN / 32 * np.outer(FIRST, np.arange(32))
    fore = split_table(rotation(angle))
    back = split_table(rotation(-angle.T) / N)
    small = TURN / 8 * np.outer(np.arange(8), np.arange(8))
    cosine, sine = (np.kron(np.eye(16), f(small)) for f in (np.cos, np.sin))
    lanes_fore = split_table(np.concatenate([cosine, sine], 1))
    lanes_back = split_table(np.concatenate([cosine, -sine], 1))
    phase = TURN / N * np.outer(FIRST, np.tile(np.arange(8), 16))
    twiddle = np.stack([np.cos(phase), np.sin(phase)]).astype(np.float32)[:, :, None, :]
    phase = TURN / N * np.outer(FIRST, np.arange(128) // 8 % 8)
    side_twiddle = np.stack([np.cos(phase), np.sin(phase)]).astype(np.float32)[:, :, None, :]
    side = np.zeros((128, 2, 128))
    for c in range(3):
        for y in range(8):
            side[8 * y + 4 + c, 0, 8 * c:8 * c + 8] = np.cos(small[y])
            side[8 * y + 4 + c, 1, 8 * c:8 * c + 8] = np.sin(small[y])
    return fore, back, lanes_fore, lanes_back, twiddle, split_table(side.reshape(128, 256)), side_twiddle


def x_tables():
    angle = TURN / 16 * np.outer(np.arange(16), np.arange(16))
    pair = np.eye(2)

    def both(turn):
        grid = np.zeros((16, 2, 8, 16, 2, 8))
        base = rotation(turn).reshape(16, 8, 16, 8)
        for p in range(2):
            grid[:, p, :, :, p, :] = base
        return grid

    main = both(angle).reshape(256, 256)
    extra = both(angle).reshape(8, 2, 2, 2, 4, 16, 2, 2, 4)[:, :, :, :, 0]
    extra = extra.transpose(0, 3, 1, 2, 4, 5, 6, 7).copy()
    extra[..., 1:] = 0.0
    extra = extra.reshape(64, 256)
    back_main = both(-angle).reshape(256, 256) / N
    back_extra = both(-angle).reshape(16, 2, 2, 4, 8, 2, 2, 2, 4)[..., 0]
    back_extra = back_extra.transpose(0, 1, 2, 3, 4, 7, 5, 6).copy()
    back_extra[:, :, :, 1:] = 0.0
    back_extra = back_extra.reshape(256, 64) / N
    back = np.concatenate([back_main, back_extra], 1)
    cosine, sine = (np.kron(f(angle), np.eye(8)) for f in (np.cos, np.sin))
    lanes_fore = split_table(np.concatenate([cosine, sine], 1))
    lanes_back = split_table(np.concatenate([cosine, -sine], 1))
    phase = TURN / N * np.outer(np.arange(16), np.repeat(np.arange(16), 8))
    wide = np.zeros((2, 320, 128), np.float32)
    k_main = np.repeat(np.arange(16), 16)
    k_extra = (2 * np.arange(8)[:, None, None, None] + np.arange(2)[None, None, :, None]
               + np.zeros((8, 2, 2, 2), int)).reshape(64)
    p_main = np.tile(np.repeat(np.arange(2), 8), 16)
    p_extra = np.tile(np.arange(2), 32)
    j_main = np.tile(np.arange(4), 64)
    first = np.concatenate([k_main, k_extra])
    wide[0] = np.cos(phase)[first]
    wide[1] = np.sin(phase)[first]
    marks = (first, np.concatenate([p_main, p_extra]), np.concatenate([j_main, np.full(64, -1)]))
    reverse = np.kron(np.eye(16), np.eye(8)[(7 - np.arange(8))])
    negate = np.kron(np.eye(16), np.eye(8)[(-np.arange(8)) % 8])
    flips = np.concatenate([reverse, negate], 1).astype(BF16)
    return (split_table(main), split_table(extra), split_table(back), lanes_fore, lanes_back,
            wide.reshape(2, 40, 8, 128), marks, flips)


def dot(a, b, dims=((1,), (0,))):
    return lax.dot_general(a, b, (dims, ((), ())), preferred_element_type=F32)


def halves(x):
    high = x.astype(BF16)
    return high, (x - high.astype(F32)).astype(BF16)


def table_left(table, x, dims=((1,), (0,))):
    high, low = halves(x)
    return dot(table[0], high, dims) + dot(table[0], low, dims) + dot(table[1], high, dims)


def table_right(x, table, dims=((1,), (0,))):
    high, low = halves(x)
    return dot(high, table[0], dims) + dot(low, table[0], dims) + dot(high, table[1], dims)


def signs(shape):
    at = lax.broadcasted_iota(jnp.int32, shape, len(shape) - 2)
    return jnp.where(at % 8 < 4, 1.0, -1.0).astype(F32)


def swapped(x):
    return pltpu.roll(x, 4, 1) * signs((1, 8, 128))


def lane_pass(x, table):
    high, low = halves(x)
    twice = jnp.concatenate([table[0], table[0]], 0)
    both = dot(jnp.concatenate([high, low], 1), twice) + dot(high, table[1])
    rows = x.shape[0]
    cosine = both[:, :128].reshape(rows // 8, 8, 128)
    sine = both[:, 128:].reshape(rows // 8, 8, 128)
    return cosine + swapped(sine)


def stacked(x):
    return jnp.concatenate([x[:, 128 * c:128 * c + 128] for c in range(3)], 0)


def unstacked(x):
    rows = x.shape[0] // 3
    return jnp.concatenate([x[rows * c:rows * c + rows] for c in range(3)], 1)


def twiddled(x, cosine, sine):
    groups = cosine.shape[0]
    turned = swapped(x)
    parts = [x[groups * c:groups * c + groups] * cosine + turned[groups * c:groups * c + groups] * sine
             for c in range(3)]
    return jnp.concatenate(parts, 0)


def tile_place(slot, c):
    at = 3 * slot + c
    return at >> 1, at & 1


def lane_half(shape=(8, 128)):
    return lax.broadcasted_iota(jnp.int32, shape, len(shape) - 1) // 64


def to_exponent(largest):
    return jnp.ceil(16.0 * jnp.log(jnp.maximum(largest, 1e-36)))


def steps_per_unit(exponent):
    return 32767.0 * jnp.exp(exponent * (-1.0 / 16.0))


def step(exponent):
    return jnp.exp(exponent * (1.0 / 16.0)) * (1.0 / 32767.0)


def narrow(codes):
    return codes.astype(jnp.int32).astype(jnp.int16)


def wide(codes):
    return codes.astype(jnp.int32).astype(F32)


def row_largest(x):
    return jnp.max(jnp.abs(x), axis=-1, keepdims=True)


def encoded(x):
    largest = jnp.max(jnp.abs(x), axis=0)
    largest = jnp.broadcast_to(jnp.max(largest, axis=-1, keepdims=True), largest.shape)
    exponent = to_exponent(largest)
    return jnp.round(x * steps_per_unit(exponent)[None]), exponent


def put_pairs(out, spectrum, side=None):
    if side is not None:
        spectrum = jnp.concatenate([spectrum, side[None]], 0)
    codes, exponent = encoded(spectrum)
    codes = codes.reshape(-1, 16, 2, 8, 128)
    exponent = exponent.reshape(16, 2, 8, 128)
    for p in range(2):
        for c in range(3):
            out[:, 3 * p + c] = narrow(codes[c, :, p])
    lane = lax.broadcasted_iota(jnp.int32, (1, 8, 128), 2)
    rest = 0.0 if side is None else codes[3, :, 0] + pltpu.roll(codes[3, :, 1], 32, 2)
    out[:, 6] = narrow(jnp.where(lane == 64, exponent[:, 0], jnp.where(lane == 65, exponent[:, 1], rest)))


def take_pairs(values, sides=False):
    rest = wide(values[:, 6])
    steps = [jnp.broadcast_to(step(rest[:, :, 64 + p:65 + p]), (16, 8, 128)) for p in range(2)]
    top = lax.broadcasted_iota(jnp.int32, (1, 8, 128), 2) >= 120
    parts = []
    for c in range(3):
        pair = []
        for p in range(2):
            part = wide(values[:, 3 * p + c]) * steps[p]
            if sides:
                side = rest * steps[p]
                side = jnp.concatenate([side[1:], side[:1]], 0)
                part = part + jnp.where(top, pltpu.roll(side, 120 - 32 * p - 8 * c, 2), 0.0)
            pair.append(part)
        parts.append(jnp.stack(pair, 1).reshape(256, 128))
    return jnp.concatenate(parts, 0)


def to_column(row):
    size = row.shape[1]
    same = (lax.broadcasted_iota(jnp.int32, (size, size), 0)
            == lax.broadcasted_iota(jnp.int32, (size, size), 1))
    return jnp.sum(jnp.where(same, row, 0.0), axis=1, keepdims=True)


def spread_kernel(owner_in, brick_in, stiffness_in, rest_in, positions_in, weights_in, out, slots, owner, brick, stiffness, rest_sq, positions, weights, count, cubes, marks, total, arrived):
    pairs = ((weights_in, weights), (positions_in, positions), (rest_in, rest_sq),
             (stiffness_in, stiffness), (owner_in, owner), (brick_in, brick))
    copies = [pltpu.make_async_copy(a, b, arrived.at[i]) for i, (a, b) in enumerate(pairs)]
    for copy in copies:
        copy.start()
    total[...] = jnp.zeros(total.shape, F32)
    for d in range(32):
        count[d] = 0
    for copy in copies:
        copy.wait()
    place = [positions[c].astype(F32) for c in range(3)]
    segment = [pltpu.roll(p, 127, 1) - p for p in place]
    stretch = (segment[0] * segment[0] + segment[1] * segment[1] + segment[2] * segment[2])
    stretch = stretch / to_column(rest_sq[...].astype(F32))
    pull = 0.5 * to_column(stiffness[...].astype(F32)) * (stretch - 1.0)
    force = []
    for c in range(3):
        tension = pull * segment[c]
        force.append(tension - pltpu.roll(tension, 1, 1))
    largest = []
    for n in range(32):
        w0, w1, w2 = (weights[n, a].astype(F32) for a in range(3))
        cells = (w0[:, None, :] * w1[None, :, :]).reshape(64, 128)
        cells = jnp.concatenate([cells, cells], 0)
        pushed = jnp.concatenate([force[c][n:n + 1] * w2 for c in range(3)], 0)
        cells_high, cells_low = halves(cells)
        pushed_high, pushed_low = halves(pushed)
        both = ((1,), (1,))
        cube = dot(jnp.concatenate([pushed_high, pushed_low], 1), jnp.concatenate([cells_high, cells_high], 1), both)
        cube = cube + dot(pushed_high, cells_low, both)
        cubes[n] = cube
        largest += [jnp.max(jnp.abs(cube[8 * c:8 * c + 8]), axis=0, keepdims=True) for c in range(3)]
    largest = jnp.concatenate(largest, 0)
    exponent = to_exponent(jnp.broadcast_to(row_largest(largest), (96, 128)))
    marks[...] = exponent
    steps = steps_per_unit(exponent)
    for n in range(32):
        for c in range(3):
            cubes[n, 8 * c:8 * c + 8] = jnp.round(cubes[n, 8 * c:8 * c + 8] * steps[3 * n + c:3 * n + c + 1])
    half = lane_half()
    lane = lax.broadcasted_iota(jnp.int32, (8, 128), 1)

    @pl.loop(0, 32, unroll=4)
    def _(n):
        d = owner[n]
        s = count[d]
        count[d] = s + 1
        slots[n] = s
        slots[32 + n] = d
        last = jnp.where(lane == 73 + s, brick[n].astype(F32), 0.0)
        for c in range(3):
            tile, side = tile_place(s, c)
            pltpu.store(total.at[d, tile], cubes[n, 8 * c:8 * c + 8, :], mask=half == side)
            last = jnp.where(lane == 64 + 3 * s + c, marks[pl.ds(3 * n + c, 1), :], last)
        own = (lane == 73 + s) | ((lane >= 64 + 3 * s) & (lane < 67 + 3 * s))
        pltpu.store(total.at[d, 4], last, mask=own)

    out[...] = narrow(total[...])


def planes_kernel(_, velocity, x_last, y_last):
    for c in range(3):
        x_last[c] = velocity[c, 15:16]
        y_last[c] = velocity[c, :, 7:8, :]


def add_up_kernel(ids, pushes, field0, field1, field2, other0, other1, other2):
    sums = ((field0, field1, field2), (other0, other1, other2))
    for group in sums:
        for field in group:
            field[...] = jnp.zeros(field.shape, F32)
    half = lane_half()

    @pl.loop(0, 16, unroll=4)
    def _(pair):
        for odd in range(2):
            src = 2 * pair + odd
            tiles = [wide(pushes[src, t]) for t in range(5)]
            turned = [pltpu.roll(tile, 64, 1) for tile in tiles]
            steps = step(tiles[4])
            for slot in range(3):
                brick = ids[src, slot]
                x_half, z_block = brick >> 5, brick & 31
                for c in range(3):
                    at = 3 * slot + c
                    tile, side = tile_place(slot, c)
                    codes = jnp.where(half == side, tiles[tile], turned[tile])
                    cube = codes * jnp.broadcast_to(steps[:, 64 + at:65 + at], (8, 128))
                    sums[odd][c][z_block] += jnp.where(half == x_half, cube, 0.0)

    for c in range(3):
        sums[0][c][...] = sums[0][c][...] + sums[1][c][...]


def star_kernel(table, velocity, x_low, y_low, field0, field1, field2, out, turned):
    u = [velocity[c].reshape(128, 256) for c in range(3)]
    sub = lax.broadcasted_iota(jnp.int32, (16, 8, 256), 1)
    rows = []
    beyond = jnp.zeros((16, 8, 256), F32)
    for c in range(3):
        v = velocity[c]
        beyond = jnp.where(sub == c, v[:, 0:1, :], beyond)
        turned[c] = jnp.transpose(u[c]).reshape(32, 8, 128)
        ahead = jnp.concatenate([v[1:], jnp.zeros((1, 8, 256), F32)], 0)
        behind = jnp.concatenate([x_low[c], v[:-1]], 0)
        total = u[0] * (ahead - behind).reshape(128, 256)
        ahead = jnp.where(sub == 7, 0.0, pltpu.roll(v, 7, 1))
        behind = jnp.where(sub == 0, y_low[c], pltpu.roll(v, 1, 1))
        total = total + u[1] * (ahead - behind).reshape(128, 256)
        total = total + u[2] * (pltpu.roll(u[c], 255, 1) - pltpu.roll(u[c], 1, 1))
        rows.append(u[c] - (0.5 * DT_STEP) * total)
    beyond = y_low[1] * beyond
    side = jnp.zeros((8, 8, 256), F32)
    for c in range(3):
        side = jnp.where(sub[:8] == 4 + c, (x_low[0, 0] * velocity[c, 0]).reshape(8, 1, 256), side)
    beyond = (-0.5 * DT_STEP) * (beyond + jnp.concatenate([side, jnp.zeros((8, 8, 256), F32)], 0))
    star = jnp.concatenate(rows + [beyond.reshape(128, 256)], 0)
    spectrum = table_left(table, star, ((1,), (1,)))
    field = jnp.concatenate([field[...].reshape(256, 128) for field in (field0, field1, field2)], 1)
    total = spectrum[:, :384] + table_left(table, DT_STEP * field)
    total = jnp.concatenate([stacked(total), spectrum[:, 384:]], 0)
    codes, exponent = encoded(total.reshape(4, 32, 8, 128))
    for t in range(3):
        out[:, t] = narrow(codes[t])
    lane = lax.broadcasted_iota(jnp.int32, (1, 8, 128), 2)
    out[:, 3] = narrow(jnp.where(lane == 3, exponent, codes[3]))


def reply_kernel(ids, turned, weights, out, cells_high, cells_low):
    for n in range(32):
        w0, w1 = (weights[n, a].astype(F32) for a in range(2))
        cells_high[n], cells_low[n] = halves((w0[:, None, :] * w1[None, :, :]).reshape(64, 128))
    half = lane_half()
    lane = lax.broadcasted_iota(jnp.int32, (8, 128), 1)

    @pl.loop(0, 32, unroll=4)
    def _(src):
        cubes, largest = [], []
        for slot in range(3):
            brick = ids[src, slot]
            x_half, z_block = brick >> 5, brick & 31
            for c in range(3):
                tile = turned[c, z_block]
                cube = jnp.where(half == x_half, tile, pltpu.roll(tile, 64, 1))
                largest.append(jnp.max(jnp.abs(cube), axis=0, keepdims=True))
                cubes.append(cube)
        largest = jnp.concatenate(largest + largest[:7], 0)
        exponent = to_exponent(jnp.broadcast_to(row_largest(largest), (16, 128)))
        steps = steps_per_unit(exponent)
        codes = [jnp.round(cube * steps[at:at + 1]) for at, cube in enumerate(cubes)]
        last = jnp.zeros((8, 128), F32)
        for at in range(9):
            last = jnp.where(lane == 64 + at, exponent[at:at + 1], last)
        codes.append(last)
        for t in range(5):
            out[src, t] = narrow(jnp.where(half == 0, codes[2 * t], codes[2 * t + 1]))


def interpolate(slots, replies, weights, cells_high, cells_low, out):
    half = lane_half()
    lane = lax.broadcasted_iota(jnp.int32, (8, 128), 1)
    for n in range(32):
        d, s = slots[32 + n], slots[n]
        steps = step(wide(replies[d, 7]))
        parts = []
        for c in range(3):
            tile, side = tile_place(s, c)
            cube = wide(replies[d, 3 + tile])
            cube = jnp.where(half == side, cube, pltpu.roll(cube, 64, 1))
            own = jnp.sum(jnp.where(lane == 64 + 3 * s + c, steps, 0.0), axis=1, keepdims=True)
            parts.append(cube * own)
        cube_high, cube_low = halves(jnp.concatenate(parts, 0)[:, :64])
        w2 = weights[n, 2].astype(F32)
        high = cells_high[n]
        partial = dot(cube_high, high) + dot(cube_low, high) + dot(cube_high, cells_low[n])
        for c in range(3):
            out[c, n:n + 1] = jnp.sum(partial[8 * c:8 * c + 8] * w2, axis=0, keepdims=True)


def y_kernel(left, lanes, twiddle, side_lanes, side_twiddle, values, out):
    beyond = wide(values[:, 3])
    steps = jnp.broadcast_to(step(beyond[:, :, 3:4]), (32, 8, 128))
    beyond = beyond * steps
    lane = lax.broadcasted_iota(jnp.int32, (1, 8, 128), 2) % 8
    last = lane == 7
    side = jnp.where(lane >= 4, beyond, 0.0).reshape(256, 128)
    beyond = jnp.concatenate([beyond[1:], beyond[:1]], 0)
    spectrum = []
    for c in range(3):
        part = wide(values[:, c]) * steps + jnp.where(last, pltpu.roll(beyond, 7 - c, 2), 0.0)
        spectrum.append(part.reshape(256, 128))
    spectrum = table_left(left, jnp.concatenate(spectrum + [side], 1))
    side = spectrum[:, 384:].reshape(32, 8, 128)
    side = side * side_twiddle[0] + swapped(side) * side_twiddle[1]
    spectrum = stacked(spectrum).reshape(96, 8, 128)
    spectrum = twiddled(spectrum, twiddle[0], twiddle[1])
    spectrum = lane_pass(spectrum.reshape(768, 128), lanes)
    side = lane_pass(side.reshape(256, 128), side_lanes)
    put_pairs(out, spectrum.reshape(3, 32, 8, 128), side)


def x_kernel(flags, left, left_extra, back, lanes, lanes_back, twiddle, flips, waves, damping, values, out):
    packed = take_pairs(values, True)
    high, low = halves(packed)
    flipped = dot(jnp.concatenate([high, low], 1), jnp.concatenate([flips[...], flips[...]], 0))
    by_pair = (3, 16, 2, 8, 128)
    reverse = flipped[:, :128].reshape(by_pair)
    negate = flipped[:, 128:].reshape(by_pair)
    packed = packed.reshape(by_pair)
    own = flags[0] == 1
    first = jnp.where(own, negate[:, :, 0:1], reverse[:, :, 1:2])
    second = jnp.where(own, reverse[:, :, 1:2], reverse[:, :, 0:1])
    mirrored = jnp.concatenate([first, second], 2) * signs((1, 1, 1, 8, 128))
    sub = lax.broadcasted_iota(jnp.int32, (1, 1, 1, 8, 128), 3)
    lowest = (sub % 4 == 0) & (flags[1] == 1)
    main = jnp.where(lowest, 0.5 * (packed + mirrored), packed)
    extra = jnp.where(lowest, 0.5 * (packed - mirrored), 0.0)
    main = table_left(left, unstacked(main.reshape(768, 128)))
    extra = table_left(left_extra, unstacked(extra.reshape(768, 128)))
    spectrum = stacked(jnp.concatenate([main, extra], 0)).reshape(120, 8, 128)
    spectrum = twiddled(spectrum, twiddle[0], twiddle[1])
    spectrum = lane_pass(spectrum.reshape(960, 128), lanes).reshape(3, 320, 128)
    normal = waves[0] * spectrum[0] + waves[1] * spectrum[1] + waves[2] * spectrum[2]
    damp = damping[...]
    projected = jnp.concatenate([(spectrum[c] - waves[c] * normal) * damp for c in range(3)], 0)
    projected = lane_pass(projected, lanes_back)
    projected = twiddled(projected, twiddle[0], -twiddle[1])
    projected = unstacked(projected.reshape(960, 128))
    put_pairs(out, stacked(table_left(back, projected)).reshape(3, 32, 8, 128))


def y_back_kernel(back, lanes, twiddle, values, replies, out):
    spectrum = lane_pass(take_pairs(values), lanes)
    spectrum = twiddled(spectrum, twiddle[0], -twiddle[1])
    spectrum = table_left(back, unstacked(spectrum.reshape(768, 128)))
    codes, exponent = encoded(stacked(spectrum).reshape(3, 32, 8, 128))
    for c in range(3):
        out[:, c] = narrow(codes[c])
    for t in range(4):
        out[:, 3 + t] = replies[:, t]
    lane = lax.broadcasted_iota(jnp.int32, (1, 8, 128), 2)
    out[:, 7] = narrow(jnp.where(lane == 76, exponent, wide(replies[:, 4])))


def last_kernel(slots, back, values, weights, cells_high, cells_low, out, markers):
    interpolate(slots, values, weights, cells_high, cells_low, markers)
    steps = step(wide(values[:, 7])[:, :, 76:77])
    spectrum = [(wide(values[:, c]) * steps).reshape(256, 128) for c in range(3)]
    field = table_right(jnp.transpose(jnp.concatenate(spectrum, 1)), back)
    out[...] = field.reshape(3, 16, 8, 256)


VMEM = pl.BlockSpec(memory_space=pltpu.VMEM)
SMEM = pl.BlockSpec(memory_space=pltpu.SMEM)
HBM = pl.BlockSpec(memory_space=pltpu.HBM)


def call(kernel, specs, shapes, scratch=(), out_specs=None):
    single = not isinstance(shapes, tuple)
    structs = [jax.ShapeDtypeStruct(s, F32) if isinstance(s, list) else s
               for s in ((shapes,) if single else shapes)]
    outs = out_specs or [VMEM] * len(structs)
    return pl.pallas_call(
        kernel,
        out_shape=structs[0] if single else structs,
        in_specs=specs,
        out_specs=outs[0] if single else outs,
        scratch_shapes=list(scratch),
        compiler_params=pltpu.CompilerParams(vmem_limit_bytes=48 << 20),
    )


def codes_of(count, tiles):
    return jax.ShapeDtypeStruct((count, tiles, 8, 128), jnp.int16)


def signed(indices):
    return jnp.where(indices <= (N - 1) // 2, indices, indices - N)


def wave_tables(marks, row, col):
    first, pair, slot = (m[:, None] for m in marks)
    lane = jnp.arange(128, dtype=jnp.int32)[None, :]
    second = jnp.where(row == 0, 16, 32 - row)
    index_x = first + 16 * (lane // 8)
    index_y = jnp.where(pair == 0, row, second) + 32 * (lane % 8)
    index_z = jnp.where(slot < 0, N // 2, 4 * col + slot) + 0 * lane
    scale = 2.0 * jnp.pi / N
    full_sq, waves = 0.0, []
    for index in (index_x, index_y, index_z):
        full = scale * signed(index).astype(F32)
        full_sq = full_sq + full * full
        waves.append(jnp.where(2 * index == N, 0.0, full))
    wave_sq = waves[0] * waves[0] + waves[1] * waves[1] + waves[2] * waves[2]
    still = wave_sq == 0.0
    inverse = jnp.where(still, 0.0, lax.rsqrt(jnp.where(still, 1.0, wave_sq)))
    units = jnp.stack([w * inverse for w in waves])
    return units, 1.0 / (1.0 + DT_STEP * VISCOSITY * full_sq)


def moved(x, axis):
    return lax.all_to_all(x, axis, split_axis=0, concat_axis=0, tiled=True)


def shifted(plane, axis, by):
    count = lax.axis_size(axis)
    return lax.ppermute(plane, axis, [(i, (i + by) % count) for i in range(count)])


def local(velocity, positions, weights, stiffness, rest_sq, owner_column, brick_index):
    row, col = lax.axis_index("row"), lax.axis_index("col")
    z_fore, z_back = z_tables()
    y_fore, y_back, y_lanes, y_lanes_back, y_twiddle, side_lanes, side_twiddle = y_tables()
    x_fore, x_extra, x_back, x_lanes, x_lanes_back, x_twiddle, marks, flips = x_tables()
    flags = jnp.stack([row == 0, col == 0]).astype(jnp.int32)

    owner = owner_column.reshape(32)
    spread_outs = (codes_of(32, 5), jax.ShapeDtypeStruct((64,), jnp.int32))
    pushes, slots = call(
        spread_kernel, [HBM] * 6, spread_outs,
        [pltpu.SMEM((32,), jnp.int32), pltpu.SMEM((32,), jnp.int32), pltpu.VMEM((1, 32), BF16),
         pltpu.VMEM((1, 32), BF16), pltpu.VMEM((3, 32, 128), BF16), pltpu.VMEM((32, 3, 8, 128), BF16),
         pltpu.SMEM((32,), jnp.int32), pltpu.VMEM((32, 24, 128), F32), pltpu.VMEM((96, 128), F32),
         pltpu.VMEM((32, 5, 8, 128), F32), pltpu.SemaphoreType.DMA((6,))], [VMEM, SMEM],
    )(*(pltpu.with_memory_space_constraint(x, pltpu.HBM) for x in (
        owner, brick_index, stiffness.reshape(1, 32), rest_sq.reshape(1, 32), positions.transpose(1, 0, 2), weights)))
    x_last, y_last = call(planes_kernel, [SMEM, VMEM], ([3, 1, 8, 256], [3, 16, 1, 256]))(slots, velocity)
    y_low = shifted(y_last, "col", 1)
    x_low = shifted(x_last, "row", 1)
    pushes = moved(pushes, "col")
    ids = pushes[:, 4, 0, 73:76].astype(jnp.int32)

    field = call(add_up_kernel, [SMEM, VMEM], ([32, 8, 128],) * 3, [pltpu.VMEM((32, 8, 128), F32)] * 3)(ids, pushes)
    spectrum, turned = call(star_kernel, [VMEM] * 7, (codes_of(32, 4), [3, 32, 8, 128]))(
        z_fore, velocity, x_low, y_low, *field)
    spectrum = moved(spectrum, "col")
    spectrum = call(y_kernel, [VMEM] * 6, codes_of(16, 7))(
        y_fore, y_lanes, y_twiddle, side_lanes, side_twiddle, spectrum)
    marks = [jnp.asarray(m, jnp.int32) for m in marks]
    spectrum, marks = lax.optimization_barrier((spectrum, marks))
    spectrum = moved(spectrum, "row")
    units, damping = wave_tables(marks, row, col)
    spectrum = call(x_kernel, [SMEM] + [VMEM] * 10, codes_of(16, 7))(
        flags, x_fore, x_extra, x_back, x_lanes, x_lanes_back, x_twiddle, flips, units, damping, spectrum)
    spectrum = moved(spectrum, "row")
    cells = jax.ShapeDtypeStruct((32, 64, 128), BF16)
    replies, cells_high, cells_low = call(reply_kernel, [SMEM, VMEM, VMEM], (codes_of(32, 5), cells, cells))(
        ids, turned, weights)
    spectrum = call(y_back_kernel, [VMEM] * 5, codes_of(32, 8))(
        y_back, y_lanes_back, y_twiddle, spectrum, replies)
    spectrum = moved(spectrum, "col")
    new_velocity, marker_velocity = call(
        last_kernel, [SMEM] + [VMEM] * 5, ([3, 16, 8, 256], [3, 32, 128]))(
        slots, z_back, spectrum, weights, cells_high, cells_low)
    return new_velocity, marker_velocity.transpose(1, 0, 2)


def solution(mesh):
    both = ("row", "col")
    placed = (
        P(None, "row", "col", None),
        P(both, None, None),
        P(both, None, None, None),
        P(both),
        P(both),
        P(both, None),
        P(both),
    )
    return jax.shard_map(
        local,
        mesh=mesh,
        in_specs=placed,
        out_specs=(P(None, "row", "col", None), P(both, None, None)),
        check_vma=False,
    )
```

```python
import jax
import jax.numpy as jnp
import numpy as np
from jax import lax
from jax.experimental import pallas as pl
from jax.experimental.pallas import tpu as pltpu
from jax.sharding import PartitionSpec as P


DT_STEP = 0.5
VISCOSITY = 0.1
N = 256
FIRST = np.array([k for r in range(16) for k in ((0, 16) if r == 0 else (r, 32 - r))])
F32 = jnp.float32
BF16 = jnp.bfloat16
TURN = 2.0 * np.pi


def split_table(table):
    table = np.asarray(table, np.float32)
    high = table.astype(BF16)
    low = (table - high.astype(np.float32)).astype(BF16)
    return np.stack([high, low])


def rotation(angle):
    rows, cols = angle.shape
    out = np.zeros((rows, 2, 4, cols, 2, 4))
    for j in range(4):
        out[:, 0, j, :, 0, j] = np.cos(angle)
        out[:, 0, j, :, 1, j] = np.sin(angle)
        out[:, 1, j, :, 0, j] = -np.sin(angle)
        out[:, 1, j, :, 1, j] = np.cos(angle)
    return out.reshape(rows * 8, cols * 8)


def z_tables():
    z = np.arange(N)
    fore = np.zeros((32, 2, 4, N))
    back = np.zeros((32, 2, 4, N))
    for k in range(128):
        angle = TURN / N * (k * z % N)
        twice = 2.0 if k else 1.0
        sine = np.sin(angle) if k else -np.cos(np.pi * z)
        fore[k // 4, 0, k % 4] = np.cos(angle)
        fore[k // 4, 1, k % 4] = -sine
        back[k // 4, 0, k % 4] = twice * np.cos(angle) / N
        back[k // 4, 1, k % 4] = -twice * sine / N
    return split_table(fore.reshape(N, N)), split_table(back.reshape(N, N))


def y_tables():
    angle = TURN / 32 * np.outer(FIRST, np.arange(32))
    fore = split_table(rotation(angle))
    back = split_table(rotation(-angle.T) / N)
    small = TURN / 8 * np.outer(np.arange(8), np.arange(8))
    cosine, sine = (np.kron(np.eye(16), f(small)) for f in (np.cos, np.sin))
    lanes_fore = split_table(np.concatenate([cosine, sine], 1))
    lanes_back = split_table(np.concatenate([cosine, -sine], 1))
    phase = TURN / N * np.outer(FIRST, np.tile(np.arange(8), 16))
    twiddle = np.stack([np.cos(phase), np.sin(phase)]).astype(np.float32)[:, :, None, :]
    phase = TURN / N * np.outer(FIRST, np.arange(128) // 8 % 8)
    side_twiddle = np.stack([np.cos(phase), np.sin(phase)]).astype(np.float32)[:, :, None, :]
    side = np.zeros((128, 2, 128))
    for c in range(3):
        for y in range(8):
            side[8 * y + 4 + c, 0, 8 * c:8 * c + 8] = np.cos(small[y])
            side[8 * y + 4 + c, 1, 8 * c:8 * c + 8] = np.sin(small[y])
    return fore, back, lanes_fore, lanes_back, twiddle, split_table(side.reshape(128, 256)), side_twiddle


def x_tables():
    angle = TURN / 16 * np.outer(np.arange(16), np.arange(16))
    pair = np.eye(2)

    def both(turn):
        grid = np.zeros((16, 2, 8, 16, 2, 8))
        base = rotation(turn).reshape(16, 8, 16, 8)
        for p in range(2):
            grid[:, p, :, :, p, :] = base
        return grid

    main = both(angle).reshape(256, 256)
    extra = both(angle).reshape(8, 2, 2, 2, 4, 16, 2, 2, 4)[:, :, :, :, 0]
    extra = extra.transpose(0, 3, 1, 2, 4, 5, 6, 7).copy()
    extra[..., 1:] = 0.0
    extra = extra.reshape(64, 256)
    back_main = both(-angle).reshape(256, 256) / N
    back_extra = both(-angle).reshape(16, 2, 2, 4, 8, 2, 2, 2, 4)[..., 0]
    back_extra = back_extra.transpose(0, 1, 2, 3, 4, 7, 5, 6).copy()
    back_extra[:, :, :, 1:] = 0.0
    back_extra = back_extra.reshape(256, 64) / N
    back = np.concatenate([back_main, back_extra], 1)
    cosine, sine = (np.kron(f(angle), np.eye(8)) for f in (np.cos, np.sin))
    lanes_fore = split_table(np.concatenate([cosine, sine], 1))
    lanes_back = split_table(np.concatenate([cosine, -sine], 1))
    phase = TURN / N * np.outer(np.arange(16), np.repeat(np.arange(16), 8))
    wide = np.zeros((2, 320, 128), np.float32)
    k_main = np.repeat(np.arange(16), 16)
    k_extra = (2 * np.arange(8)[:, None, None, None] + np.arange(2)[None, None, :, None]
               + np.zeros((8, 2, 2, 2), int)).reshape(64)
    p_main = np.tile(np.repeat(np.arange(2), 8), 16)
    p_extra = np.tile(np.arange(2), 32)
    j_main = np.tile(np.arange(4), 64)
    first = np.concatenate([k_main, k_extra])
    wide[0] = np.cos(phase)[first]
    wide[1] = np.sin(phase)[first]
    marks = (first, np.concatenate([p_main, p_extra]), np.concatenate([j_main, np.full(64, -1)]))
    reverse = np.kron(np.eye(16), np.eye(8)[(7 - np.arange(8))])
    negate = np.kron(np.eye(16), np.eye(8)[(-np.arange(8)) % 8])
    flips = np.concatenate([reverse, negate], 1).astype(BF16)
    return (split_table(main), split_table(extra), split_table(back), lanes_fore, lanes_back,
            wide.reshape(2, 40, 8, 128), marks, flips)


def dot(a, b, dims=((1,), (0,))):
    return lax.dot_general(a, b, (dims, ((), ())), preferred_element_type=F32)


def halves(x):
    high = x.astype(BF16)
    return high, (x - high.astype(F32)).astype(BF16)


def table_left(table, x, dims=((1,), (0,))):
    high, low = halves(x)
    return dot(table[0], high, dims) + dot(table[0], low, dims) + dot(table[1], high, dims)


def table_right(x, table, dims=((1,), (0,))):
    high, low = halves(x)
    return dot(high, table[0], dims) + dot(low, table[0], dims) + dot(high, table[1], dims)


def signs(shape):
    at = lax.broadcasted_iota(jnp.int32, shape, len(shape) - 2)
    return jnp.where(at % 8 < 4, 1.0, -1.0).astype(F32)


def swapped(x):
    return pltpu.roll(x, 4, 1) * signs((1, 8, 128))


def lane_pass(x, table):
    high, low = halves(x)
    twice = jnp.concatenate([table[0], table[0]], 0)
    both = dot(jnp.concatenate([high, low], 1), twice) + dot(high, table[1])
    rows = x.shape[0]
    cosine = both[:, :128].reshape(rows // 8, 8, 128)
    sine = both[:, 128:].reshape(rows // 8, 8, 128)
    return cosine + swapped(sine)


def stacked(x):
    return jnp.concatenate([x[:, 128 * c:128 * c + 128] for c in range(3)], 0)


def unstacked(x):
    rows = x.shape[0] // 3
    return jnp.concatenate([x[rows * c:rows * c + rows] for c in range(3)], 1)


def twiddled(x, cosine, sine):
    groups = cosine.shape[0]
    turned = swapped(x)
    parts = [x[groups * c:groups * c + groups] * cosine + turned[groups * c:groups * c + groups] * sine
             for c in range(3)]
    return jnp.concatenate(parts, 0)


def tile_place(slot, c):
    at = 3 * slot + c
    return at >> 1, at & 1


def lane_half(shape=(8, 128)):
    return lax.broadcasted_iota(jnp.int32, shape, len(shape) - 1) // 64


def to_exponent(largest):
    return jnp.ceil(16.0 * jnp.log(jnp.maximum(largest, 1e-36)))


def steps_per_unit(exponent):
    return 32767.0 * jnp.exp(exponent * (-1.0 / 16.0))


def step(exponent):
    return jnp.exp(exponent * (1.0 / 16.0)) * (1.0 / 32767.0)


def narrow(codes):
    return codes.astype(jnp.int32).astype(jnp.int16)


def wide(codes):
    return codes.astype(jnp.int32).astype(F32)


def row_largest(x):
    return jnp.max(jnp.abs(x), axis=-1, keepdims=True)


def encoded(x):
    largest = jnp.max(jnp.abs(x), axis=0)
    largest = jnp.broadcast_to(jnp.max(largest, axis=-1, keepdims=True), largest.shape)
    exponent = to_exponent(largest)
    return jnp.round(x * steps_per_unit(exponent)[None]), exponent


def put_pairs(out, spectrum, side=None):
    if side is not None:
        spectrum = jnp.concatenate([spectrum, side[None]], 0)
    codes, exponent = encoded(spectrum)
    codes = codes.reshape(-1, 16, 2, 8, 128)
    exponent = exponent.reshape(16, 2, 8, 128)
    for p in range(2):
        for c in range(3):
            out[:, 3 * p + c] = narrow(codes[c, :, p])
    lane = lax.broadcasted_iota(jnp.int32, (1, 8, 128), 2)
    rest = 0.0 if side is None else codes[3, :, 0] + pltpu.roll(codes[3, :, 1], 32, 2)
    out[:, 6] = narrow(jnp.where(lane == 64, exponent[:, 0], jnp.where(lane == 65, exponent[:, 1], rest)))


def take_pairs(values, sides=False):
    rest = wide(values[:, 6])
    steps = [jnp.broadcast_to(step(rest[:, :, 64 + p:65 + p]), (16, 8, 128)) for p in range(2)]
    top = lax.broadcasted_iota(jnp.int32, (1, 8, 128), 2) >= 120
    parts = []
    for c in range(3):
        pair = []
        for p in range(2):
            part = wide(values[:, 3 * p + c]) * steps[p]
            if sides:
                side = rest * steps[p]
                side = jnp.concatenate([side[1:], side[:1]], 0)
                part = part + jnp.where(top, pltpu.roll(side, 120 - 32 * p - 8 * c, 2), 0.0)
            pair.append(part)
        parts.append(jnp.stack(pair, 1).reshape(256, 128))
    return jnp.concatenate(parts, 0)


def to_column(row):
    size = row.shape[1]
    same = (lax.broadcasted_iota(jnp.int32, (size, size), 0)
            == lax.broadcasted_iota(jnp.int32, (size, size), 1))
    return jnp.sum(jnp.where(same, row, 0.0), axis=1, keepdims=True)


def spread_kernel(owner_in, brick_in, stiffness_in, rest_in, positions_in, weights_in, out, slots, owner, brick, stiffness, rest_sq, positions, weights, count, cubes, marks, total, arrived):
    pairs = ((weights_in, weights), (positions_in, positions), (rest_in, rest_sq),
             (stiffness_in, stiffness), (owner_in, owner), (brick_in, brick))
    copies = [pltpu.make_async_copy(a, b, arrived.at[i]) for i, (a, b) in enumerate(pairs)]
    for copy in copies:
        copy.start()
    total[...] = jnp.zeros(total.shape, F32)
    for d in range(32):
        count[d] = 0
    for copy in copies:
        copy.wait()
    place = [positions[c].astype(F32) for c in range(3)]
    segment = [pltpu.roll(p, 127, 1) - p for p in place]
    stretch = (segment[0] * segment[0] + segment[1] * segment[1] + segment[2] * segment[2])
    stretch = stretch / to_column(rest_sq[...].astype(F32))
    pull = 0.5 * to_column(stiffness[...].astype(F32)) * (stretch - 1.0)
    force = []
    for c in range(3):
        tension = pull * segment[c]
        force.append(tension - pltpu.roll(tension, 1, 1))
    largest = []
    for n in range(32):
        w0, w1, w2 = (weights[n, a].astype(F32) for a in range(3))
        cells = (w0[:, None, :] * w1[None, :, :]).reshape(64, 128)
        cells = jnp.concatenate([cells, cells], 0)
        pushed = jnp.concatenate([force[c][n:n + 1] * w2 for c in range(3)], 0)
        cells_high, cells_low = halves(cells)
        pushed_high, pushed_low = halves(pushed)
        both = ((1,), (1,))
        cube = dot(jnp.concatenate([pushed_high, pushed_low], 1), jnp.concatenate([cells_high, cells_high], 1), both)
        cube = cube + dot(pushed_high, cells_low, both)
        cubes[n] = cube
        largest += [jnp.max(jnp.abs(cube[8 * c:8 * c + 8]), axis=0, keepdims=True) for c in range(3)]
    largest = jnp.concatenate(largest, 0)
    exponent = to_exponent(jnp.broadcast_to(row_largest(largest), (96, 128)))
    marks[...] = exponent
    steps = steps_per_unit(exponent)
    for n in range(32):
        for c in range(3):
            cubes[n, 8 * c:8 * c + 8] = jnp.round(cubes[n, 8 * c:8 * c + 8] * steps[3 * n + c:3 * n + c + 1])
    half = lane_half()
    lane = lax.broadcasted_iota(jnp.int32, (8, 128), 1)

    @pl.loop(0, 32, unroll=4)
    def _(n):
        d = owner[n]
        s = count[d]
        count[d] = s + 1
        slots[n] = s
        slots[32 + n] = d
        last = jnp.where(lane == 73 + s, brick[n].astype(F32), 0.0)
        for c in range(3):
            tile, side = tile_place(s, c)
            pltpu.store(total.at[d, tile], cubes[n, 8 * c:8 * c + 8, :], mask=half == side)
            last = jnp.where(lane == 64 + 3 * s + c, marks[pl.ds(3 * n + c, 1), :], last)
        own = (lane == 73 + s) | ((lane >= 64 + 3 * s) & (lane < 67 + 3 * s))
        pltpu.store(total.at[d, 4], last, mask=own)

    out[...] = narrow(total[...])


def y_plane_kernel(_, velocity, y_last):
    for c in range(3):
        y_last[c] = velocity[c, :, 7:8, :]


def x_plane_kernel(_, velocity, x_last):
    for c in range(3):
        x_last[c] = velocity[c, 15:16]


def add_up_kernel(ids, pushes, field0, field1, field2, other0, other1, other2):
    sums = ((field0, field1, field2), (other0, other1, other2))
    for group in sums:
        for field in group:
            field[...] = jnp.zeros(field.shape, F32)
    half = lane_half()

    @pl.loop(0, 16, unroll=4)
    def _(pair):
        for odd in range(2):
            src = 2 * pair + odd
            tiles = [wide(pushes[src, t]) for t in range(5)]
            turned = [pltpu.roll(tile, 64, 1) for tile in tiles]
            steps = step(tiles[4])
            for slot in range(3):
                brick = ids[src, slot]
                x_half, z_block = brick >> 5, brick & 31
                for c in range(3):
                    at = 3 * slot + c
                    tile, side = tile_place(slot, c)
                    codes = jnp.where(half == side, tiles[tile], turned[tile])
                    cube = codes * jnp.broadcast_to(steps[:, 64 + at:65 + at], (8, 128))
                    sums[odd][c][z_block] += jnp.where(half == x_half, cube, 0.0)

    for c in range(3):
        sums[0][c][...] = sums[0][c][...] + sums[1][c][...]


def star_kernel(table, velocity, x_low, y_low, field0, field1, field2, out, turned):
    u = [velocity[c].reshape(128, 256) for c in range(3)]
    sub = lax.broadcasted_iota(jnp.int32, (16, 8, 256), 1)
    rows = []
    beyond = jnp.zeros((16, 8, 256), F32)
    for c in range(3):
        v = velocity[c]
        beyond = jnp.where(sub == c, v[:, 0:1, :], beyond)
        turned[c] = jnp.transpose(u[c]).reshape(32, 8, 128)
        ahead = jnp.concatenate([v[1:], jnp.zeros((1, 8, 256), F32)], 0)
        behind = jnp.concatenate([x_low[c], v[:-1]], 0)
        total = u[0] * (ahead - behind).reshape(128, 256)
        ahead = jnp.where(sub == 7, 0.0, pltpu.roll(v, 7, 1))
        behind = jnp.where(sub == 0, y_low[c], pltpu.roll(v, 1, 1))
        total = total + u[1] * (ahead - behind).reshape(128, 256)
        total = total + u[2] * (pltpu.roll(u[c], 255, 1) - pltpu.roll(u[c], 1, 1))
        rows.append(u[c] - (0.5 * DT_STEP) * total)
    beyond = y_low[1] * beyond
    side = jnp.zeros((8, 8, 256), F32)
    for c in range(3):
        side = jnp.where(sub[:8] == 4 + c, (x_low[0, 0] * velocity[c, 0]).reshape(8, 1, 256), side)
    beyond = (-0.5 * DT_STEP) * (beyond + jnp.concatenate([side, jnp.zeros((8, 8, 256), F32)], 0))
    star = jnp.concatenate(rows + [beyond.reshape(128, 256)], 0)
    spectrum = table_left(table, star, ((1,), (1,)))
    field = jnp.concatenate([field[...].reshape(256, 128) for field in (field0, field1, field2)], 1)
    total = spectrum[:, :384] + table_left(table, DT_STEP * field)
    total = jnp.concatenate([stacked(total), spectrum[:, 384:]], 0)
    codes, exponent = encoded(total.reshape(4, 32, 8, 128))
    for t in range(3):
        out[:, t] = narrow(codes[t])
    lane = lax.broadcasted_iota(jnp.int32, (1, 8, 128), 2)
    out[:, 3] = narrow(jnp.where(lane == 3, exponent, codes[3]))


def reply_kernel(ids, turned, weights, out, cells_high, cells_low):
    for n in range(32):
        w0, w1 = (weights[n, a].astype(F32) for a in range(2))
        cells_high[n], cells_low[n] = halves((w0[:, None, :] * w1[None, :, :]).reshape(64, 128))
    half = lane_half()
    lane = lax.broadcasted_iota(jnp.int32, (8, 128), 1)

    @pl.loop(0, 32, unroll=4)
    def _(src):
        cubes, largest = [], []
        for slot in range(3):
            brick = ids[src, slot]
            x_half, z_block = brick >> 5, brick & 31
            for c in range(3):
                tile = turned[c, z_block]
                cube = jnp.where(half == x_half, tile, pltpu.roll(tile, 64, 1))
                largest.append(jnp.max(jnp.abs(cube), axis=0, keepdims=True))
                cubes.append(cube)
        largest = jnp.concatenate(largest + largest[:7], 0)
        exponent = to_exponent(jnp.broadcast_to(row_largest(largest), (16, 128)))
        steps = steps_per_unit(exponent)
        codes = [jnp.round(cube * steps[at:at + 1]) for at, cube in enumerate(cubes)]
        last = jnp.zeros((8, 128), F32)
        for at in range(9):
            last = jnp.where(lane == 64 + at, exponent[at:at + 1], last)
        codes.append(last)
        for t in range(5):
            out[src, t] = narrow(jnp.where(half == 0, codes[2 * t], codes[2 * t + 1]))


def interpolate(slots, replies, weights, cells_high, cells_low, out):
    half = lane_half()
    lane = lax.broadcasted_iota(jnp.int32, (8, 128), 1)
    for n in range(32):
        d, s = slots[32 + n], slots[n]
        steps = step(wide(replies[d, 7]))
        parts = []
        for c in range(3):
            tile, side = tile_place(s, c)
            cube = wide(replies[d, 3 + tile])
            cube = jnp.where(half == side, cube, pltpu.roll(cube, 64, 1))
            own = jnp.sum(jnp.where(lane == 64 + 3 * s + c, steps, 0.0), axis=1, keepdims=True)
            parts.append(cube * own)
        cube_high, cube_low = halves(jnp.concatenate(parts, 0)[:, :64])
        w2 = weights[n, 2].astype(F32)
        high = cells_high[n]
        partial = dot(jnp.concatenate([cube_high, cube_low], 1), jnp.concatenate([high, high], 0))
        partial = partial + dot(cube_high, cells_low[n])
        for c in range(3):
            out[c, n:n + 1] = jnp.sum(partial[8 * c:8 * c + 8] * w2, axis=0, keepdims=True)


def y_kernel(left, lanes, twiddle, side_lanes, side_twiddle, values, out):
    beyond = wide(values[:, 3])
    steps = jnp.broadcast_to(step(beyond[:, :, 3:4]), (32, 8, 128))
    beyond = beyond * steps
    lane = lax.broadcasted_iota(jnp.int32, (1, 8, 128), 2) % 8
    last = lane == 7
    side = jnp.where(lane >= 4, beyond, 0.0).reshape(256, 128)
    beyond = jnp.concatenate([beyond[1:], beyond[:1]], 0)
    spectrum = []
    for c in range(3):
        part = wide(values[:, c]) * steps + jnp.where(last, pltpu.roll(beyond, 7 - c, 2), 0.0)
        spectrum.append(part.reshape(256, 128))
    spectrum = table_left(left, jnp.concatenate(spectrum + [side], 1))
    side = spectrum[:, 384:].reshape(32, 8, 128)
    side = side * side_twiddle[0] + swapped(side) * side_twiddle[1]
    spectrum = stacked(spectrum).reshape(96, 8, 128)
    spectrum = twiddled(spectrum, twiddle[0], twiddle[1])
    spectrum = lane_pass(spectrum.reshape(768, 128), lanes)
    side = lane_pass(side.reshape(256, 128), side_lanes)
    put_pairs(out, spectrum.reshape(3, 32, 8, 128), side)


def x_kernel(flags, left, left_extra, back, lanes, lanes_back, twiddle, flips, waves, damping, values, out):
    packed = take_pairs(values, True)
    high, low = halves(packed)
    flipped = dot(jnp.concatenate([high, low], 1), jnp.concatenate([flips[...], flips[...]], 0))
    by_pair = (3, 16, 2, 8, 128)
    reverse = flipped[:, :128].reshape(by_pair)
    negate = flipped[:, 128:].reshape(by_pair)
    packed = packed.reshape(by_pair)
    own = flags[0] == 1
    first = jnp.where(own, negate[:, :, 0:1], reverse[:, :, 1:2])
    second = jnp.where(own, reverse[:, :, 1:2], reverse[:, :, 0:1])
    mirrored = jnp.concatenate([first, second], 2) * signs((1, 1, 1, 8, 128))
    sub = lax.broadcasted_iota(jnp.int32, (1, 1, 1, 8, 128), 3)
    lowest = (sub % 4 == 0) & (flags[1] == 1)
    main = jnp.where(lowest, 0.5 * (packed + mirrored), packed)
    extra = jnp.where(lowest, 0.5 * (packed - mirrored), 0.0)
    main = table_left(left, unstacked(main.reshape(768, 128)))
    extra = table_left(left_extra, unstacked(extra.reshape(768, 128)))
    spectrum = stacked(jnp.concatenate([main, extra], 0)).reshape(120, 8, 128)
    spectrum = twiddled(spectrum, twiddle[0], twiddle[1])
    spectrum = lane_pass(spectrum.reshape(960, 128), lanes).reshape(3, 320, 128)
    normal = waves[0] * spectrum[0] + waves[1] * spectrum[1] + waves[2] * spectrum[2]
    damp = damping[...]
    projected = jnp.concatenate([(spectrum[c] - waves[c] * normal) * damp for c in range(3)], 0)
    projected = lane_pass(projected, lanes_back)
    projected = twiddled(projected, twiddle[0], -twiddle[1])
    projected = unstacked(projected.reshape(960, 128))
    put_pairs(out, stacked(table_left(back, projected)).reshape(3, 32, 8, 128))


def y_back_kernel(back, lanes, twiddle, values, replies, out):
    spectrum = lane_pass(take_pairs(values), lanes)
    spectrum = twiddled(spectrum, twiddle[0], -twiddle[1])
    spectrum = table_left(back, unstacked(spectrum.reshape(768, 128)))
    codes, exponent = encoded(stacked(spectrum).reshape(3, 32, 8, 128))
    for c in range(3):
        out[:, c] = narrow(codes[c])
    for t in range(4):
        out[:, 3 + t] = replies[:, t]
    lane = lax.broadcasted_iota(jnp.int32, (1, 8, 128), 2)
    out[:, 7] = narrow(jnp.where(lane == 76, exponent, wide(replies[:, 4])))


def last_kernel(slots, back, values, weights, cells_high, cells_low, out, markers):
    interpolate(slots, values, weights, cells_high, cells_low, markers)
    steps = step(wide(values[:, 7])[:, :, 76:77])
    spectrum = [(wide(values[:, c]) * steps).reshape(256, 128) for c in range(3)]
    field = table_right(jnp.transpose(jnp.concatenate(spectrum, 1)), back)
    out[...] = field.reshape(3, 16, 8, 256)


VMEM = pl.BlockSpec(memory_space=pltpu.VMEM)
SMEM = pl.BlockSpec(memory_space=pltpu.SMEM)
HBM = pl.BlockSpec(memory_space=pltpu.HBM)


def call(kernel, specs, shapes, scratch=(), out_specs=None):
    single = not isinstance(shapes, tuple)
    structs = [jax.ShapeDtypeStruct(s, F32) if isinstance(s, list) else s
               for s in ((shapes,) if single else shapes)]
    outs = out_specs or [VMEM] * len(structs)
    return pl.pallas_call(
        kernel,
        out_shape=structs[0] if single else structs,
        in_specs=specs,
        out_specs=outs[0] if single else outs,
        scratch_shapes=list(scratch),
        compiler_params=pltpu.CompilerParams(vmem_limit_bytes=48 << 20),
    )


def codes_of(count, tiles):
    return jax.ShapeDtypeStruct((count, tiles, 8, 128), jnp.int16)


def signed(indices):
    return jnp.where(indices <= (N - 1) // 2, indices, indices - N)


def wave_tables(marks, row, col):
    first, pair, slot = (m[:, None] for m in marks)
    lane = jnp.arange(128, dtype=jnp.int32)[None, :]
    second = jnp.where(row == 0, 16, 32 - row)
    index_x = first + 16 * (lane // 8)
    index_y = jnp.where(pair == 0, row, second) + 32 * (lane % 8)
    index_z = jnp.where(slot < 0, N // 2, 4 * col + slot) + 0 * lane
    scale = 2.0 * jnp.pi / N
    full_sq, waves = 0.0, []
    for index in (index_x, index_y, index_z):
        full = scale * signed(index).astype(F32)
        full_sq = full_sq + full * full
        waves.append(jnp.where(2 * index == N, 0.0, full))
    wave_sq = waves[0] * waves[0] + waves[1] * waves[1] + waves[2] * waves[2]
    still = wave_sq == 0.0
    inverse = jnp.where(still, 0.0, lax.rsqrt(jnp.where(still, 1.0, wave_sq)))
    units = jnp.stack([w * inverse for w in waves])
    return units, 1.0 / (1.0 + DT_STEP * VISCOSITY * full_sq)


def moved(x, axis):
    return lax.all_to_all(x, axis, split_axis=0, concat_axis=0, tiled=True)


def shifted(plane, axis, by):
    count = lax.axis_size(axis)
    return lax.ppermute(plane, axis, [(i, (i + by) % count) for i in range(count)])


def local(velocity, positions, weights, stiffness, rest_sq, owner_column, brick_index):
    row, col = lax.axis_index("row"), lax.axis_index("col")
    z_fore, z_back = z_tables()
    y_fore, y_back, y_lanes, y_lanes_back, y_twiddle, side_lanes, side_twiddle = y_tables()
    x_fore, x_extra, x_back, x_lanes, x_lanes_back, x_twiddle, marks, flips = x_tables()
    flags = jnp.stack([row == 0, col == 0]).astype(jnp.int32)

    owner = owner_column.reshape(32)
    spread_outs = (codes_of(32, 5), jax.ShapeDtypeStruct((64,), jnp.int32))
    pushes, slots = call(
        spread_kernel, [HBM] * 6, spread_outs,
        [pltpu.SMEM((32,), jnp.int32), pltpu.SMEM((32,), jnp.int32), pltpu.VMEM((1, 32), BF16),
         pltpu.VMEM((1, 32), BF16), pltpu.VMEM((3, 32, 128), BF16), pltpu.VMEM((32, 3, 8, 128), BF16),
         pltpu.SMEM((32,), jnp.int32), pltpu.VMEM((32, 24, 128), F32), pltpu.VMEM((96, 128), F32),
         pltpu.VMEM((32, 5, 8, 128), F32), pltpu.SemaphoreType.DMA((6,))], [VMEM, SMEM],
    )(*(pltpu.with_memory_space_constraint(x, pltpu.HBM) for x in (
        owner, brick_index, stiffness.reshape(1, 32), rest_sq.reshape(1, 32), positions.transpose(1, 0, 2), weights)))
    y_last = call(y_plane_kernel, [SMEM, VMEM], [3, 16, 1, 256])(slots, velocity)
    x_last = call(x_plane_kernel, [VMEM, VMEM], [3, 1, 8, 256])(y_last, velocity)
    y_low = shifted(y_last, "col", 1)
    x_low = shifted(x_last, "row", 1)
    pushes = moved(pushes, "col")
    ids = pushes[:, 4, 0, 73:76].astype(jnp.int32)

    field = call(add_up_kernel, [SMEM, VMEM], ([32, 8, 128],) * 3, [pltpu.VMEM((32, 8, 128), F32)] * 3)(ids, pushes)
    spectrum, turned = call(star_kernel, [VMEM] * 7, (codes_of(32, 4), [3, 32, 8, 128]))(
        z_fore, velocity, x_low, y_low, *field)
    spectrum = moved(spectrum, "col")
    spectrum = call(y_kernel, [VMEM] * 6, codes_of(16, 7))(
        y_fore, y_lanes, y_twiddle, side_lanes, side_twiddle, spectrum)
    marks = [jnp.asarray(m, jnp.int32) for m in marks]
    spectrum, marks = lax.optimization_barrier((spectrum, marks))
    spectrum = moved(spectrum, "row")
    units, damping = wave_tables(marks, row, col)
    spectrum = call(x_kernel, [SMEM] + [VMEM] * 10, codes_of(16, 7))(
        flags, x_fore, x_extra, x_back, x_lanes, x_lanes_back, x_twiddle, flips, units, damping, spectrum)
    spectrum = moved(spectrum, "row")
    cells = jax.ShapeDtypeStruct((32, 64, 128), BF16)
    replies, cells_high, cells_low = call(reply_kernel, [SMEM, VMEM, VMEM], (codes_of(32, 5), cells, cells))(
        ids, turned, weights)
    spectrum = call(y_back_kernel, [VMEM] * 5, codes_of(32, 8))(
        y_back, y_lanes_back, y_twiddle, spectrum, replies)
    spectrum = moved(spectrum, "col")
    new_velocity, marker_velocity = call(
        last_kernel, [SMEM] + [VMEM] * 5, ([3, 16, 8, 256], [3, 32, 128]))(
        slots, z_back, spectrum, weights, cells_high, cells_low)
    return new_velocity, marker_velocity.transpose(1, 0, 2)


def solution(mesh):
    both = ("row", "col")
    placed = (
        P(None, "row", "col", None),
        P(both, None, None),
        P(both, None, None, None),
        P(both),
        P(both),
        P(both, None),
        P(both),
    )
    return jax.shard_map(
        local,
        mesh=mesh,
        in_specs=placed,
        out_specs=(P(None, "row", "col", None), P(both, None, None)),
        check_vma=False,
    )
```

```python
import jax
import jax.numpy as jnp
import numpy as np
from jax import lax
from jax.experimental import pallas as pl
from jax.experimental.pallas import tpu as pltpu
from jax.sharding import PartitionSpec as P


DT_STEP = 0.5
VISCOSITY = 0.1
N = 256
FIRST = np.array([k for r in range(16) for k in ((0, 16) if r == 0 else (r, 32 - r))])
F32 = jnp.float32
BF16 = jnp.bfloat16
TURN = 2.0 * np.pi


def split_table(table):
    table = np.asarray(table, np.float32)
    high = table.astype(BF16)
    low = (table - high.astype(np.float32)).astype(BF16)
    return np.stack([high, low])


def rotation(angle):
    rows, cols = angle.shape
    out = np.zeros((rows, 2, 4, cols, 2, 4))
    for j in range(4):
        out[:, 0, j, :, 0, j] = np.cos(angle)
        out[:, 0, j, :, 1, j] = np.sin(angle)
        out[:, 1, j, :, 0, j] = -np.sin(angle)
        out[:, 1, j, :, 1, j] = np.cos(angle)
    return out.reshape(rows * 8, cols * 8)


def z_tables():
    z = np.arange(N)
    fore = np.zeros((32, 2, 4, N))
    back = np.zeros((32, 2, 4, N))
    for k in range(128):
        angle = TURN / N * (k * z % N)
        twice = 2.0 if k else 1.0
        sine = np.sin(angle) if k else -np.cos(np.pi * z)
        fore[k // 4, 0, k % 4] = np.cos(angle)
        fore[k // 4, 1, k % 4] = -sine
        back[k // 4, 0, k % 4] = twice * np.cos(angle) / N
        back[k // 4, 1, k % 4] = -twice * sine / N
    return split_table(fore.reshape(N, N)), split_table(back.reshape(N, N))


def y_tables():
    angle = TURN / 32 * np.outer(FIRST, np.arange(32))
    fore = split_table(rotation(angle))
    back = split_table(rotation(-angle.T) / N)
    small = TURN / 8 * np.outer(np.arange(8), np.arange(8))
    cosine, sine = (np.kron(np.eye(16), f(small)) for f in (np.cos, np.sin))
    lanes_fore = split_table(np.concatenate([cosine, sine], 1))
    lanes_back = split_table(np.concatenate([cosine, -sine], 1))
    phase = TURN / N * np.outer(FIRST, np.tile(np.arange(8), 16))
    twiddle = np.stack([np.cos(phase), np.sin(phase)]).astype(np.float32)[:, :, None, :]
    phase = TURN / N * np.outer(FIRST, np.arange(128) // 8 % 8)
    side_twiddle = np.stack([np.cos(phase), np.sin(phase)]).astype(np.float32)[:, :, None, :]
    side = np.zeros((128, 2, 128))
    for c in range(3):
        for y in range(8):
            side[8 * y + 4 + c, 0, 8 * c:8 * c + 8] = np.cos(small[y])
            side[8 * y + 4 + c, 1, 8 * c:8 * c + 8] = np.sin(small[y])
    return fore, back, lanes_fore, lanes_back, twiddle, split_table(side.reshape(128, 256)), side_twiddle


def x_tables():
    angle = TURN / 16 * np.outer(np.arange(16), np.arange(16))
    pair = np.eye(2)

    def both(turn):
        grid = np.zeros((16, 2, 8, 16, 2, 8))
        base = rotation(turn).reshape(16, 8, 16, 8)
        for p in range(2):
            grid[:, p, :, :, p, :] = base
        return grid

    main = both(angle).reshape(256, 256)
    extra = both(angle).reshape(8, 2, 2, 2, 4, 16, 2, 2, 4)[:, :, :, :, 0]
    extra = extra.transpose(0, 3, 1, 2, 4, 5, 6, 7).copy()
    extra[..., 1:] = 0.0
    extra = extra.reshape(64, 256)
    back_main = both(-angle).reshape(256, 256) / N
    back_extra = both(-angle).reshape(16, 2, 2, 4, 8, 2, 2, 2, 4)[..., 0]
    back_extra = back_extra.transpose(0, 1, 2, 3, 4, 7, 5, 6).copy()
    back_extra[:, :, :, 1:] = 0.0
    back_extra = back_extra.reshape(256, 64) / N
    back = np.concatenate([back_main, back_extra], 1)
    cosine, sine = (np.kron(f(angle), np.eye(8)) for f in (np.cos, np.sin))
    lanes_fore = split_table(np.concatenate([cosine, sine], 1))
    lanes_back = split_table(np.concatenate([cosine, -sine], 1))
    phase = TURN / N * np.outer(np.arange(16), np.repeat(np.arange(16), 8))
    wide = np.zeros((2, 320, 128), np.float32)
    k_main = np.repeat(np.arange(16), 16)
    k_extra = (2 * np.arange(8)[:, None, None, None] + np.arange(2)[None, None, :, None]
               + np.zeros((8, 2, 2, 2), int)).reshape(64)
    p_main = np.tile(np.repeat(np.arange(2), 8), 16)
    p_extra = np.tile(np.arange(2), 32)
    j_main = np.tile(np.arange(4), 64)
    first = np.concatenate([k_main, k_extra])
    wide[0] = np.cos(phase)[first]
    wide[1] = np.sin(phase)[first]
    marks = (first, np.concatenate([p_main, p_extra]), np.concatenate([j_main, np.full(64, -1)]))
    reverse = np.kron(np.eye(16), np.eye(8)[(7 - np.arange(8))])
    negate = np.kron(np.eye(16), np.eye(8)[(-np.arange(8)) % 8])
    flips = np.concatenate([reverse, negate], 1).astype(BF16)
    return (split_table(main), split_table(extra), split_table(back), lanes_fore, lanes_back,
            wide.reshape(2, 40, 8, 128), marks, flips)


def dot(a, b, dims=((1,), (0,))):
    return lax.dot_general(a, b, (dims, ((), ())), preferred_element_type=F32)


def halves(x):
    high = x.astype(BF16)
    return high, (x - high.astype(F32)).astype(BF16)


def table_left(table, x, dims=((1,), (0,))):
    high, low = halves(x)
    return dot(table[0], high, dims) + dot(table[0], low, dims) + dot(table[1], high, dims)


def table_right(x, table, dims=((1,), (0,))):
    high, low = halves(x)
    return dot(high, table[0], dims) + dot(low, table[0], dims) + dot(high, table[1], dims)


def signs(shape):
    at = lax.broadcasted_iota(jnp.int32, shape, len(shape) - 2)
    return jnp.where(at % 8 < 4, 1.0, -1.0).astype(F32)


def swapped(x):
    return pltpu.roll(x, 4, 1) * signs((1, 8, 128))


def lane_pass(x, table):
    high, low = halves(x)
    twice = jnp.concatenate([table[0], table[0]], 0)
    both = dot(jnp.concatenate([high, low], 1), twice) + dot(high, table[1])
    rows = x.shape[0]
    cosine = both[:, :128].reshape(rows // 8, 8, 128)
    sine = both[:, 128:].reshape(rows // 8, 8, 128)
    return cosine + swapped(sine)


def stacked(x):
    return jnp.concatenate([x[:, 128 * c:128 * c + 128] for c in range(3)], 0)


def unstacked(x):
    rows = x.shape[0] // 3
    return jnp.concatenate([x[rows * c:rows * c + rows] for c in range(3)], 1)


def twiddled(x, cosine, sine):
    groups = cosine.shape[0]
    turned = swapped(x)
    parts = [x[groups * c:groups * c + groups] * cosine + turned[groups * c:groups * c + groups] * sine
             for c in range(3)]
    return jnp.concatenate(parts, 0)


def tile_place(slot, c):
    at = 3 * slot + c
    return at >> 1, at & 1


def lane_half(shape=(8, 128)):
    return lax.broadcasted_iota(jnp.int32, shape, len(shape) - 1) // 64


def to_exponent(largest):
    return jnp.ceil(16.0 * jnp.log(jnp.maximum(largest, 1e-36)))


def steps_per_unit(exponent):
    return 32767.0 * jnp.exp(exponent * (-1.0 / 16.0))


def step(exponent):
    return jnp.exp(exponent * (1.0 / 16.0)) * (1.0 / 32767.0)


def narrow(codes):
    return codes.astype(jnp.int32).astype(jnp.int16)


def wide(codes):
    return codes.astype(jnp.int32).astype(F32)


def row_largest(x):
    return jnp.max(jnp.abs(x), axis=-1, keepdims=True)


def encoded(x):
    largest = jnp.max(jnp.abs(x), axis=0)
    largest = jnp.broadcast_to(jnp.max(largest, axis=-1, keepdims=True), largest.shape)
    exponent = to_exponent(largest)
    return jnp.round(x * steps_per_unit(exponent)[None]), exponent


def put_pairs(out, spectrum, side=None):
    if side is not None:
        spectrum = jnp.concatenate([spectrum, side[None]], 0)
    codes, exponent = encoded(spectrum)
    codes = codes.reshape(-1, 16, 2, 8, 128)
    exponent = exponent.reshape(16, 2, 8, 128)
    for p in range(2):
        for c in range(3):
            out[:, 3 * p + c] = narrow(codes[c, :, p])
    lane = lax.broadcasted_iota(jnp.int32, (1, 8, 128), 2)
    rest = 0.0 if side is None else codes[3, :, 0] + pltpu.roll(codes[3, :, 1], 32, 2)
    out[:, 6] = narrow(jnp.where(lane == 64, exponent[:, 0], jnp.where(lane == 65, exponent[:, 1], rest)))


def take_pairs(values, sides=False):
    rest = wide(values[:, 6])
    steps = [jnp.broadcast_to(step(rest[:, :, 64 + p:65 + p]), (16, 8, 128)) for p in range(2)]
    top = lax.broadcasted_iota(jnp.int32, (1, 8, 128), 2) >= 120
    parts = []
    for c in range(3):
        pair = []
        for p in range(2):
            part = wide(values[:, 3 * p + c]) * steps[p]
            if sides:
                side = rest * steps[p]
                side = jnp.concatenate([side[1:], side[:1]], 0)
                part = part + jnp.where(top, pltpu.roll(side, 120 - 32 * p - 8 * c, 2), 0.0)
            pair.append(part)
        parts.append(jnp.stack(pair, 1).reshape(256, 128))
    return jnp.concatenate(parts, 0)


def to_column(row):
    size = row.shape[1]
    same = (lax.broadcasted_iota(jnp.int32, (size, size), 0)
            == lax.broadcasted_iota(jnp.int32, (size, size), 1))
    return jnp.sum(jnp.where(same, row, 0.0), axis=1, keepdims=True)


def spread_kernel(owner_in, brick_in, stiffness_in, rest_in, positions_in, weights_in, out, slots, owner, brick, stiffness, rest_sq, positions, weights, count, cubes, marks, total, arrived):
    pairs = ((weights_in, weights), (positions_in, positions), (rest_in, rest_sq),
             (stiffness_in, stiffness), (owner_in, owner), (brick_in, brick))
    copies = [pltpu.make_async_copy(a, b, arrived.at[i]) for i, (a, b) in enumerate(pairs)]
    for copy in copies:
        copy.start()
    total[...] = jnp.zeros(total.shape, F32)
    for d in range(32):
        count[d] = 0
    for copy in copies:
        copy.wait()
    place = [positions[c].astype(F32) for c in range(3)]
    segment = [pltpu.roll(p, 127, 1) - p for p in place]
    stretch = (segment[0] * segment[0] + segment[1] * segment[1] + segment[2] * segment[2])
    stretch = stretch / to_column(rest_sq[...].astype(F32))
    pull = 0.5 * to_column(stiffness[...].astype(F32)) * (stretch - 1.0)
    force = []
    for c in range(3):
        tension = pull * segment[c]
        force.append(tension - pltpu.roll(tension, 1, 1))
    largest = []
    for n in range(32):
        w0, w1, w2 = (weights[n, a].astype(F32) for a in range(3))
        cells = (w0[:, None, :] * w1[None, :, :]).reshape(64, 128)
        cells = jnp.concatenate([cells, cells], 0)
        pushed = jnp.concatenate([force[c][n:n + 1] * w2 for c in range(3)], 0)
        cells_high, cells_low = halves(cells)
        pushed_high, pushed_low = halves(pushed)
        both = ((1,), (1,))
        cube = dot(jnp.concatenate([pushed_high, pushed_low], 1), jnp.concatenate([cells_high, cells_high], 1), both)
        cube = cube + dot(pushed_high, cells_low, both)
        cubes[n] = cube
        largest += [jnp.max(jnp.abs(cube[8 * c:8 * c + 8]), axis=0, keepdims=True) for c in range(3)]
    largest = jnp.concatenate(largest, 0)
    exponent = to_exponent(jnp.broadcast_to(row_largest(largest), (96, 128)))
    marks[...] = exponent
    steps = steps_per_unit(exponent)
    for n in range(32):
        for c in range(3):
            cubes[n, 8 * c:8 * c + 8] = jnp.round(cubes[n, 8 * c:8 * c + 8] * steps[3 * n + c:3 * n + c + 1])
    half = lane_half()
    lane = lax.broadcasted_iota(jnp.int32, (8, 128), 1)

    @pl.loop(0, 32, unroll=4)
    def _(n):
        d = owner[n]
        s = count[d]
        count[d] = s + 1
        slots[n] = s
        slots[32 + n] = d
        last = jnp.where(lane == 73 + s, brick[n].astype(F32), 0.0)
        for c in range(3):
            tile, side = tile_place(s, c)
            pltpu.store(total.at[d, tile], cubes[n, 8 * c:8 * c + 8, :], mask=half == side)
            last = jnp.where(lane == 64 + 3 * s + c, marks[pl.ds(3 * n + c, 1), :], last)
        own = (lane == 73 + s) | ((lane >= 64 + 3 * s) & (lane < 67 + 3 * s))
        pltpu.store(total.at[d, 4], last, mask=own)

    out[...] = narrow(total[...])


def planes_kernel(_, velocity, x_last, y_last):
    for c in range(3):
        x_last[c] = velocity[c, 15:16]
        y_last[c] = velocity[c, :, 7:8, :]


def add_up_kernel(ids, pushes, table, velocity, out, turned_out, field0, field1, field2, other0, other1, other2):
    sums = ((field0, field1, field2), (other0, other1, other2))
    for group in sums:
        for field in group:
            field[...] = jnp.zeros(field.shape, F32)
    half = lane_half()

    @pl.loop(0, 16, unroll=4)
    def _(pair):
        for odd in range(2):
            src = 2 * pair + odd
            tiles = [wide(pushes[src, t]) for t in range(5)]
            turned = [pltpu.roll(tile, 64, 1) for tile in tiles]
            steps = step(tiles[4])
            for slot in range(3):
                brick = ids[src, slot]
                x_half, z_block = brick >> 5, brick & 31
                for c in range(3):
                    at = 3 * slot + c
                    tile, side = tile_place(slot, c)
                    codes = jnp.where(half == side, tiles[tile], turned[tile])
                    cube = codes * jnp.broadcast_to(steps[:, 64 + at:65 + at], (8, 128))
                    sums[odd][c][z_block] += jnp.where(half == x_half, cube, 0.0)

    for c in range(3):
        turned_out[c] = jnp.transpose(velocity[c].reshape(128, 256)).reshape(32, 8, 128)
    field = jnp.concatenate([(sums[0][c][...] + sums[1][c][...]).reshape(256, 128) for c in range(3)], 1)
    out[...] = table_left(table, DT_STEP * field)


def star_kernel(table, velocity, x_low, y_low, field, out):
    u = [velocity[c].reshape(128, 256) for c in range(3)]
    sub = lax.broadcasted_iota(jnp.int32, (16, 8, 256), 1)
    rows = []
    beyond = jnp.zeros((16, 8, 256), F32)
    for c in range(3):
        v = velocity[c]
        beyond = jnp.where(sub == c, v[:, 0:1, :], beyond)
        ahead = jnp.concatenate([v[1:], jnp.zeros((1, 8, 256), F32)], 0)
        behind = jnp.concatenate([x_low[c], v[:-1]], 0)
        total = u[0] * (ahead - behind).reshape(128, 256)
        ahead = jnp.where(sub == 7, 0.0, pltpu.roll(v, 7, 1))
        behind = jnp.where(sub == 0, y_low[c], pltpu.roll(v, 1, 1))
        total = total + u[1] * (ahead - behind).reshape(128, 256)
        total = total + u[2] * (pltpu.roll(u[c], 255, 1) - pltpu.roll(u[c], 1, 1))
        rows.append(u[c] - (0.5 * DT_STEP) * total)
    beyond = y_low[1] * beyond
    side = jnp.zeros((8, 8, 256), F32)
    for c in range(3):
        side = jnp.where(sub[:8] == 4 + c, (x_low[0, 0] * velocity[c, 0]).reshape(8, 1, 256), side)
    beyond = (-0.5 * DT_STEP) * (beyond + jnp.concatenate([side, jnp.zeros((8, 8, 256), F32)], 0))
    star = jnp.concatenate(rows + [beyond.reshape(128, 256)], 0)
    spectrum = table_left(table, star, ((1,), (1,)))
    total = spectrum[:, :384] + field[...]
    total = jnp.concatenate([stacked(total), spectrum[:, 384:]], 0)
    codes, exponent = encoded(total.reshape(4, 32, 8, 128))
    for t in range(3):
        out[:, t] = narrow(codes[t])
    lane = lax.broadcasted_iota(jnp.int32, (1, 8, 128), 2)
    out[:, 3] = narrow(jnp.where(lane == 3, exponent, codes[3]))


def reply_kernel(ids, turned, weights, out, cells_high, cells_low):
    for n in range(32):
        w0, w1 = (weights[n, a].astype(F32) for a in range(2))
        cells_high[n], cells_low[n] = halves((w0[:, None, :] * w1[None, :, :]).reshape(64, 128))
    half = lane_half()
    lane = lax.broadcasted_iota(jnp.int32, (8, 128), 1)

    @pl.loop(0, 32, unroll=4)
    def _(src):
        cubes, largest = [], []
        for slot in range(3):
            brick = ids[src, slot]
            x_half, z_block = brick >> 5, brick & 31
            for c in range(3):
                tile = turned[c, z_block]
                cube = jnp.where(half == x_half, tile, pltpu.roll(tile, 64, 1))
                largest.append(jnp.max(jnp.abs(cube), axis=0, keepdims=True))
                cubes.append(cube)
        largest = jnp.concatenate(largest + largest[:7], 0)
        exponent = to_exponent(jnp.broadcast_to(row_largest(largest), (16, 128)))
        steps = steps_per_unit(exponent)
        codes = [jnp.round(cube * steps[at:at + 1]) for at, cube in enumerate(cubes)]
        last = jnp.zeros((8, 128), F32)
        for at in range(9):
            last = jnp.where(lane == 64 + at, exponent[at:at + 1], last)
        codes.append(last)
        for t in range(5):
            out[src, t] = narrow(jnp.where(half == 0, codes[2 * t], codes[2 * t + 1]))


def interpolate(slots, replies, weights, cells_high, cells_low, out):
    half = lane_half()
    lane = lax.broadcasted_iota(jnp.int32, (8, 128), 1)
    for n in range(32):
        d, s = slots[32 + n], slots[n]
        steps = step(wide(replies[d, 7]))
        parts = []
        for c in range(3):
            tile, side = tile_place(s, c)
            cube = wide(replies[d, 3 + tile])
            cube = jnp.where(half == side, cube, pltpu.roll(cube, 64, 1))
            own = jnp.sum(jnp.where(lane == 64 + 3 * s + c, steps, 0.0), axis=1, keepdims=True)
            parts.append(cube * own)
        cube_high, cube_low = halves(jnp.concatenate(parts, 0)[:, :64])
        w2 = weights[n, 2].astype(F32)
        high = cells_high[n]
        partial = dot(cube_high, high) + dot(cube_low, high) + dot(cube_high, cells_low[n])
        for c in range(3):
            out[c, n:n + 1] = jnp.sum(partial[8 * c:8 * c + 8] * w2, axis=0, keepdims=True)


def y_kernel(left, lanes, twiddle, side_lanes, side_twiddle, values, out):
    beyond = wide(values[:, 3])
    steps = jnp.broadcast_to(step(beyond[:, :, 3:4]), (32, 8, 128))
    beyond = beyond * steps
    lane = lax.broadcasted_iota(jnp.int32, (1, 8, 128), 2) % 8
    last = lane == 7
    side = jnp.where(lane >= 4, beyond, 0.0).reshape(256, 128)
    beyond = jnp.concatenate([beyond[1:], beyond[:1]], 0)
    spectrum = []
    for c in range(3):
        part = wide(values[:, c]) * steps + jnp.where(last, pltpu.roll(beyond, 7 - c, 2), 0.0)
        spectrum.append(part.reshape(256, 128))
    spectrum = table_left(left, jnp.concatenate(spectrum + [side], 1))
    side = spectrum[:, 384:].reshape(32, 8, 128)
    side = side * side_twiddle[0] + swapped(side) * side_twiddle[1]
    spectrum = stacked(spectrum).reshape(96, 8, 128)
    spectrum = twiddled(spectrum, twiddle[0], twiddle[1])
    spectrum = lane_pass(spectrum.reshape(768, 128), lanes)
    side = lane_pass(side.reshape(256, 128), side_lanes)
    put_pairs(out, spectrum.reshape(3, 32, 8, 128), side)


def x_kernel(flags, left, left_extra, back, lanes, lanes_back, twiddle, flips, waves, damping, values, out):
    packed = take_pairs(values, True)
    high, low = halves(packed)
    flipped = dot(jnp.concatenate([high, low], 1), jnp.concatenate([flips[...], flips[...]], 0))
    by_pair = (3, 16, 2, 8, 128)
    reverse = flipped[:, :128].reshape(by_pair)
    negate = flipped[:, 128:].reshape(by_pair)
    packed = packed.reshape(by_pair)
    own = flags[0] == 1
    first = jnp.where(own, negate[:, :, 0:1], reverse[:, :, 1:2])
    second = jnp.where(own, reverse[:, :, 1:2], reverse[:, :, 0:1])
    mirrored = jnp.concatenate([first, second], 2) * signs((1, 1, 1, 8, 128))
    sub = lax.broadcasted_iota(jnp.int32, (1, 1, 1, 8, 128), 3)
    lowest = (sub % 4 == 0) & (flags[1] == 1)
    main = jnp.where(lowest, 0.5 * (packed + mirrored), packed)
    extra = jnp.where(lowest, 0.5 * (packed - mirrored), 0.0)
    main = table_left(left, unstacked(main.reshape(768, 128)))
    extra = table_left(left_extra, unstacked(extra.reshape(768, 128)))
    spectrum = stacked(jnp.concatenate([main, extra], 0)).reshape(120, 8, 128)
    spectrum = twiddled(spectrum, twiddle[0], twiddle[1])
    spectrum = lane_pass(spectrum.reshape(960, 128), lanes).reshape(3, 320, 128)
    normal = waves[0] * spectrum[0] + waves[1] * spectrum[1] + waves[2] * spectrum[2]
    damp = damping[...]
    projected = jnp.concatenate([(spectrum[c] - waves[c] * normal) * damp for c in range(3)], 0)
    projected = lane_pass(projected, lanes_back)
    projected = twiddled(projected, twiddle[0], -twiddle[1])
    projected = unstacked(projected.reshape(960, 128))
    put_pairs(out, stacked(table_left(back, projected)).reshape(3, 32, 8, 128))


def y_back_kernel(back, lanes, twiddle, values, replies, out):
    spectrum = lane_pass(take_pairs(values), lanes)
    spectrum = twiddled(spectrum, twiddle[0], -twiddle[1])
    spectrum = table_left(back, unstacked(spectrum.reshape(768, 128)))
    codes, exponent = encoded(stacked(spectrum).reshape(3, 32, 8, 128))
    for c in range(3):
        out[:, c] = narrow(codes[c])
    for t in range(4):
        out[:, 3 + t] = replies[:, t]
    lane = lax.broadcasted_iota(jnp.int32, (1, 8, 128), 2)
    out[:, 7] = narrow(jnp.where(lane == 76, exponent, wide(replies[:, 4])))


def last_kernel(slots, back, values, weights, cells_high, cells_low, out, markers):
    interpolate(slots, values, weights, cells_high, cells_low, markers)
    steps = step(wide(values[:, 7])[:, :, 76:77])
    spectrum = [(wide(values[:, c]) * steps).reshape(256, 128) for c in range(3)]
    field = table_right(jnp.transpose(jnp.concatenate(spectrum, 1)), back)
    out[...] = field.reshape(3, 16, 8, 256)


VMEM = pl.BlockSpec(memory_space=pltpu.VMEM)
SMEM = pl.BlockSpec(memory_space=pltpu.SMEM)
HBM = pl.BlockSpec(memory_space=pltpu.HBM)


def call(kernel, specs, shapes, scratch=(), out_specs=None):
    single = not isinstance(shapes, tuple)
    structs = [jax.ShapeDtypeStruct(s, F32) if isinstance(s, list) else s
               for s in ((shapes,) if single else shapes)]
    outs = out_specs or [VMEM] * len(structs)
    return pl.pallas_call(
        kernel,
        out_shape=structs[0] if single else structs,
        in_specs=specs,
        out_specs=outs[0] if single else outs,
        scratch_shapes=list(scratch),
        compiler_params=pltpu.CompilerParams(vmem_limit_bytes=48 << 20),
    )


def codes_of(count, tiles):
    return jax.ShapeDtypeStruct((count, tiles, 8, 128), jnp.int16)


def signed(indices):
    return jnp.where(indices <= (N - 1) // 2, indices, indices - N)


def wave_tables(marks, row, col):
    first, pair, slot = (m[:, None] for m in marks)
    lane = jnp.arange(128, dtype=jnp.int32)[None, :]
    second = jnp.where(row == 0, 16, 32 - row)
    index_x = first + 16 * (lane // 8)
    index_y = jnp.where(pair == 0, row, second) + 32 * (lane % 8)
    index_z = jnp.where(slot < 0, N // 2, 4 * col + slot) + 0 * lane
    scale = 2.0 * jnp.pi / N
    full_sq, waves = 0.0, []
    for index in (index_x, index_y, index_z):
        full = scale * signed(index).astype(F32)
        full_sq = full_sq + full * full
        waves.append(jnp.where(2 * index == N, 0.0, full))
    wave_sq = waves[0] * waves[0] + waves[1] * waves[1] + waves[2] * waves[2]
    still = wave_sq == 0.0
    inverse = jnp.where(still, 0.0, lax.rsqrt(jnp.where(still, 1.0, wave_sq)))
    units = jnp.stack([w * inverse for w in waves])
    return units, 1.0 / (1.0 + DT_STEP * VISCOSITY * full_sq)


def moved(x, axis):
    return lax.all_to_all(x, axis, split_axis=0, concat_axis=0, tiled=True)


def shifted(plane, axis, by):
    count = lax.axis_size(axis)
    return lax.ppermute(plane, axis, [(i, (i + by) % count) for i in range(count)])


def local(velocity, positions, weights, stiffness, rest_sq, owner_column, brick_index):
    row, col = lax.axis_index("row"), lax.axis_index("col")
    z_fore, z_back = z_tables()
    y_fore, y_back, y_lanes, y_lanes_back, y_twiddle, side_lanes, side_twiddle = y_tables()
    x_fore, x_extra, x_back, x_lanes, x_lanes_back, x_twiddle, marks, flips = x_tables()
    flags = jnp.stack([row == 0, col == 0]).astype(jnp.int32)

    owner = owner_column.reshape(32)
    spread_outs = (codes_of(32, 5), jax.ShapeDtypeStruct((64,), jnp.int32))
    pushes, slots = call(
        spread_kernel, [HBM] * 6, spread_outs,
        [pltpu.SMEM((32,), jnp.int32), pltpu.SMEM((32,), jnp.int32), pltpu.VMEM((1, 32), BF16),
         pltpu.VMEM((1, 32), BF16), pltpu.VMEM((3, 32, 128), BF16), pltpu.VMEM((32, 3, 8, 128), BF16),
         pltpu.SMEM((32,), jnp.int32), pltpu.VMEM((32, 24, 128), F32), pltpu.VMEM((96, 128), F32),
         pltpu.VMEM((32, 5, 8, 128), F32), pltpu.SemaphoreType.DMA((6,))], [VMEM, SMEM],
    )(*(pltpu.with_memory_space_constraint(x, pltpu.HBM) for x in (
        owner, brick_index, stiffness.reshape(1, 32), rest_sq.reshape(1, 32), positions.transpose(1, 0, 2), weights)))
    x_last, y_last = call(planes_kernel, [SMEM, VMEM], ([3, 1, 8, 256], [3, 16, 1, 256]))(slots, velocity)
    y_low = shifted(y_last, "col", 1)
    x_low = shifted(x_last, "row", 1)
    pushes = moved(pushes, "col")
    ids = pushes[:, 4, 0, 73:76].astype(jnp.int32)

    field, turned = call(add_up_kernel, [SMEM] + [VMEM] * 3, ([256, 384], [3, 32, 8, 128]),
                         [pltpu.VMEM((32, 8, 128), F32)] * 6)(ids, pushes, z_fore, velocity)
    spectrum = call(star_kernel, [VMEM] * 5, codes_of(32, 4))(z_fore, velocity, x_low, y_low, field)
    spectrum = moved(spectrum, "col")
    spectrum = call(y_kernel, [VMEM] * 6, codes_of(16, 7))(
        y_fore, y_lanes, y_twiddle, side_lanes, side_twiddle, spectrum)
    marks = [jnp.asarray(m, jnp.int32) for m in marks]
    spectrum, marks = lax.optimization_barrier((spectrum, marks))
    spectrum = moved(spectrum, "row")
    units, damping = wave_tables(marks, row, col)
    spectrum = call(x_kernel, [SMEM] + [VMEM] * 10, codes_of(16, 7))(
        flags, x_fore, x_extra, x_back, x_lanes, x_lanes_back, x_twiddle, flips, units, damping, spectrum)
    spectrum = moved(spectrum, "row")
    cells = jax.ShapeDtypeStruct((32, 64, 128), BF16)
    replies, cells_high, cells_low = call(reply_kernel, [SMEM, VMEM, VMEM], (codes_of(32, 5), cells, cells))(
        ids, turned, weights)
    spectrum = call(y_back_kernel, [VMEM] * 5, codes_of(32, 8))(
        y_back, y_lanes_back, y_twiddle, spectrum, replies)
    spectrum = moved(spectrum, "col")
    new_velocity, marker_velocity = call(
        last_kernel, [SMEM] + [VMEM] * 5, ([3, 16, 8, 256], [3, 32, 128]))(
        slots, z_back, spectrum, weights, cells_high, cells_low)
    return new_velocity, marker_velocity.transpose(1, 0, 2)


def solution(mesh):
    both = ("row", "col")
    placed = (
        P(None, "row", "col", None),
        P(both, None, None),
        P(both, None, None, None),
        P(both),
        P(both),
        P(both, None),
        P(both),
    )
    return jax.shard_map(
        local,
        mesh=mesh,
        in_specs=placed,
        out_specs=(P(None, "row", "col", None), P(both, None, None)),
        check_vma=False,
    )
```
